256 devices in a mesh: grp: 8 (over x, core), box: 32 (over y, z).
Axes of the slice: x: 4, y: 4, z: 8, core: 2. Of those that a mesh axis runs over, the one named last changes fastest.
Arguments:
- source_field: float32 [256, 1024, 128], P('grp', 'box'), may hold values from -7 to 7
- region_tags: int32 [256, 1024, 128], P('grp', 'box'), may hold values from 0 to 7
- region_coef: float32 [8], replicated, may hold values from 0.2 to 5
- roughness: float32 [256, 1024, 128], P('grp', 'box'), may hold values from 0.5 to 2
Outputs:
- solution: float32 [256, 1024, 128], P('grp', 'box')
- residual: float32 [256, 1024, 128], P('grp', 'box')
The draws below stay inside these ranges and needn't reach their ends.
All inputs are finite; a program needn't handle non-finite values.
Results may differ from the reference program's by a relative error of at most 0.0003.
Values sent between devices are 32-bit elements; how exact they have to be, the bound alone decides.
No kernel may reach another device: no remote copies, remote signals or barrier semaphores. Data moves between devices by JAX's collectives and lax.ppermute only.
A program may use at most 192 MiB of HBM per device.

```python
import math
import jax
import jax.numpy as jnp

LEVELS = 5
NU = 2
NB = 4
CYCLES = 2
REGIONS = 8
NX = 256
NY = 1024
NZ = 128


def draw_source_field(key, part):
    pos_x = (jnp.arange(NX, dtype=jnp.float32) + 0.5) / NX
    pos_y = (jnp.arange(NY, dtype=jnp.float32) + 0.5) / NY
    pos_z = (jnp.arange(NZ, dtype=jnp.float32) + 0.5) / NZ
    rough = jnp.clip(jax.random.normal(key, (NX, NY, NZ), jnp.float32), -6.0, 6.0)
    bump = jnp.sin(math.pi * pos_x)[:, None, None] * jnp.sin(math.pi * pos_y)[None, :, None] * jnp.sin(math.pi * pos_z)[None, None, :]
    return rough + 0.5 * bump


def plant(values, stream_key, low, high):
    extent = values.shape
    spot = [jax.random.randint(jax.random.fold_in(stream_key, axis), (), 0, extent[axis]) for axis in range(len(extent))]
    values = values.at[tuple(spot)].set(low)
    longest = extent.index(max(extent))
    spot[longest] = (spot[longest] + 1) % extent[longest]
    return values.at[tuple(spot)].set(high)


def levels(key, extent, shards, smallest, top_value):
    level = 1.0
    for axis_at, shards_of in shards:
        heights = jax.random.uniform(jax.random.fold_in(jax.random.fold_in(key, 6), axis_at), (shards_of,), jnp.float32, smallest / len(shards), top_value / len(shards))
        level = level * jnp.repeat(jnp.exp(heights), extent[axis_at] // shards_of).reshape((-1,) + (1,) * (len(extent) - 1 - axis_at))
    return level


def setup_inputs(seed: int = 0) -> dict:
    key_list = jax.random.split(jax.random.key(seed), 5)
    source_field = draw_source_field(jax.random.fold_in(key_list[4], 71), 0)
    region_tags = plant(jax.random.randint(key_list[1], (NX, NY, NZ), 0, REGIONS), jax.random.fold_in(key_list[1], 1), 0, REGIONS - 1).astype(jnp.int32)
    region_coef = jnp.clip(jnp.exp(jax.random.uniform(key_list[2], (REGIONS,), jnp.float32, math.log(0.2), math.log(5.0))), 0.2, 5.0)
    roughness = jnp.clip(jnp.exp(math.log(2.0) - 1.3862944 * jax.random.uniform(key_list[3], (NX, NY, NZ), jnp.float32) ** levels(key_list[3], (NX, NY, NZ), ((0, 8), (1, 32)), -0.2, 0.2)), 0.5, 2.0)
    return {"source_field": source_field, "region_tags": region_tags, "region_coef": region_coef, "roughness": roughness}


relax_weight = 0.8


def coarsen(values):
    size_x, size_y, size_z = values.shape
    return values.reshape(size_x // 2, 2, size_y // 2, 2, size_z // 2, 2).sum(axis=(1, 3, 5))


def refine(values):
    return jnp.repeat(jnp.repeat(jnp.repeat(values, 2, 0), 2, 1), 2, 2)


def neighbours(padded):
    return [padded[2:, 1:-1, 1:-1], padded[:-2, 1:-1, 1:-1], padded[1:-1, 2:, 1:-1],
            padded[1:-1, :-2, 1:-1], padded[1:-1, 1:-1, 2:], padded[1:-1, 1:-1, :-2]]


def weights_of(coef_padded):
    center = coef_padded[1:-1, 1:-1, 1:-1]
    face_weights = [(center + other) * 0.5 for other in neighbours(coef_padded)]
    diag_sum = face_weights[0]
    for other in face_weights[1:]:
        diag_sum = diag_sum + other
    return face_weights, diag_sum


def apply_op(values, face_weights, diag_sum):
    near = neighbours(jnp.pad(values, 1))
    total = face_weights[0] * near[0]
    for index in range(1, 6):
        total = total + face_weights[index] * near[index]
    return diag_sum * values - total


def smooth(values, source, face_weights, diag_sum, count):
    for sweep_index in range(count):
        values = values + relax_weight * (source - apply_op(values, face_weights, diag_sum)) / diag_sum
    return values


def krylov_solve(source, face_weights, diag_sum):
    values = jnp.zeros_like(source)
    remain = source
    direction = source
    norm_now = jnp.sum(remain * remain)
    for step_index in range(NB):
        image = apply_op(direction, face_weights, diag_sum)
        alpha = norm_now / jnp.sum(direction * image)
        values = values + alpha * direction
        remain = remain - alpha * image
        norm_next = jnp.sum(remain * remain)
        direction = remain + (norm_next / norm_now) * direction
        norm_now = norm_next
    return values


def v_cycle(level_index, values, source, operators):
    face_weights, diag_sum = operators[level_index]
    if level_index == LEVELS - 1:
        return krylov_solve(source, face_weights, diag_sum)
    values = smooth(values, source, face_weights, diag_sum, NU)
    remain = source - apply_op(values, face_weights, diag_sum)
    coarse_source = 0.5 * coarsen(remain)
    correction = v_cycle(level_index + 1, jnp.zeros_like(coarse_source), coarse_source, operators)
    values = values + refine(correction)
    return smooth(values, source, face_weights, diag_sum, NU)


def reference(source_field, region_tags, region_coef, roughness):
    coefficient = region_coef[region_tags] * roughness
    fields = [coefficient]
    for level_index in range(1, LEVELS):
        fields.append(coarsen(fields[-1]) * 0.125)
    operators = [weights_of(jnp.pad(field, 1)) for field in fields]
    solution = jnp.zeros_like(source_field)
    for cycle_index in range(CYCLES):
        solution = v_cycle(0, solution, source_field, operators)
    residual = source_field - apply_op(solution, operators[0][0], operators[0][1])
    return solution, residual
```

```python
import jax
import jax.numpy as jnp
from jax import lax
from jax.experimental import pallas as pl
from jax.experimental.pallas import tpu as pltpu
from jax.sharding import PartitionSpec as P

F32 = jnp.float32
NB = 4
INTERPRET = False


def params():
    return pltpu.CompilerParams(vmem_limit_bytes=56 << 20)


def call(kernel, ins, outs, scratch=(), smem=()):
    specs = [
        pl.BlockSpec(memory_space=pltpu.SMEM if i in smem else pltpu.VMEM) for i in range(len(ins))
    ]
    return pl.pallas_call(
        kernel,
        out_shape=[jax.ShapeDtypeStruct(s, F32) for s in outs],
        in_specs=specs,
        out_specs=[pl.BlockSpec(memory_space=pltpu.VMEM) for _ in outs],
        scratch_shapes=[pltpu.VMEM(s, F32) for s in scratch],
        compiler_params=params(),
        interpret=INTERPRET,
    )(*ins)


def iota(shape, dim):
    return lax.broadcasted_iota(jnp.int32, shape, dim)


def halver(n):
    k, j = iota((n, n), 0), iota((n, n), 1)
    return jnp.where((k >> 1) == j, F32(0.5), F32(0.0))


def doubler(n):
    j, k = iota((n, n), 0), iota((n, n), 1)
    return jnp.where((k >> 1) == j, F32(1.0), F32(0.0))


def dot(a, b):
    return lax.dot_general(
        a, b, (((1,), (0,)), ((), ())), precision=lax.Precision.HIGHEST, preferred_element_type=F32
    )


def up(v, axis):
    return pltpu.roll(v, v.shape[axis] - 1, axis)


def down(v, axis):
    return pltpu.roll(v, 1, axis)


def near_sum(vc, vn, carry, wxx, wss, wll):
    t = wxx * vn + carry
    t = t + (wss * up(vc, 0) + down(wss * vc, 0))
    return t + (wll * up(vc, 1) + down(wll * vc, 1))


def sweep(v, f, op, lo, hi):
    wx, ws, wl, di = op

    def step(x, state):
        carry, vc = state
        vn = v[x + 1]
        wxx = wx[x]
        t = near_sum(vc, vn, carry, wxx, ws[x], wl[x])
        v[x] = F32(0.2) * vc + di[x] * (f[x] + t)
        return (wxx * vc, vn)

    lax.fori_loop(lo, hi, step, (wx[lo - 1] * v[lo - 1], v[lo]), unroll=2)


def first_sweep(v, f, op, lo, hi):
    di = op[3]

    def step(x, _):
        v[x] = di[x] * f[x]
        return 0

    lax.fori_loop(lo, hi, step, 0, unroll=2)


def resid(v, f, op, x):
    wx, ws, wl, di = op
    vc = v[x]
    t = near_sum(vc, v[x + 1], wx[x - 1] * v[x - 1], wx[x], ws[x], wl[x])
    dinv = di[x]
    inside = dinv > 0
    diag = jnp.where(inside, F32(0.8) / jnp.where(inside, dinv, F32(1.0)), F32(0.0))
    return f[x] - (diag * vc - t)


def resid_pairs(v, f, op, lo, n, out):
    def step(i, _):
        x = lo + 2 * i
        out[i] = resid(v, f, op, x) + resid(v, f, op, x + 1)
        return 0

    lax.fori_loop(0, n, step, 0)


def weights(c, cbase, op, lo, hi, lane_last, sub_last, edge=None):
    wx, ws, wl, di = op
    half = F32(0.5)

    def step(x, _):
        cc = c[x + cbase]
        ch = cc * half
        cp = ch + c[x + cbase + 1] * half
        cm = ch + c[x + cbase - 1] * half
        rows, lanes = iota(cc.shape, 0), iota(cc.shape, 1)
        ny, nl = cc.shape
        s_next, s_prev = up(ch, 0), down(ch, 0)
        if sub_last:
            s_next = jnp.where(rows == ny - 1, F32(0.0), s_next)
            s_prev = jnp.where(rows == 0, F32(0.0), s_prev)
        if edge is not None:
            s_next = jnp.where(rows == ny - 1, edge[1, pl.ds(x + cbase, 1), :] * half, s_next)
            s_prev = jnp.where(rows == 0, edge[0, pl.ds(x + cbase, 1), :] * half, s_prev)
        l_next = jnp.where(lanes >= lane_last, F32(0.0), up(ch, 1))
        l_prev = jnp.where(lanes == 0, F32(0.0), down(ch, 1))
        s_up, l_up = ch + s_next, ch + l_next
        diag = (cp + cm) + (s_up + (ch + s_prev)) + (l_up + (ch + l_prev))
        inside = cc > 0
        wx[x] = cp
        ws[x] = jnp.where(rows == ny - 1, F32(0.0), s_up) if sub_last else s_up
        wl[x] = jnp.where(lanes >= lane_last, F32(0.0), l_up)
        di[x] = jnp.where(inside, F32(0.8) / jnp.where(inside, diag, F32(1.0)), F32(0.0))
        return 0

    lax.fori_loop(lo, hi, step, 0)


def pair_rows(s, start, n):
    return s[:, pl.ds(start, n, stride=2), :] + s[:, pl.ds(start + 1, n, stride=2), :]


def flat(a):
    return a.reshape(a.shape[0] * a.shape[1], a.shape[2])


def add_double(v, es, lo, hi):
    def step(x, _):
        v[x] = v[x] + es[x >> 1]
        return 0

    lax.fori_loop(lo, hi, step, 0, unroll=2)


def coef_kernel(f, tags, table, rough, coef, to_next, to_prev):
    def step(x, _):
        tag = tags[x]
        picked = jnp.zeros(tag.shape, F32)
        for region in range(8):
            picked = jnp.where(tag == region, table[region], picked)
        coef[x] = picked * rough[x]
        return 0

    lax.fori_loop(0, 32, step, 0)
    to_next[0:8] = f[24:32]
    to_next[8:17] = coef[23:32]
    to_prev[0:8] = f[0:8]
    to_prev[8:17] = coef[0:9]


def rows_kernel(f, coef, left, right, to_next, to_prev):
    for out, row, extra in ((to_next, 24, 23), (to_prev, 0, 8)):
        sl = slice(row, row + 8)
        out[0:8] = left[0:8, sl]
        out[8:40] = f[:, sl]
        out[40:48] = right[0:8, sl]
        out[48:57] = left[8:17, sl]
        out[57:89] = coef[:, sl]
        out[89:98] = right[8:17, sl]
        for x in range(50):
            if x < 9:
                line = left[8 + x, extra : extra + 1, :]
            elif x < 41:
                line = coef[x - 9, extra : extra + 1, :]
            else:
                line = right[8 + x - 41, extra : extra + 1, :]
            out[98 + x // 8, x % 8 : x % 8 + 1, :] = line
        out[104, 2:8, :] = jnp.zeros((6, 128), F32)


def edge_flags(ng, nb):
    g, b = lax.axis_index("grp"), lax.axis_index("box")
    one, zero = F32(1.0), F32(0.0)
    return (
        jnp.where(g > 0, one, zero),
        jnp.where(g < ng - 1, one, zero),
        jnp.where(b > 0, one, zero),
        jnp.where(b < nb - 1, one, zero),
    )


def fine_restrict(v, f, op, s):
    resid_pairs(v, f, op, 8, 16, s)
    pairs = pair_rows(s, 8, 16)
    return dot(flat(pairs), halver(128)).reshape(16, 16, 128)


def start_kernel(
    ng, nb, f, coef, left, right, above, below, v, fx, wx, ws, wl, di, packed, cx, edge, s
):
    gl, gr, bl, br = edge_flags(ng, nb)
    fx[0:8, 8:40] = left[0:8]
    fx[8:40, 8:40] = f[...]
    fx[40:48, 8:40] = right[0:8]
    fx[:, 0:8] = above[0:48]
    fx[:, 40:48] = below[0:48]
    cx[0:9, 8:40] = left[8:17] * gl
    cx[9:41, 8:40] = coef[...]
    cx[41:50, 8:40] = right[8:17] * gr
    for rows, src, flag in ((slice(0, 8), above, bl), (slice(40, 48), below, br)):
        cx[0:9, rows] = src[48:57] * (gl * flag)
        cx[9:41, rows] = src[57:89] * flag
        cx[41:50, rows] = src[89:98] * (gr * flag)
    for i, (src, flag) in enumerate(((above, bl), (below, br))):
        lines = flat(src[98:105])
        x = iota(lines.shape, 0)
        scale = jnp.where(x < 9, gl * flag, jnp.where(x < 41, flag, gr * flag))
        edge[i] = lines * scale
    op = (wx, ws, wl, di)
    weights(cx, 1, op, 0, 48, 127, False, edge)
    first_sweep(v, fx, op, 0, 48)
    sweep(v, fx, op, 1, 47)
    f1 = fine_restrict(v, fx, op, s)

    def pair(i, _):
        s[i, 8:40] = coef[2 * i] + coef[2 * i + 1]
        return 0

    lax.fori_loop(0, 16, pair, 0)
    c1 = dot(flat(pair_rows(s, 8, 16) * F32(0.25)), halver(128)).reshape(16, 16, 128)
    packed[...] = f1 + pltpu.roll(c1, 64, 2)


def mid_down(f1, v1, op1, f2, v2, op2, s, payload, extra):
    first_sweep(v1, f1, op1, 2, 46)
    sweep(v1, f1, op1, 3, 45)
    resid_pairs(v1, f1, op1, 4, 20, s)
    half = halver(128)
    f2[2:22] = dot(flat(pair_rows(s.at[0:20], 0, 24)), half).reshape(20, 24, 128)
    first_sweep(v2, f2, op2, 2, 22)
    sweep(v2, f2, op2, 3, 21)
    resid_pairs(v2, f2, op2, 8, 4, s.at[0:4, 0:24])
    send = collect(s, half, 0, F32(1.0))
    if extra is not None:
        send = send + extra
    payload[...] = jnp.broadcast_to(send[None], payload.shape)


def collect(s, half, lane, scale):
    total = jnp.zeros((12, 128), F32)
    lanes = iota((12, 128), 1)
    for x in range(4):
        pairs = flat(pair_rows(s.at[x : x + 1], 0, 12))
        cut = jnp.where(lanes < 16, dot(pairs * scale, half), F32(0.0))
        shift = lane + 16 * x
        total = total + (pltpu.roll(cut, shift, 1) if shift else cut)
    return total[4:8]


def mid_kernel(
    ng, nb, own, left, right, above, below,
    f1, v1, wx1, ws1, wl1, di1, f2, v2, wx2, ws2, wl2, di2, payload, c1, c2, s,
):
    gl, gr, bl, br = edge_flags(ng, nb)
    lanes = iota((16, 128), 1)

    def put(x, rows, slab, flag):
        f1[x, rows] = jnp.where(lanes < 64, slab, F32(0.0))
        c1[x, rows] = jnp.where(lanes < 64, pltpu.roll(slab, 64, 1) * flag, F32(0.0))

    for x in range(48):
        src, flag = ((left, gl), (own, None), (right, gr))[x // 16]
        fx = F32(1.0) if flag is None else flag
        put(x, slice(16, 32), src[x % 16], fx)
        put(x, slice(0, 16), above[x], fx * bl)
        put(x, slice(32, 48), below[x], fx * br)
    op1, op2 = (wx1, ws1, wl1, di1), (wx2, ws2, wl2, di2)
    weights(c1, 0, op1, 1, 47, 63, False)

    def pair(i, _):
        s[i] = c1[2 * i] + c1[2 * i + 1]
        return 0

    lax.fori_loop(0, 24, pair, 0)
    half = halver(128)
    c2[...] = dot(flat(pair_rows(s, 0, 24) * F32(0.25)), half).reshape(24, 24, 128)
    weights(c2, 0, op2, 1, 23, 31, False)
    for x in range(4):
        s[x, 0:24] = c2[8 + 2 * x] + c2[9 + 2 * x]
    extra = collect(s, half, 64, F32(0.25))
    mid_down(f1, v1, op1, f2, v2, op2, s, payload, extra)


def mid2_kernel(
    own, left, right, above, below, wx1, ws1, wl1, di1, wx2, ws2, wl2, di2,
    f1, v1, f2, v2, payload, s,
):
    lanes = iota((16, 128), 1)

    def put(x, rows, slab):
        if x % 16 >= 8:
            slab = pltpu.roll(slab, 64, 1)
        f1[x, rows] = jnp.where(lanes < 64, slab, F32(0.0))

    for x in range(48):
        i = x % 8
        put(x, slice(16, 32), (left, own, right)[x // 16][i])
        put(x, slice(0, 16), above[8 * (x // 16) + i])
        put(x, slice(32, 48), below[8 * (x // 16) + i])
    op1, op2 = (wx1, ws1, wl1, di1), (wx2, ws2, wl2, di2)
    mid_down(f1, v1, op1, f2, v2, op2, s, payload, None)


def apply3(p, wx, ws, wl, diag):
    zero = jnp.zeros_like(p[:1])
    q = wx * jnp.concatenate([p[1:], zero], 0)
    q = q + jnp.concatenate([zero, (wx * p)[:-1]], 0)
    q = q + (ws * up(p, 1) + down(ws * p, 1))
    q = q + (wl * up(p, 2) + down(wl * p, 2))
    return diag * p - q


def bottom(f4, c4, ny4):
    nx, nz, nl = c4.shape
    ch = c4 * F32(0.5)
    zero = jnp.zeros_like(ch[:1])
    rows, lanes, slabs = iota(c4.shape, 1), iota(c4.shape, 2), iota(c4.shape, 0)
    o = F32(0.0)
    x_up = ch + jnp.concatenate([ch[1:], zero], 0)
    x_dn = ch + jnp.concatenate([zero, ch[:-1]], 0)
    s_up = ch + jnp.where(rows == nz - 1, o, up(ch, 1))
    s_dn = ch + jnp.where(rows == 0, o, down(ch, 1))
    l_up = ch + jnp.where(lanes >= ny4 - 1, o, up(ch, 2))
    l_dn = ch + jnp.where(lanes == 0, o, down(ch, 2))
    diag = x_up + x_dn + s_up + s_dn + l_up + l_dn
    wx = jnp.where(slabs == nx - 1, o, x_up)
    ws = jnp.where(rows == nz - 1, o, s_up)
    wl = jnp.where(lanes >= ny4 - 1, o, l_up)

    def total(a):
        return jnp.sum(jnp.sum(a, axis=0))

    v = None
    r = p = f4
    rr = total(r * r)
    for i in range(NB):
        q = apply3(p, wx, ws, wl, diag)
        alpha = rr / total(p * q)
        v = alpha * p if v is None else v + alpha * p
        if i < NB - 1:
            r = r - alpha * q
            new = total(r * r)
            p = r + (new / rr) * p
            rr = new
    return v


def coarse(ng, nb, got, got_c, v3, f3, op3, c3, s3):
    n3, nl = 4 * ng, 4 * nb
    for g in range(ng):
        t = got[g * nl : (g + 1) * nl, :].T
        f3[4 + 4 * g : 8 + 4 * g] = t[0:64].reshape(4, 16, nl)
        if got_c is not got:
            t = got_c[g * nl : (g + 1) * nl, :].T
        c3[4 + 4 * g : 8 + 4 * g] = t[64:128].reshape(4, 16, nl)
    pad = jnp.zeros((4, 16, nl), F32)
    for ref in (v3, c3, op3[0]):
        ref[0:4] = pad
        ref[4 + n3 : 8 + n3] = pad
    weights(c3, 0, op3, 4, 4 + n3, nl - 1, True)
    lo, hi = 4, 4 + n3
    first_sweep(v3, f3, op3, lo, hi)
    sweep(v3, f3, op3, lo, hi)
    half = halver(nl)

    def pair(i, _):
        s3[i] = c3[4 + 2 * i] + c3[5 + 2 * i]
        return 0

    lax.fori_loop(0, n3 // 2, pair, 0)
    c4 = dot(flat(pair_rows(s3, 0, 8) * F32(0.25)), half).reshape(n3 // 2, 8, nl)
    resid_pairs(v3, f3, op3, 4, n3 // 2, s3)
    f4 = dot(flat(pair_rows(s3, 0, 8)), half).reshape(n3 // 2, 8, nl)
    v4 = bottom(f4, c4, nl // 2)
    e = dot(flat(v4), doubler(nl)).reshape(n3 // 2, 8, nl)
    s3[:, pl.ds(0, 8, stride=2), :] = e
    s3[:, pl.ds(1, 8, stride=2), :] = e

    def add(x, _):
        v3[4 + x] = v3[4 + x] + s3[x >> 1]
        return 0

    lax.fori_loop(0, n3, add, 0)
    sweep(v3, f3, op3, lo, hi)
    sweep(v3, f3, op3, lo, hi)


def coarse_to_mid(nb, v3, v2, s2, nl):
    g, b = lax.axis_index("grp"), lax.axis_index("box")
    for x in range(12):
        e = v3[4 * g + x]
        s2[x : x + 1, pl.ds(0, 16, stride=2), :] = e[None]
        s2[x : x + 1, pl.ds(1, 16, stride=2), :] = e[None]
    j, y = iota((24, nl), 0), iota((24, nl), 1)
    pick = jnp.where(y == 4 * b - 4 + (j >> 1), F32(1.0), F32(0.0))
    lanes = iota((24, 128), 1)
    zero = F32(0.0)
    for q in range(3):
        block = flat(s2[4 * q : 4 * q + 4])
        e = lax.dot_general(
            pick, block, (((1,), (1,)), ((), ())),
            precision=lax.Precision.HIGHEST, preferred_element_type=F32,
        )
        for i in range(4):
            part = e if i == 0 else pltpu.roll(e, 128 - 32 * i, 1)
            part = jnp.where(lanes < 32, part, zero)
            x = 2 * (4 * q + i)
            v2[x] = v2[x] + part
            v2[x + 1] = v2[x + 1] + part


def climb(ng, nb, got, got_c, v0, f0, op0, v1, f1, op1, v2, f2, op2, scr):
    v3, f3, c3, wx3, ws3, wl3, di3, s3, s2, es = scr
    op3 = (wx3, ws3, wl3, di3)
    coarse(ng, nb, got, got_c, v3, f3, op3, c3, s3)
    coarse_to_mid(nb, v3, v2, s2, 4 * nb)
    sweep(v2, f2, op2, 4, 20)
    sweep(v2, f2, op2, 5, 19)
    twice = doubler(128)
    e = dot(flat(v2[5:19]), twice).reshape(14, 24, 128)
    es[5:19, pl.ds(0, 24, stride=2), :] = e
    es[5:19, pl.ds(1, 24, stride=2), :] = e
    add_double(v1, es, 10, 38)
    sweep(v1, f1, op1, 11, 37)
    sweep(v1, f1, op1, 12, 36)
    e = dot(flat(v1[12:36, 12:36, :]), twice).reshape(24, 24, 128)
    es[:, pl.ds(0, 24, stride=2), :] = e
    es[:, pl.ds(1, 24, stride=2), :] = e


def turn_kernel(ng, nb, *refs):
    got, f0, wx0, ws0, wl0, di0, f1, wx1, ws1, wl1, di1, f2, wx2, ws2, wl2, di2 = refs[:16]
    v0i, v1i, v2i = refs[16:19]
    v0, packed = refs[19:21]
    v1, v2, s = refs[21:24]
    scr = refs[24:]
    v0[...] = v0i[...]
    v1[...] = v1i[...]
    v2[...] = v2i[...]
    op0, op1, op2 = (wx0, ws0, wl0, di0), (wx1, ws1, wl1, di1), (wx2, ws2, wl2, di2)
    climb(ng, nb, got, got, v0, f0, op0, v1, f1, op1, v2, f2, op2, scr)
    add_double(v0, scr[-1], 1, 47)
    for lo in (2, 3, 4, 5):
        sweep(v0, f0, op0, lo, 48 - lo)
    f1n = fine_restrict(v0, f0, op0, s)
    packed[...] = f1n[0:8] + pltpu.roll(f1n[8:16], 64, 2)


def end_kernel(ng, nb, *refs):
    got, got_c = refs[:2]
    f0, wx0, ws0, wl0, di0, f1, wx1, ws1, wl1, di1, f2, wx2, ws2, wl2, di2 = refs[2:17]
    v0i, v1i, v2i = refs[17:20]
    sol, res = refs[20:22]
    v0, v1, v2 = refs[22:25]
    scr = refs[25:]
    v0[...] = v0i[...]
    v1[...] = v1i[...]
    v2[...] = v2i[...]
    op0, op1, op2 = (wx0, ws0, wl0, di0), (wx1, ws1, wl1, di1), (wx2, ws2, wl2, di2)
    climb(ng, nb, got, got_c, v0, f0, op0, v1, f1, op1, v2, f2, op2, scr)
    add_double(v0, scr[-1], 5, 43)
    sweep(v0, f0, op0, 6, 42)
    sweep(v0, f0, op0, 7, 41)

    def step(x, _):
        sol[x] = v0[x + 8, 8:40]
        res[x] = resid(v0, f0, op0, x + 8)[8:40]
        return 0

    lax.fori_loop(0, 32, step, 0)


def ring(x, axis, n):
    before = lax.ppermute(x[0], axis, [(i, (i + 1) % n) for i in range(n)])
    after = lax.ppermute(x[1], axis, [(i, (i - 1) % n) for i in range(n)])
    return before, after


def gather_all(payload):
    got = lax.all_to_all(payload, ("grp", "box"), 0, 0, tiled=True)
    return got.reshape(got.shape[0] * got.shape[1], got.shape[2])


def make_body(ng, nb):
    big, mid, low = (48, 48, 128), (48, 48, 128), (24, 24, 128)
    n3, nl = 4 * ng, 4 * nb
    nd = ng * nb
    pay = (nd, 4, 128)
    lev3 = (n3 + 8, 16, nl)
    climb_scratch = [lev3] * 7 + [(n3 // 2, 16, nl), (12, 32, nl), (24, 48, 128)]

    def fix(kernel):
        return lambda *refs: kernel(ng, nb, *refs)

    def body(f, tags, table, rough):
        coef, to_next, to_prev = call(
            coef_kernel, (f, tags, table, rough), [(32, 32, 128), (17, 32, 128), (17, 32, 128)],
            smem=(2,),
        )
        left, right = ring((to_next, to_prev), "grp", ng)
        to_next, to_prev = call(rows_kernel, (f, coef, left, right), [(105, 8, 128)] * 2)
        above, below = ring((to_next, to_prev), "box", nb)
        v0, f0, wx0, ws0, wl0, di0, packed = call(
            fix(start_kernel), (f, coef, left, right, above, below), [big] * 6 + [(16, 16, 128)],
            scratch=[(50, 48, 128), (2, 56, 128), (16, 48, 128)],
        )
        l0 = (f0, wx0, ws0, wl0, di0)
        left, right = ring((packed, packed), "grp", ng)
        wide = jnp.concatenate([left, packed, right], 0)
        above, below = ring((wide, wide), "box", nb)
        f1, v1, wx1, ws1, wl1, di1, f2, v2, wx2, ws2, wl2, di2, payload = call(
            fix(mid_kernel), (packed, left, right, above, below), [mid] * 6 + [low] * 6 + [pay],
            scratch=[(48, 48, 128), (24, 24, 128), (24, 48, 128)],
        )
        got_c = gather_all(payload)
        l1, l2 = (f1, wx1, ws1, wl1, di1), (f2, wx2, ws2, wl2, di2)
        v0, packed = call(
            fix(turn_kernel), (got_c,) + l0 + l1 + l2 + (v0, v1, v2), [big, (8, 16, 128)],
            scratch=[mid, low, (16, 48, 128)] + climb_scratch,
        )
        left, right = ring((packed, packed), "grp", ng)
        wide = jnp.concatenate([left, packed, right], 0)
        above, below = ring((wide, wide), "box", nb)
        f1, v1, f2, v2, payload = call(
            mid2_kernel, (packed, left, right, above, below) + l1[1:] + l2[1:],
            [mid, mid, low, low, pay], scratch=[(24, 48, 128)],
        )
        got = gather_all(payload)
        l1, l2 = (f1,) + l1[1:], (f2,) + l2[1:]
        return tuple(call(
            fix(end_kernel), (got, got_c) + l0 + l1 + l2 + (v0, v1, v2), [(32, 32, 128)] * 2,
            scratch=[big, mid, low] + climb_scratch,
        ))

    return body


def solution(mesh):
    body = make_body(mesh.shape["grp"], mesh.shape["box"])
    return jax.shard_map(
        body,
        mesh=mesh,
        in_specs=(P("grp", "box", None), P("grp", "box", None), P(), P("grp", "box", None)),
        out_specs=(P("grp", "box", None), P("grp", "box", None)),
        check_vma=False,
    )
```

```python
import jax
import jax.numpy as jnp
from jax import lax
from jax.experimental import pallas as pl
from jax.experimental.pallas import tpu as pltpu
from jax.sharding import PartitionSpec as P

F32 = jnp.float32
NB = 4
INTERPRET = False


def params():
    return pltpu.CompilerParams(vmem_limit_bytes=24 << 20)


def call(kernel, ins, outs, scratch=(), smem=(), leave=(), aliases=None):
    def shape_of(i, s):
        if INTERPRET or i in leave:
            return jax.ShapeDtypeStruct(s, F32)
        return pltpu.VMEM(s, F32)

    def place(i, x):
        if INTERPRET or i in smem:
            return x
        return pltpu.with_memory_space_constraint(x, pltpu.VMEM)

    specs = [
        pl.BlockSpec(memory_space=pltpu.SMEM if i in smem else pltpu.VMEM) for i in range(len(ins))
    ]
    return pl.pallas_call(
        kernel,
        out_shape=[shape_of(i, s) for i, s in enumerate(outs)],
        in_specs=specs,
        out_specs=[pl.BlockSpec(memory_space=pltpu.VMEM) for _ in outs],
        scratch_shapes=[pltpu.VMEM(s, F32) for s in scratch],
        compiler_params=params(),
        input_output_aliases=aliases or {},
        interpret=INTERPRET,
    )(*[place(i, x) for i, x in enumerate(ins)])


def iota(shape, dim):
    return lax.broadcasted_iota(jnp.int32, shape, dim)


def halver(n):
    k, j = iota((n, n), 0), iota((n, n), 1)
    return jnp.where((k >> 1) == j, F32(0.5), F32(0.0))


def doubler(n):
    j, k = iota((n, n), 0), iota((n, n), 1)
    return jnp.where((k >> 1) == j, F32(1.0), F32(0.0))


def dot(a, b):
    return lax.dot_general(
        a, b, (((1,), (0,)), ((), ())), precision=lax.Precision.HIGHEST, preferred_element_type=F32
    )


def up(v, axis):
    return pltpu.roll(v, v.shape[axis] - 1, axis)


def down(v, axis):
    return pltpu.roll(v, 1, axis)


def near_sum(vc, vn, carry, wxx, wss, wll):
    t = wxx * vn + carry
    t = t + (wss * up(vc, 0) + down(wss * vc, 0))
    return t + (wll * up(vc, 1) + down(wll * vc, 1))


def sweep(v, f, op, lo, hi):
    wx, ws, wl, di = op

    def step(x, state):
        carry, vc = state
        vn = v[x + 1]
        wxx = wx[x]
        t = near_sum(vc, vn, carry, wxx, ws[x], wl[x])
        v[x] = F32(0.2) * vc + di[x] * (f[x] + t)
        return (wxx * vc, vn)

    lax.fori_loop(lo, hi, step, (wx[lo - 1] * v[lo - 1], v[lo]), unroll=2)


def first_sweep(v, f, op, lo, hi):
    di = op[3]

    def step(x, _):
        v[x] = di[x] * f[x]
        return 0

    lax.fori_loop(lo, hi, step, 0, unroll=2)


def resid(v, f, op, x):
    wx, ws, wl, di = op
    vc = v[x]
    t = near_sum(vc, v[x + 1], wx[x - 1] * v[x - 1], wx[x], ws[x], wl[x])
    dinv = di[x]
    inside = dinv > 0
    diag = jnp.where(inside, F32(0.8) / jnp.where(inside, dinv, F32(1.0)), F32(0.0))
    return f[x] - (diag * vc - t)


def resid_pairs(v, f, op, lo, n, out):
    def step(i, _):
        x = lo + 2 * i
        out[i] = resid(v, f, op, x) + resid(v, f, op, x + 1)
        return 0

    lax.fori_loop(0, n, step, 0)


def weights(c, cbase, op, lo, hi, lane_last, sub_last, edge=None):
    wx, ws, wl, di = op
    half = F32(0.5)

    def step(x, _):
        cc = c[x + cbase]
        ch = cc * half
        cp = ch + c[x + cbase + 1] * half
        cm = ch + c[x + cbase - 1] * half
        rows, lanes = iota(cc.shape, 0), iota(cc.shape, 1)
        ny, nl = cc.shape
        s_next, s_prev = up(ch, 0), down(ch, 0)
        if sub_last:
            s_next = jnp.where(rows == ny - 1, F32(0.0), s_next)
            s_prev = jnp.where(rows == 0, F32(0.0), s_prev)
        if edge is not None:
            s_next = jnp.where(rows == ny - 1, edge[1, pl.ds(x + cbase, 1), :] * half, s_next)
            s_prev = jnp.where(rows == 0, edge[0, pl.ds(x + cbase, 1), :] * half, s_prev)
        l_next = jnp.where(lanes >= lane_last, F32(0.0), up(ch, 1))
        l_prev = jnp.where(lanes == 0, F32(0.0), down(ch, 1))
        s_up, l_up = ch + s_next, ch + l_next
        diag = (cp + cm) + (s_up + (ch + s_prev)) + (l_up + (ch + l_prev))
        inside = cc > 0
        wx[x] = cp
        ws[x] = jnp.where(rows == ny - 1, F32(0.0), s_up) if sub_last else s_up
        wl[x] = jnp.where(lanes >= lane_last, F32(0.0), l_up)
        di[x] = jnp.where(inside, F32(0.8) / jnp.where(inside, diag, F32(1.0)), F32(0.0))
        return 0

    lax.fori_loop(lo, hi, step, 0)


def pair_rows(s, start, n):
    return s[:, pl.ds(start, n, stride=2), :] + s[:, pl.ds(start + 1, n, stride=2), :]


def flat(a):
    return a.reshape(a.shape[0] * a.shape[1], a.shape[2])


def add_double(v, es, lo, hi):
    def step(x, _):
        v[x] = v[x] + es[x >> 1]
        return 0

    lax.fori_loop(lo, hi, step, 0, unroll=2)


def coef_kernel(f, tags, table, rough, coef, to_next, to_prev):
    def step(x, _):
        tag = tags[x]
        picked = jnp.zeros(tag.shape, F32)
        for region in range(8):
            picked = jnp.where(tag == region, table[region], picked)
        coef[x] = picked * rough[x]
        return 0

    lax.fori_loop(0, 32, step, 0)
    to_next[0:8] = f[24:32]
    to_next[8:17] = coef[23:32]
    to_prev[0:8] = f[0:8]
    to_prev[8:17] = coef[0:9]


def rows_kernel(f, coef, left, right, to_next, to_prev):
    for out, row, extra in ((to_next, 24, 23), (to_prev, 0, 8)):
        sl = slice(row, row + 8)
        out[0:8] = left[0:8, sl]
        out[8:40] = f[:, sl]
        out[40:48] = right[0:8, sl]
        out[48:57] = left[8:17, sl]
        out[57:89] = coef[:, sl]
        out[89:98] = right[8:17, sl]
        for x in range(50):
            if x < 9:
                line = left[8 + x, extra : extra + 1, :]
            elif x < 41:
                line = coef[x - 9, extra : extra + 1, :]
            else:
                line = right[8 + x - 41, extra : extra + 1, :]
            out[98 + x // 8, x % 8 : x % 8 + 1, :] = line
        out[104, 2:8, :] = jnp.zeros((6, 128), F32)


def edge_flags(ng, nb):
    g, b = lax.axis_index("grp"), lax.axis_index("box")
    one, zero = F32(1.0), F32(0.0)
    return (
        jnp.where(g > 0, one, zero),
        jnp.where(g < ng - 1, one, zero),
        jnp.where(b > 0, one, zero),
        jnp.where(b < nb - 1, one, zero),
    )


def fine_restrict(v, f, op, s):
    resid_pairs(v, f, op, 8, 16, s)
    pairs = pair_rows(s, 8, 16)
    return dot(flat(pairs), halver(128)).reshape(16, 16, 128)


def start_kernel(
    ng, nb, f, coef, left, right, above, below, v, fx, wx, ws, wl, di, packed, cx, edge, s
):
    gl, gr, bl, br = edge_flags(ng, nb)
    fx[0:8, 8:40] = left[0:8]
    fx[8:40, 8:40] = f[...]
    fx[40:48, 8:40] = right[0:8]
    fx[:, 0:8] = above[0:48]
    fx[:, 40:48] = below[0:48]
    cx[0:9, 8:40] = left[8:17] * gl
    cx[9:41, 8:40] = coef[...]
    cx[41:50, 8:40] = right[8:17] * gr
    for rows, src, flag in ((slice(0, 8), above, bl), (slice(40, 48), below, br)):
        cx[0:9, rows] = src[48:57] * (gl * flag)
        cx[9:41, rows] = src[57:89] * flag
        cx[41:50, rows] = src[89:98] * (gr * flag)
    for i, (src, flag) in enumerate(((above, bl), (below, br))):
        lines = flat(src[98:105])
        x = iota(lines.shape, 0)
        scale = jnp.where(x < 9, gl * flag, jnp.where(x < 41, flag, gr * flag))
        edge[i] = lines * scale
    op = (wx, ws, wl, di)
    weights(cx, 1, op, 0, 48, 127, False, edge)
    first_sweep(v, fx, op, 0, 48)
    sweep(v, fx, op, 1, 47)
    f1 = fine_restrict(v, fx, op, s)

    def pair(i, _):
        s[i, 8:40] = coef[2 * i] + coef[2 * i + 1]
        return 0

    lax.fori_loop(0, 16, pair, 0)
    c1 = dot(flat(pair_rows(s, 8, 16) * F32(0.25)), halver(128)).reshape(16, 16, 128)
    packed[...] = f1 + pltpu.roll(c1, 64, 2)


def fold_rows(send):
    lanes = iota((2, 128), 1)
    even = jnp.concatenate([send[0:1], send[2:3]], 0)
    odd = jnp.concatenate([send[1:2], send[3:4]], 0)
    return jnp.where(lanes < 64, even, pltpu.roll(odd, 64, 1))


def mid_down(f1, v1, op1, f2, v2, op2, s, payload, extra):
    first_sweep(v1, f1, op1, 2, 46)
    sweep(v1, f1, op1, 3, 45)
    resid_pairs(v1, f1, op1, 4, 20, s)
    half = halver(128)
    f2[2:22] = dot(flat(pair_rows(s.at[0:20], 0, 24)), half).reshape(20, 24, 128)
    first_sweep(v2, f2, op2, 2, 22)
    sweep(v2, f2, op2, 3, 21)
    resid_pairs(v2, f2, op2, 8, 4, s.at[0:4, 0:24])
    send = collect(s, half, 0, F32(1.0))
    send = fold_rows(send) if extra is None else send + extra
    payload[...] = jnp.broadcast_to(send[None], payload.shape)


def collect(s, half, lane, scale):
    total = jnp.zeros((12, 128), F32)
    lanes = iota((12, 128), 1)
    for x in range(4):
        pairs = flat(pair_rows(s.at[x : x + 1], 0, 12))
        cut = jnp.where(lanes < 16, dot(pairs * scale, half), F32(0.0))
        shift = lane + 16 * x
        total = total + (pltpu.roll(cut, shift, 1) if shift else cut)
    return total[4:8]


def mid_kernel(
    ng, nb, own, left, right, above, below,
    f1, v1, wx1, ws1, wl1, di1, f2, v2, wx2, ws2, wl2, di2, payload, c1, c2, s,
):
    gl, gr, bl, br = edge_flags(ng, nb)
    lanes = iota((16, 128), 1)

    def put(x, rows, slab, flag):
        f1[x, rows] = jnp.where(lanes < 64, slab, F32(0.0))
        c1[x, rows] = jnp.where(lanes < 64, pltpu.roll(slab, 64, 1) * flag, F32(0.0))

    for x in range(48):
        src, flag = ((left, gl), (own, None), (right, gr))[x // 16]
        fx = F32(1.0) if flag is None else flag
        put(x, slice(16, 32), src[x % 16], fx)
        put(x, slice(0, 16), above[x], fx * bl)
        put(x, slice(32, 48), below[x], fx * br)
    op1, op2 = (wx1, ws1, wl1, di1), (wx2, ws2, wl2, di2)
    weights(c1, 0, op1, 1, 47, 63, False)

    def pair(i, _):
        s[i] = c1[2 * i] + c1[2 * i + 1]
        return 0

    lax.fori_loop(0, 24, pair, 0)
    half = halver(128)
    c2[...] = dot(flat(pair_rows(s, 0, 24) * F32(0.25)), half).reshape(24, 24, 128)
    weights(c2, 0, op2, 1, 23, 31, False)
    for x in range(4):
        s[x, 0:24] = c2[8 + 2 * x] + c2[9 + 2 * x]
    extra = collect(s, half, 64, F32(0.25))
    mid_down(f1, v1, op1, f2, v2, op2, s, payload, extra)


def mid2_kernel(
    own, left, right, above, below, wx1, ws1, wl1, di1, wx2, ws2, wl2, di2,
    f1, v1, f2, v2, payload, s,
):
    lanes = iota((16, 128), 1)

    def put(x, rows, slab):
        if x % 16 >= 8:
            slab = pltpu.roll(slab, 64, 1)
        f1[x, rows] = jnp.where(lanes < 64, slab, F32(0.0))

    for x in range(48):
        i = x % 8
        put(x, slice(16, 32), (left, own, right)[x // 16][i])
        put(x, slice(0, 16), above[8 * (x // 16) + i])
        put(x, slice(32, 48), below[8 * (x // 16) + i])
    op1, op2 = (wx1, ws1, wl1, di1), (wx2, ws2, wl2, di2)
    mid_down(f1, v1, op1, f2, v2, op2, s, payload, None)


def apply3(p, wx, ws, wl, diag):
    zero = jnp.zeros_like(p[:1])
    q = wx * jnp.concatenate([p[1:], zero], 0)
    q = q + jnp.concatenate([zero, (wx * p)[:-1]], 0)
    q = q + (ws * up(p, 1) + down(ws * p, 1))
    q = q + (wl * up(p, 2) + down(wl * p, 2))
    return diag * p - q


def bottom(f4, c4, ny4):
    nx, nz, nl = c4.shape
    ch = c4 * F32(0.5)
    zero = jnp.zeros_like(ch[:1])
    rows, lanes, slabs = iota(c4.shape, 1), iota(c4.shape, 2), iota(c4.shape, 0)
    o = F32(0.0)
    x_up = ch + jnp.concatenate([ch[1:], zero], 0)
    x_dn = ch + jnp.concatenate([zero, ch[:-1]], 0)
    s_up = ch + jnp.where(rows == nz - 1, o, up(ch, 1))
    s_dn = ch + jnp.where(rows == 0, o, down(ch, 1))
    l_up = ch + jnp.where(lanes >= ny4 - 1, o, up(ch, 2))
    l_dn = ch + jnp.where(lanes == 0, o, down(ch, 2))
    diag = x_up + x_dn + s_up + s_dn + l_up + l_dn
    wx = jnp.where(slabs == nx - 1, o, x_up)
    ws = jnp.where(rows == nz - 1, o, s_up)
    wl = jnp.where(lanes >= ny4 - 1, o, l_up)

    def total(a):
        return jnp.sum(jnp.sum(a, axis=0))

    v = None
    r = p = f4
    rr = total(r * r)
    for i in range(NB):
        q = apply3(p, wx, ws, wl, diag)
        alpha = rr / total(p * q)
        v = alpha * p if v is None else v + alpha * p
        if i < NB - 1:
            r = r - alpha * q
            new = total(r * r)
            p = r + (new / rr) * p
            rr = new
    return v


def coarse(ng, nb, got, got_c, v3, f3, op3, c3, s3):
    n3, nl = 4 * ng, 4 * nb
    for g in range(ng):
        slabs = slice(4 + 4 * g, 8 + 4 * g)
        t = got_c[g * nl : (g + 1) * nl, :].T
        c3[slabs] = t[64:128].reshape(4, 16, nl)
        if got is None:
            f3[slabs] = t[0:64].reshape(4, 16, nl)
    if got is not None:
        k, y = iota((nl // 2, nl), 0), iota((nl // 2, nl), 1)
        even = jnp.where(y == 2 * k, F32(1.0), F32(0.0))
        odd = jnp.where(y == 2 * k + 1, F32(1.0), F32(0.0))
        ts = [got[g * (nl // 2) : (g + 1) * (nl // 2), :].T for g in range(ng)]
        lhs0 = jnp.concatenate([t[0:64] for t in ts], 0)
        lhs1 = jnp.concatenate([t[64:128] for t in ts], 0)
        f3[4 : 4 + n3] = (dot(lhs0, even) + dot(lhs1, odd)).reshape(n3, 16, nl)
    pad = jnp.zeros((4, 16, nl), F32)
    for ref in (v3, c3, op3[0]):
        ref[0:4] = pad
        ref[4 + n3 : 8 + n3] = pad
    weights(c3, 0, op3, 4, 4 + n3, nl - 1, True)
    lo, hi = 4, 4 + n3
    first_sweep(v3, f3, op3, lo, hi)
    sweep(v3, f3, op3, lo, hi)
    half = halver(nl)

    def pair(i, _):
        s3[i] = c3[4 + 2 * i] + c3[5 + 2 * i]
        return 0

    lax.fori_loop(0, n3 // 2, pair, 0)
    c4 = dot(flat(pair_rows(s3, 0, 8) * F32(0.25)), half).reshape(n3 // 2, 8, nl)
    resid_pairs(v3, f3, op3, 4, n3 // 2, s3)
    f4 = dot(flat(pair_rows(s3, 0, 8)), half).reshape(n3 // 2, 8, nl)
    v4 = bottom(f4, c4, nl // 2)
    e = dot(flat(v4), doubler(nl)).reshape(n3 // 2, 8, nl)
    s3[:, pl.ds(0, 8, stride=2), :] = e
    s3[:, pl.ds(1, 8, stride=2), :] = e

    def add(x, _):
        v3[4 + x] = v3[4 + x] + s3[x >> 1]
        return 0

    lax.fori_loop(0, n3, add, 0)
    sweep(v3, f3, op3, lo, hi)
    sweep(v3, f3, op3, lo, hi)


def coarse_to_mid(nb, v3, v2, s2, nl):
    g, b = lax.axis_index("grp"), lax.axis_index("box")
    for x in range(12):
        e = v3[4 * g + x]
        s2[x : x + 1, pl.ds(0, 16, stride=2), :] = e[None]
        s2[x : x + 1, pl.ds(1, 16, stride=2), :] = e[None]
    j, y = iota((24, nl), 0), iota((24, nl), 1)
    pick = jnp.where(y == 4 * b - 4 + (j >> 1), F32(1.0), F32(0.0))
    lanes = iota((24, 128), 1)
    zero = F32(0.0)
    for q in range(3):
        block = flat(s2[4 * q : 4 * q + 4])
        e = lax.dot_general(
            pick, block, (((1,), (1,)), ((), ())),
            precision=lax.Precision.HIGHEST, preferred_element_type=F32,
        )
        for i in range(4):
            part = e if i == 0 else pltpu.roll(e, 128 - 32 * i, 1)
            part = jnp.where(lanes < 32, part, zero)
            x = 2 * (4 * q + i)
            v2[x] = v2[x] + part
            v2[x + 1] = v2[x + 1] + part


def climb(ng, nb, got, got_c, v0, f0, op0, v1, f1, op1, v2, f2, op2, scr):
    v3, f3, c3, wx3, ws3, wl3, di3, s3, s2, es = scr
    op3 = (wx3, ws3, wl3, di3)
    coarse(ng, nb, got, got_c, v3, f3, op3, c3, s3)
    coarse_to_mid(nb, v3, v2, s2, 4 * nb)
    sweep(v2, f2, op2, 4, 20)
    sweep(v2, f2, op2, 5, 19)
    twice = doubler(128)
    e = dot(flat(v2[5:19]), twice).reshape(14, 24, 128)
    es[5:19, pl.ds(0, 24, stride=2), :] = e
    es[5:19, pl.ds(1, 24, stride=2), :] = e
    add_double(v1, es, 10, 38)
    sweep(v1, f1, op1, 11, 37)
    sweep(v1, f1, op1, 12, 36)
    e = dot(flat(v1[12:36, 12:36, :]), twice).reshape(24, 24, 128)
    es[:, pl.ds(0, 24, stride=2), :] = e
    es[:, pl.ds(1, 24, stride=2), :] = e


def turn_kernel(ng, nb, *refs):
    got, f0, wx0, ws0, wl0, di0, f1, wx1, ws1, wl1, di1, f2, wx2, ws2, wl2, di2 = refs[:16]
    v0i, v1i, v2i = refs[16:19]
    v0, packed = refs[19:21]
    v1, v2, s = refs[21:24]
    scr = refs[24:]
    v1[...] = v1i[...]
    v2[...] = v2i[...]
    op0, op1, op2 = (wx0, ws0, wl0, di0), (wx1, ws1, wl1, di1), (wx2, ws2, wl2, di2)
    climb(ng, nb, None, got, v0, f0, op0, v1, f1, op1, v2, f2, op2, scr)
    add_double(v0, scr[-1], 1, 47)
    for lo in (2, 3, 4, 5):
        sweep(v0, f0, op0, lo, 48 - lo)
    f1n = fine_restrict(v0, f0, op0, s)
    packed[...] = f1n[0:8] + pltpu.roll(f1n[8:16], 64, 2)


def end_kernel(ng, nb, *refs):
    got, got_c = refs[:2]
    f0, wx0, ws0, wl0, di0, f1, wx1, ws1, wl1, di1, f2, wx2, ws2, wl2, di2 = refs[2:17]
    v0i, v1i, v2i = refs[17:20]
    sol, res = refs[20:22]
    v0, v1, v2 = refs[22:25]
    scr = refs[25:]
    v0[...] = v0i[...]
    v1[...] = v1i[...]
    v2[...] = v2i[...]
    op0, op1, op2 = (wx0, ws0, wl0, di0), (wx1, ws1, wl1, di1), (wx2, ws2, wl2, di2)
    climb(ng, nb, got, got_c, v0, f0, op0, v1, f1, op1, v2, f2, op2, scr)
    add_double(v0, scr[-1], 5, 43)
    sweep(v0, f0, op0, 6, 42)
    sweep(v0, f0, op0, 7, 41)

    def step(x, _):
        sol[x] = v0[x + 8, 8:40]
        res[x] = resid(v0, f0, op0, x + 8)[8:40]
        return 0

    lax.fori_loop(0, 32, step, 0)


def ring(x, axis, n):
    before = lax.ppermute(x[0], axis, [(i, (i + 1) % n) for i in range(n)])
    after = lax.ppermute(x[1], axis, [(i, (i - 1) % n) for i in range(n)])
    return before, after


def gather_all(payload):
    got = lax.all_to_all(payload, ("grp", "box"), 0, 0, tiled=True)
    return got.reshape(got.shape[0] * got.shape[1], got.shape[2])


def make_body(ng, nb):
    big, mid, low = (48, 48, 128), (48, 48, 128), (24, 24, 128)
    n3, nl = 4 * ng, 4 * nb
    nd = ng * nb
    pay, pay2 = (nd, 4, 128), (nd, 2, 128)
    lev3 = (n3 + 8, 16, nl)
    climb_scratch = [lev3] * 7 + [(n3 // 2, 16, nl), (12, 32, nl), (24, 48, 128)]

    def fix(kernel):
        return lambda *refs: kernel(ng, nb, *refs)

    def body(f, tags, table, rough):
        coef, to_next, to_prev = call(
            coef_kernel, (f, tags, table, rough), [(32, 32, 128), (17, 32, 128), (17, 32, 128)],
            smem=(2,),
        )
        left, right = ring((to_next, to_prev), "grp", ng)
        to_next, to_prev = call(rows_kernel, (f, coef, left, right), [(105, 8, 128)] * 2)
        above, below = ring((to_next, to_prev), "box", nb)
        v0, f0, wx0, ws0, wl0, di0, packed = call(
            fix(start_kernel), (f, coef, left, right, above, below), [big] * 6 + [(16, 16, 128)],
            scratch=[(50, 48, 128), (2, 56, 128), (16, 48, 128)],
        )
        l0 = (f0, wx0, ws0, wl0, di0)
        left, right = ring((packed, packed), "grp", ng)
        wide = jnp.concatenate([left, packed, right], 0)
        above, below = ring((wide, wide), "box", nb)
        f1, v1, wx1, ws1, wl1, di1, f2, v2, wx2, ws2, wl2, di2, payload = call(
            fix(mid_kernel), (packed, left, right, above, below), [mid] * 6 + [low] * 6 + [pay],
            scratch=[(48, 48, 128), (24, 24, 128), (24, 48, 128)], leave=(12,),
        )
        got_c = gather_all(payload)
        l1, l2 = (f1, wx1, ws1, wl1, di1), (f2, wx2, ws2, wl2, di2)
        v0, packed = call(
            fix(turn_kernel), (got_c,) + l0 + l1 + l2 + (v0, v1, v2), [big, (8, 16, 128)],
            aliases={16: 0}, scratch=[mid, low, (16, 48, 128)] + climb_scratch,
        )
        left, right = ring((packed, packed), "grp", ng)
        wide = jnp.concatenate([left, packed, right], 0)
        above, below = ring((wide, wide), "box", nb)
        f1, v1, f2, v2, payload = call(
            mid2_kernel, (packed, left, right, above, below) + l1[1:] + l2[1:],
            [mid, mid, low, low, pay2], scratch=[(24, 48, 128)], leave=(4,),
        )
        got = gather_all(payload)
        l1, l2 = (f1,) + l1[1:], (f2,) + l2[1:]
        return tuple(call(
            fix(end_kernel), (got, got_c) + l0 + l1 + l2 + (v0, v1, v2), [(32, 32, 128)] * 2,
            scratch=[big, mid, low] + climb_scratch, leave=(0, 1),
        ))

    return body


def solution(mesh):
    body = make_body(mesh.shape["grp"], mesh.shape["box"])
    return jax.shard_map(
        body,
        mesh=mesh,
        in_specs=(P("grp", "box", None), P("grp", "box", None), P(), P("grp", "box", None)),
        out_specs=(P("grp", "box", None), P("grp", "box", None)),
        check_vma=False,
    )
```

```python
import jax
import jax.numpy as jnp
from jax import lax
from jax.experimental import pallas as pl
from jax.experimental.pallas import tpu as pltpu
from jax.sharding import PartitionSpec as P

F32 = jnp.float32
NB = 4
INTERPRET = False


def params():
    return pltpu.CompilerParams(vmem_limit_bytes=24 << 20)


def call(kernel, ins, outs, scratch=(), smem=(), leave=(), aliases=None):
    def shape_of(i, s):
        if INTERPRET or i in leave:
            return jax.ShapeDtypeStruct(s, F32)
        return pltpu.VMEM(s, F32)

    def place(i, x):
        if INTERPRET or i in smem:
            return x
        return pltpu.with_memory_space_constraint(x, pltpu.VMEM)

    specs = [
        pl.BlockSpec(memory_space=pltpu.SMEM if i in smem else pltpu.VMEM) for i in range(len(ins))
    ]
    return pl.pallas_call(
        kernel,
        out_shape=[shape_of(i, s) for i, s in enumerate(outs)],
        in_specs=specs,
        out_specs=[pl.BlockSpec(memory_space=pltpu.VMEM) for _ in outs],
        scratch_shapes=[pltpu.VMEM(s, F32) for s in scratch],
        compiler_params=params(),
        input_output_aliases=aliases or {},
        interpret=INTERPRET,
    )(*[place(i, x) for i, x in enumerate(ins)])


def iota(shape, dim):
    return lax.broadcasted_iota(jnp.int32, shape, dim)


def halver(n):
    k, j = iota((n, n), 0), iota((n, n), 1)
    return jnp.where((k >> 1) == j, F32(0.5), F32(0.0))


def doubler(n):
    j, k = iota((n, n), 0), iota((n, n), 1)
    return jnp.where((k >> 1) == j, F32(1.0), F32(0.0))


def dot(a, b):
    return lax.dot_general(
        a, b, (((1,), (0,)), ((), ())), precision=lax.Precision.HIGHEST, preferred_element_type=F32
    )


def up(v, axis):
    return pltpu.roll(v, v.shape[axis] - 1, axis)


def down(v, axis):
    return pltpu.roll(v, 1, axis)


def near_sum(vc, vn, carry, wxx, wss, wll):
    t = wxx * vn + carry
    t = t + (wss * up(vc, 0) + down(wss * vc, 0))
    return t + (wll * up(vc, 1) + down(wll * vc, 1))


def blocks(lo, hi, size, fn, state=0):
    count = (hi - lo) // size
    if count > 1:
        state = lax.fori_loop(0, count, lambda i, st: fn(lo + i * size, size, st), state)
    elif count == 1:
        state = fn(lo, size, state)
    rest = (hi - lo) - count * size
    if rest:
        state = fn(hi - rest, rest, state)
    return state


def block_of(ref):
    return max(1, 384 // ref.shape[1])


def sweep(v, f, op, lo, hi):
    wx, ws, wl, di = op

    def step(x, n, state):
        carry, vc = state
        vs = [vc] + [v[x + i + 1] for i in range(n)]
        new = []
        for i in range(n):
            wxx = wx[x + i]
            t = near_sum(vs[i], vs[i + 1], carry, wxx, ws[x + i], wl[x + i])
            new.append(F32(0.2) * vs[i] + di[x + i] * (f[x + i] + t))
            carry = wxx * vs[i]
        for i in range(n):
            v[x + i] = new[i]
        return carry, vs[n]

    blocks(lo, hi, block_of(v), step, (wx[lo - 1] * v[lo - 1], v[lo]))


def first_sweep(v, f, op, lo, hi):
    di = op[3]

    def step(x, n, _):
        new = [di[x + i] * f[x + i] for i in range(n)]
        for i in range(n):
            v[x + i] = new[i]
        return 0

    blocks(lo, hi, block_of(v), step)


def resid_slabs(v, f, op, x, n):
    wx, ws, wl, di = op
    vs = [v[x + i - 1] for i in range(n + 2)]
    wxs = [wx[x + i - 1] for i in range(n + 1)]
    out = []
    for i in range(n):
        vc = vs[i + 1]
        t = near_sum(vc, vs[i + 2], wxs[i] * vs[i], wxs[i + 1], ws[x + i], wl[x + i])
        dinv = di[x + i]
        inside = dinv > 0
        diag = jnp.where(inside, F32(0.8) / jnp.where(inside, dinv, F32(1.0)), F32(0.0))
        out.append(f[x + i] - (diag * vc - t))
    return out


def resid_pairs(v, f, op, lo, n, out):
    def step(j, m, _):
        rs = resid_slabs(v, f, op, lo + 2 * j, 2 * m)
        for i in range(m):
            out[j + i] = rs[2 * i] + rs[2 * i + 1]
        return 0

    blocks(0, n, max(1, block_of(v) // 2), step)


def sum_pairs(src, lo, n, out):
    def step(j, m, _):
        new = [src[lo + 2 * (j + i)] + src[lo + 2 * (j + i) + 1] for i in range(m)]
        for i in range(m):
            out[j + i] = new[i]
        return 0

    blocks(0, n, max(1, block_of(out) // 2), step)


def weights(c, cbase, op, lo, hi, lane_last, sub_last, edge=None):
    wx, ws, wl, di = op
    ny, nl = c.shape[1:]
    half, zero = F32(0.5), F32(0.0)

    def step(x, n, _):
        x = x + cbase
        rows, lanes = iota((ny, nl), 0), iota((ny, nl), 1)
        hs = [c[x + i - 1] * half for i in range(n + 2)]
        new = []
        for i in range(n):
            ch = hs[i + 1]
            cp, cm = ch + hs[i + 2], ch + hs[i]
            s_next, s_prev = up(ch, 0), down(ch, 0)
            if sub_last:
                s_next = jnp.where(rows == ny - 1, zero, s_next)
                s_prev = jnp.where(rows == 0, zero, s_prev)
            if edge is not None:
                s_next = jnp.where(rows == ny - 1, edge[1, pl.ds(x + i, 1), :] * half, s_next)
                s_prev = jnp.where(rows == 0, edge[0, pl.ds(x + i, 1), :] * half, s_prev)
            l_next = jnp.where(lanes >= lane_last, zero, up(ch, 1))
            l_prev = jnp.where(lanes == 0, zero, down(ch, 1))
            s_up, l_up = ch + s_next, ch + l_next
            diag = (cp + cm) + (s_up + (ch + s_prev)) + (l_up + (ch + l_prev))
            inside = ch > 0
            dinv = jnp.where(inside, F32(0.8) / jnp.where(inside, diag, F32(1.0)), zero)
            s_up = jnp.where(rows == ny - 1, zero, s_up) if sub_last else s_up
            new.append((cp, s_up, jnp.where(lanes >= lane_last, zero, l_up), dinv))
        for i in range(n):
            for ref, value in zip(op, new[i]):
                ref[x - cbase + i] = value
        return 0

    blocks(lo, hi, max(1, block_of(c) // 2), step)


def pair_rows(s, start, n):
    return s[:, pl.ds(start, n, stride=2), :] + s[:, pl.ds(start + 1, n, stride=2), :]


def flat(a):
    return a.reshape(a.shape[0] * a.shape[1], a.shape[2])


def add_double(v, es, lo, hi, base=0):
    def step(x, n, _):
        new = [v[x + i] + es[((x - base) >> 1) + (i >> 1)] for i in range(n)]
        for i in range(n):
            v[x + i] = new[i]
        return 0

    blocks(lo, hi, max(2, block_of(v) & ~1), step)


def coef_kernel(f, tags, table, rough, coef, to_next, to_prev):
    def step(x, n, _):
        new = []
        for i in range(n):
            tag = tags[x + i]
            picked = jnp.zeros(tag.shape, F32)
            for region in range(8):
                picked = jnp.where(tag == region, table[region], picked)
            new.append(picked * rough[x + i])
        for i in range(n):
            coef[x + i] = new[i]
        return 0

    blocks(0, 32, 8, step)
    to_next[0:8] = f[24:32]
    to_next[8:17] = coef[23:32]
    to_prev[0:8] = f[0:8]
    to_prev[8:17] = coef[0:9]


def rows_kernel(f, coef, left, right, to_next, to_prev):
    for out, row, extra in ((to_next, 24, 23), (to_prev, 0, 8)):
        sl = slice(row, row + 8)
        out[0:8] = left[0:8, sl]
        out[8:40] = f[:, sl]
        out[40:48] = right[0:8, sl]
        out[48:57] = left[8:17, sl]
        out[57:89] = coef[:, sl]
        out[89:98] = right[8:17, sl]
        for x in range(50):
            if x < 9:
                line = left[8 + x, extra : extra + 1, :]
            elif x < 41:
                line = coef[x - 9, extra : extra + 1, :]
            else:
                line = right[8 + x - 41, extra : extra + 1, :]
            out[98 + x // 8, x % 8 : x % 8 + 1, :] = line
        out[104, 2:8, :] = jnp.zeros((6, 128), F32)


def edge_flags(ng, nb):
    g, b = lax.axis_index("grp"), lax.axis_index("box")
    one, zero = F32(1.0), F32(0.0)
    return (
        jnp.where(g > 0, one, zero),
        jnp.where(g < ng - 1, one, zero),
        jnp.where(b > 0, one, zero),
        jnp.where(b < nb - 1, one, zero),
    )


def fine_restrict(v, f, op, s):
    resid_pairs(v, f, op, 8, 16, s)
    pairs = pair_rows(s, 8, 16)
    return dot(flat(pairs), halver(128)).reshape(16, 16, 128)


def start_kernel(
    ng, nb, f, coef, left, right, above, below, v, fx, wx, ws, wl, di, packed, cx, edge, s
):
    gl, gr, bl, br = edge_flags(ng, nb)
    fx[0:8, 8:40] = left[0:8]
    fx[8:40, 8:40] = f[...]
    fx[40:48, 8:40] = right[0:8]
    fx[:, 0:8] = above[0:48]
    fx[:, 40:48] = below[0:48]
    cx[0:9, 8:40] = left[8:17] * gl
    cx[9:41, 8:40] = coef[...]
    cx[41:50, 8:40] = right[8:17] * gr
    for rows, src, flag in ((slice(0, 8), above, bl), (slice(40, 48), below, br)):
        cx[0:9, rows] = src[48:57] * (gl * flag)
        cx[9:41, rows] = src[57:89] * flag
        cx[41:50, rows] = src[89:98] * (gr * flag)
    for i, (src, flag) in enumerate(((above, bl), (below, br))):
        lines = flat(src[98:105])
        x = iota(lines.shape, 0)
        scale = jnp.where(x < 9, gl * flag, jnp.where(x < 41, flag, gr * flag))
        edge[i] = lines * scale
    op = (wx, ws, wl, di)
    weights(cx, 1, op, 0, 48, 127, False, edge)
    first_sweep(v, fx, op, 0, 48)
    sweep(v, fx, op, 1, 47)
    f1 = fine_restrict(v, fx, op, s)

    sum_pairs(coef, 0, 16, s.at[:, 8:40])
    c1 = dot(flat(pair_rows(s, 8, 16) * F32(0.25)), halver(128)).reshape(16, 16, 128)
    packed[...] = f1 + pltpu.roll(c1, 64, 2)


def fold_rows(send):
    lanes = iota((2, 128), 1)
    even = jnp.concatenate([send[0:1], send[2:3]], 0)
    odd = jnp.concatenate([send[1:2], send[3:4]], 0)
    return jnp.where(lanes < 64, even, pltpu.roll(odd, 64, 1))


def mid_down(f1, v1, op1, f2, v2, op2, s, payload, extra):
    first_sweep(v1, f1, op1, 2, 46)
    sweep(v1, f1, op1, 3, 45)
    resid_pairs(v1, f1, op1, 4, 20, s)
    half = halver(128)
    f2[2:22] = dot(flat(pair_rows(s.at[0:20], 0, 24)), half).reshape(20, 24, 128)
    first_sweep(v2, f2, op2, 2, 22)
    sweep(v2, f2, op2, 3, 21)
    resid_pairs(v2, f2, op2, 8, 4, s.at[0:4, 0:24])
    send = collect(s, half, 0, F32(1.0))
    send = fold_rows(send) if extra is None else send + extra
    payload[...] = jnp.broadcast_to(send[None], payload.shape)


def collect(s, half, lane, scale):
    total = jnp.zeros((12, 128), F32)
    lanes = iota((12, 128), 1)
    for x in range(4):
        pairs = flat(pair_rows(s.at[x : x + 1], 0, 12))
        cut = jnp.where(lanes < 16, dot(pairs * scale, half), F32(0.0))
        shift = lane + 16 * x
        total = total + (pltpu.roll(cut, shift, 1) if shift else cut)
    return total[4:8]


def mid_kernel(
    ng, nb, own, left, right, above, below,
    f1, v1, wx1, ws1, wl1, di1, f2, v2, wx2, ws2, wl2, di2, payload, c1, c2, s,
):
    gl, gr, bl, br = edge_flags(ng, nb)
    lanes = iota((16, 128), 1)

    def put(x, rows, slab, flag):
        f1[x, rows] = jnp.where(lanes < 64, slab, F32(0.0))
        c1[x, rows] = jnp.where(lanes < 64, pltpu.roll(slab, 64, 1) * flag, F32(0.0))

    for x in range(48):
        src, flag = ((left, gl), (own, None), (right, gr))[x // 16]
        fx = F32(1.0) if flag is None else flag
        put(x, slice(16, 32), src[x % 16], fx)
        put(x, slice(0, 16), above[x], fx * bl)
        put(x, slice(32, 48), below[x], fx * br)
    op1, op2 = (wx1, ws1, wl1, di1), (wx2, ws2, wl2, di2)
    weights(c1, 0, op1, 1, 47, 63, False)

    sum_pairs(c1, 0, 24, s)
    half = halver(128)
    c2[...] = dot(flat(pair_rows(s, 0, 24) * F32(0.25)), half).reshape(24, 24, 128)
    weights(c2, 0, op2, 1, 23, 31, False)
    for x in range(4):
        s[x, 0:24] = c2[8 + 2 * x] + c2[9 + 2 * x]
    extra = collect(s, half, 64, F32(0.25))
    mid_down(f1, v1, op1, f2, v2, op2, s, payload, extra)


def mid2_kernel(
    own, left, right, above, below, wx1, ws1, wl1, di1, wx2, ws2, wl2, di2,
    f1, v1, f2, v2, payload, s,
):
    lanes = iota((16, 128), 1)

    def put(x, rows, slab):
        if x % 16 >= 8:
            slab = pltpu.roll(slab, 64, 1)
        f1[x, rows] = jnp.where(lanes < 64, slab, F32(0.0))

    for x in range(48):
        i = x % 8
        put(x, slice(16, 32), (left, own, right)[x // 16][i])
        put(x, slice(0, 16), above[8 * (x // 16) + i])
        put(x, slice(32, 48), below[8 * (x // 16) + i])
    op1, op2 = (wx1, ws1, wl1, di1), (wx2, ws2, wl2, di2)
    mid_down(f1, v1, op1, f2, v2, op2, s, payload, None)


def apply3(p, wx, ws, wl, diag):
    zero = jnp.zeros_like(p[:1])
    q = wx * jnp.concatenate([p[1:], zero], 0)
    q = q + jnp.concatenate([zero, (wx * p)[:-1]], 0)
    q = q + (ws * up(p, 1) + down(ws * p, 1))
    q = q + (wl * up(p, 2) + down(wl * p, 2))
    return diag * p - q


def bottom(f4, c4, ny4):
    nx, nz, nl = c4.shape
    ch = c4 * F32(0.5)
    zero = jnp.zeros_like(ch[:1])
    rows, lanes, slabs = iota(c4.shape, 1), iota(c4.shape, 2), iota(c4.shape, 0)
    o = F32(0.0)
    x_up = ch + jnp.concatenate([ch[1:], zero], 0)
    x_dn = ch + jnp.concatenate([zero, ch[:-1]], 0)
    s_up = ch + jnp.where(rows == nz - 1, o, up(ch, 1))
    s_dn = ch + jnp.where(rows == 0, o, down(ch, 1))
    l_up = ch + jnp.where(lanes >= ny4 - 1, o, up(ch, 2))
    l_dn = ch + jnp.where(lanes == 0, o, down(ch, 2))
    diag = x_up + x_dn + s_up + s_dn + l_up + l_dn
    wx = jnp.where(slabs == nx - 1, o, x_up)
    ws = jnp.where(rows == nz - 1, o, s_up)
    wl = jnp.where(lanes >= ny4 - 1, o, l_up)

    def total(a):
        return jnp.sum(jnp.sum(a, axis=0))

    v = None
    r = p = f4
    rr = total(r * r)
    for i in range(NB):
        q = apply3(p, wx, ws, wl, diag)
        alpha = rr / total(p * q)
        v = alpha * p if v is None else v + alpha * p
        if i < NB - 1:
            r = r - alpha * q
            new = total(r * r)
            p = r + (new / rr) * p
            rr = new
    return v


def coarse(ng, nb, got, got_c, v3, f3, op3, c3, s3):
    n3, nl = 4 * ng, 4 * nb
    for g in range(ng):
        slabs = slice(4 + 4 * g, 8 + 4 * g)
        t = got_c[g * nl : (g + 1) * nl, :].T
        c3[slabs] = t[64:128].reshape(4, 16, nl)
        if got is None:
            f3[slabs] = t[0:64].reshape(4, 16, nl)
    if got is not None:
        k, y = iota((nl // 2, nl), 0), iota((nl // 2, nl), 1)
        even = jnp.where(y == 2 * k, F32(1.0), F32(0.0))
        odd = jnp.where(y == 2 * k + 1, F32(1.0), F32(0.0))
        ts = [got[g * (nl // 2) : (g + 1) * (nl // 2), :].T for g in range(ng)]
        lhs0 = jnp.concatenate([t[0:64] for t in ts], 0)
        lhs1 = jnp.concatenate([t[64:128] for t in ts], 0)
        f3[4 : 4 + n3] = (dot(lhs0, even) + dot(lhs1, odd)).reshape(n3, 16, nl)
    pad = jnp.zeros((4, 16, nl), F32)
    for ref in (v3, c3, op3[0]):
        ref[0:4] = pad
        ref[4 + n3 : 8 + n3] = pad
    weights(c3, 0, op3, 4, 4 + n3, nl - 1, True)
    lo, hi = 4, 4 + n3
    first_sweep(v3, f3, op3, lo, hi)
    sweep(v3, f3, op3, lo, hi)
    half = halver(nl)

    sum_pairs(c3, 4, n3 // 2, s3)
    c4 = dot(flat(pair_rows(s3, 0, 8) * F32(0.25)), half).reshape(n3 // 2, 8, nl)
    resid_pairs(v3, f3, op3, 4, n3 // 2, s3)
    f4 = dot(flat(pair_rows(s3, 0, 8)), half).reshape(n3 // 2, 8, nl)
    v4 = bottom(f4, c4, nl // 2)
    e = dot(flat(v4), doubler(nl)).reshape(n3 // 2, 8, nl)
    s3[:, pl.ds(0, 8, stride=2), :] = e
    s3[:, pl.ds(1, 8, stride=2), :] = e

    add_double(v3, s3, 4, 4 + n3, 4)
    sweep(v3, f3, op3, lo, hi)
    sweep(v3, f3, op3, lo, hi)


def coarse_to_mid(nb, v3, v2, s2, nl):
    g, b = lax.axis_index("grp"), lax.axis_index("box")
    for x in range(12):
        e = v3[4 * g + x]
        s2[x : x + 1, pl.ds(0, 16, stride=2), :] = e[None]
        s2[x : x + 1, pl.ds(1, 16, stride=2), :] = e[None]
    j, y = iota((24, nl), 0), iota((24, nl), 1)
    pick = jnp.where(y == 4 * b - 4 + (j >> 1), F32(1.0), F32(0.0))
    lanes = iota((24, 128), 1)
    zero = F32(0.0)
    for q in range(3):
        block = flat(s2[4 * q : 4 * q + 4])
        e = lax.dot_general(
            pick, block, (((1,), (1,)), ((), ())),
            precision=lax.Precision.HIGHEST, preferred_element_type=F32,
        )
        for i in range(4):
            part = e if i == 0 else pltpu.roll(e, 128 - 32 * i, 1)
            part = jnp.where(lanes < 32, part, zero)
            x = 2 * (4 * q + i)
            v2[x] = v2[x] + part
            v2[x + 1] = v2[x + 1] + part


def climb(ng, nb, got, got_c, v0, f0, op0, v1, f1, op1, v2, f2, op2, scr):
    v3, f3, c3, wx3, ws3, wl3, di3, s3, s2, es = scr
    op3 = (wx3, ws3, wl3, di3)
    coarse(ng, nb, got, got_c, v3, f3, op3, c3, s3)
    coarse_to_mid(nb, v3, v2, s2, 4 * nb)
    sweep(v2, f2, op2, 4, 20)
    sweep(v2, f2, op2, 5, 19)
    twice = doubler(128)
    e = dot(flat(v2[5:19]), twice).reshape(14, 24, 128)
    es[5:19, pl.ds(0, 24, stride=2), :] = e
    es[5:19, pl.ds(1, 24, stride=2), :] = e
    add_double(v1, es, 10, 38)
    sweep(v1, f1, op1, 11, 37)
    sweep(v1, f1, op1, 12, 36)
    e = dot(flat(v1[12:36, 12:36, :]), twice).reshape(24, 24, 128)
    es[:, pl.ds(0, 24, stride=2), :] = e
    es[:, pl.ds(1, 24, stride=2), :] = e


def turn_kernel(ng, nb, *refs):
    got, f0, wx0, ws0, wl0, di0, f1, wx1, ws1, wl1, di1, f2, wx2, ws2, wl2, di2 = refs[:16]
    v0i, v1i, v2i = refs[16:19]
    v0, packed = refs[19:21]
    v1, v2, s = refs[21:24]
    scr = refs[24:]
    v1[...] = v1i[...]
    v2[...] = v2i[...]
    op0, op1, op2 = (wx0, ws0, wl0, di0), (wx1, ws1, wl1, di1), (wx2, ws2, wl2, di2)
    climb(ng, nb, None, got, v0, f0, op0, v1, f1, op1, v2, f2, op2, scr)
    add_double(v0, scr[-1], 0, 48)
    for lo in (2, 3, 4, 5):
        sweep(v0, f0, op0, lo, 48 - lo)
    f1n = fine_restrict(v0, f0, op0, s)
    packed[...] = f1n[0:8] + pltpu.roll(f1n[8:16], 64, 2)


def end_kernel(ng, nb, *refs):
    got, got_c = refs[:2]
    f0, wx0, ws0, wl0, di0, f1, wx1, ws1, wl1, di1, f2, wx2, ws2, wl2, di2 = refs[2:17]
    v0i, v1i, v2i = refs[17:20]
    sol, res = refs[20:22]
    v0, v1, v2 = refs[22:25]
    scr = refs[25:]
    v0[...] = v0i[...]
    v1[...] = v1i[...]
    v2[...] = v2i[...]
    op0, op1, op2 = (wx0, ws0, wl0, di0), (wx1, ws1, wl1, di1), (wx2, ws2, wl2, di2)
    climb(ng, nb, got, got_c, v0, f0, op0, v1, f1, op1, v2, f2, op2, scr)
    add_double(v0, scr[-1], 4, 44)
    sweep(v0, f0, op0, 6, 42)
    sweep(v0, f0, op0, 7, 41)

    def step(x, n, _):
        rs = resid_slabs(v0, f0, op0, x + 8, n)
        for i in range(n):
            res[x + i] = rs[i][8:40]
        return 0

    sol[...] = v0[8:40, 8:40]
    blocks(0, 32, 8, step)


def ring(x, axis, n):
    before = lax.ppermute(x[0], axis, [(i, (i + 1) % n) for i in range(n)])
    after = lax.ppermute(x[1], axis, [(i, (i - 1) % n) for i in range(n)])
    return before, after


def gather_all(payload):
    got = lax.all_to_all(payload, ("grp", "box"), 0, 0, tiled=True)
    return got.reshape(got.shape[0] * got.shape[1], got.shape[2])


def make_body(ng, nb):
    big, mid, low = (48, 48, 128), (48, 48, 128), (24, 24, 128)
    n3, nl = 4 * ng, 4 * nb
    nd = ng * nb
    pay, pay2 = (nd, 4, 128), (nd, 2, 128)
    lev3 = (n3 + 8, 16, nl)
    climb_scratch = [lev3] * 7 + [(n3 // 2, 16, nl), (12, 32, nl), (24, 48, 128)]

    def fix(kernel):
        return lambda *refs: kernel(ng, nb, *refs)

    def body(f, tags, table, rough):
        coef, to_next, to_prev = call(
            coef_kernel, (f, tags, table, rough), [(32, 32, 128), (17, 32, 128), (17, 32, 128)],
            smem=(2,),
        )
        left, right = ring((to_next, to_prev), "grp", ng)
        to_next, to_prev = call(rows_kernel, (f, coef, left, right), [(105, 8, 128)] * 2)
        above, below = ring((to_next, to_prev), "box", nb)
        v0, f0, wx0, ws0, wl0, di0, packed = call(
            fix(start_kernel), (f, coef, left, right, above, below), [big] * 6 + [(16, 16, 128)],
            scratch=[(50, 48, 128), (2, 56, 128), (16, 48, 128)],
        )
        l0 = (f0, wx0, ws0, wl0, di0)
        left, right = ring((packed, packed), "grp", ng)
        wide = jnp.concatenate([left, packed, right], 0)
        above, below = ring((wide, wide), "box", nb)
        f1, v1, wx1, ws1, wl1, di1, f2, v2, wx2, ws2, wl2, di2, payload = call(
            fix(mid_kernel), (packed, left, right, above, below), [mid] * 6 + [low] * 6 + [pay],
            scratch=[(48, 48, 128), (24, 24, 128), (24, 48, 128)], leave=(12,),
        )
        got_c = gather_all(payload)
        l1, l2 = (f1, wx1, ws1, wl1, di1), (f2, wx2, ws2, wl2, di2)
        v0, packed = call(
            fix(turn_kernel), (got_c,) + l0 + l1 + l2 + (v0, v1, v2), [big, (8, 16, 128)],
            aliases={16: 0}, scratch=[mid, low, (16, 48, 128)] + climb_scratch,
        )
        left, right = ring((packed, packed), "grp", ng)
        wide = jnp.concatenate([left, packed, right], 0)
        above, below = ring((wide, wide), "box", nb)
        f1, v1, f2, v2, payload = call(
            mid2_kernel, (packed, left, right, above, below) + l1[1:] + l2[1:],
            [mid, mid, low, low, pay2], scratch=[(24, 48, 128)], leave=(4,),
        )
        got = gather_all(payload)
        l1, l2 = (f1,) + l1[1:], (f2,) + l2[1:]
        return tuple(call(
            fix(end_kernel), (got, got_c) + l0 + l1 + l2 + (v0, v1, v2), [(32, 32, 128)] * 2,
            scratch=[big, mid, low] + climb_scratch, leave=(0, 1),
        ))

    return body


def solution(mesh):
    body = make_body(mesh.shape["grp"], mesh.shape["box"])
    return jax.shard_map(
        body,
        mesh=mesh,
        in_specs=(P("grp", "box", None), P("grp", "box", None), P(), P("grp", "box", None)),
        out_specs=(P("grp", "box", None), P("grp", "box", None)),
        check_vma=False,
    )
```

```python
import jax
import jax.numpy as jnp
from jax import lax
from jax.experimental import pallas as pl
from jax.experimental.pallas import tpu as pltpu
from jax.sharding import PartitionSpec as P

F32 = jnp.float32
NB = 4
INTERPRET = False


def params():
    return pltpu.CompilerParams(vmem_limit_bytes=24 << 20)


def call(kernel, ins, outs, scratch=(), leave=(), aliases=None, hbm=(), touched=0):
    def shape_of(i, s):
        if INTERPRET or i in leave:
            return jax.ShapeDtypeStruct(s, F32)
        return pltpu.VMEM(s, F32)

    def place(i, x):
        if INTERPRET:
            return x
        return pltpu.with_memory_space_constraint(x, pltpu.HBM if i in hbm else pltpu.VMEM)

    specs = [
        pl.BlockSpec(memory_space=pl.ANY if i in hbm else pltpu.VMEM) for i in range(len(ins))
    ]
    return pl.pallas_call(
        kernel,
        out_shape=[shape_of(i, s) for i, s in enumerate(outs)],
        in_specs=specs,
        out_specs=[pl.BlockSpec(memory_space=pltpu.VMEM) for _ in outs],
        scratch_shapes=[pltpu.VMEM(s, F32) if isinstance(s, tuple) else s for s in scratch],
        compiler_params=params(),
        input_output_aliases=aliases or {},
        interpret=INTERPRET,
        cost_estimate=pl.CostEstimate(
            flops=3 * touched, bytes_accessed=touched, transcendentals=0
        )
        if touched
        else None,
    )(*[place(i, x) for i, x in enumerate(ins)])


def iota(shape, dim):
    return lax.broadcasted_iota(jnp.int32, shape, dim)


def halver(n):
    k, j = iota((n, n), 0), iota((n, n), 1)
    return jnp.where((k >> 1) == j, F32(0.5), F32(0.0))


def doubler(n):
    j, k = iota((n, n), 0), iota((n, n), 1)
    return jnp.where((k >> 1) == j, F32(1.0), F32(0.0))


def dot(a, b):
    return lax.dot_general(
        a, b, (((1,), (0,)), ((), ())), precision=lax.Precision.HIGHEST, preferred_element_type=F32
    )


def up(v, axis):
    return pltpu.roll(v, v.shape[axis] - 1, axis)


def down(v, axis):
    return pltpu.roll(v, 1, axis)


def near_sum(vc, vn, carry, wxx, wss, wll):
    t = wxx * vn + carry
    t = t + (wss * up(vc, 0) + down(wss * vc, 0))
    return t + (wll * up(vc, 1) + down(wll * vc, 1))


def blocks(lo, hi, size, fn, state=0):
    count = (hi - lo) // size
    if count > 1:
        state = lax.fori_loop(0, count, lambda i, st: fn(lo + i * size, size, st), state)
    elif count == 1:
        state = fn(lo, size, state)
    rest = (hi - lo) - count * size
    if rest:
        state = fn(hi - rest, rest, state)
    return state


def block_of(ref):
    return max(1, 384 // ref.shape[1])


def sweep(v, f, op, lo, hi):
    wx, ws, wl, di = op

    def step(x, n, state):
        carry, vc = state
        vs = [vc] + [v[x + i + 1] for i in range(n)]
        new = []
        for i in range(n):
            wxx = wx[x + i]
            t = near_sum(vs[i], vs[i + 1], carry, wxx, ws[x + i], wl[x + i])
            new.append(F32(0.2) * vs[i] + di[x + i] * (f[x + i] + t))
            carry = wxx * vs[i]
        for i in range(n):
            v[x + i] = new[i]
        return carry, vs[n]

    blocks(lo, hi, block_of(v), step, (wx[lo - 1] * v[lo - 1], v[lo]))


def first_sweep(v, f, op, lo, hi):
    di = op[3]

    def step(x, n, _):
        new = [di[x + i] * f[x + i] for i in range(n)]
        for i in range(n):
            v[x + i] = new[i]
        return 0

    blocks(lo, hi, block_of(v), step)


def resid_slabs(v, f, op, x, n):
    wx, ws, wl, di = op
    vs = [v[x + i - 1] for i in range(n + 2)]
    wxs = [wx[x + i - 1] for i in range(n + 1)]
    out = []
    for i in range(n):
        vc = vs[i + 1]
        t = near_sum(vc, vs[i + 2], wxs[i] * vs[i], wxs[i + 1], ws[x + i], wl[x + i])
        dinv = di[x + i]
        inside = dinv > 0
        diag = jnp.where(inside, F32(0.8) / jnp.where(inside, dinv, F32(1.0)), F32(0.0))
        out.append(f[x + i] - (diag * vc - t))
    return out


def resid_pairs(v, f, op, lo, n, out):
    def step(j, m, _):
        rs = resid_slabs(v, f, op, lo + 2 * j, 2 * m)
        for i in range(m):
            out[j + i] = rs[2 * i] + rs[2 * i + 1]
        return 0

    blocks(0, n, max(1, block_of(v) // 2), step)


def sum_pairs(src, lo, n, out):
    def step(j, m, _):
        new = [src[lo + 2 * (j + i)] + src[lo + 2 * (j + i) + 1] for i in range(m)]
        for i in range(m):
            out[j + i] = new[i]
        return 0

    blocks(0, n, max(1, block_of(out) // 2), step)


def weights(c, cbase, op, lo, hi, lane_last, sub_last, edge=None):
    wx, ws, wl, di = op
    ny, nl = c.shape[1:]
    half, zero = F32(0.5), F32(0.0)

    def step(x, n, _):
        x = x + cbase
        rows, lanes = iota((ny, nl), 0), iota((ny, nl), 1)
        hs = [c[x + i - 1] * half for i in range(n + 2)]
        new = []
        for i in range(n):
            ch = hs[i + 1]
            cp, cm = ch + hs[i + 2], ch + hs[i]
            s_next, s_prev = up(ch, 0), down(ch, 0)
            if sub_last:
                s_next = jnp.where(rows == ny - 1, zero, s_next)
                s_prev = jnp.where(rows == 0, zero, s_prev)
            if edge is not None:
                s_next = jnp.where(rows == ny - 1, edge[1, pl.ds(x + i, 1), :] * half, s_next)
                s_prev = jnp.where(rows == 0, edge[0, pl.ds(x + i, 1), :] * half, s_prev)
            l_next = jnp.where(lanes >= lane_last, zero, up(ch, 1))
            l_prev = jnp.where(lanes == 0, zero, down(ch, 1))
            s_up, l_up = ch + s_next, ch + l_next
            diag = (cp + cm) + (s_up + (ch + s_prev)) + (l_up + (ch + l_prev))
            inside = ch > 0
            dinv = jnp.where(inside, F32(0.8) / jnp.where(inside, diag, F32(1.0)), zero)
            s_up = jnp.where(rows == ny - 1, zero, s_up) if sub_last else s_up
            new.append((cp, s_up, jnp.where(lanes >= lane_last, zero, l_up), dinv))
        for i in range(n):
            for ref, value in zip(op, new[i]):
                ref[x - cbase + i] = value
        return 0

    blocks(lo, hi, max(1, block_of(c) // 2), step)


def pair_rows(s, start, n):
    return s[:, pl.ds(start, n, stride=2), :] + s[:, pl.ds(start + 1, n, stride=2), :]


def flat(a):
    return a.reshape(a.shape[0] * a.shape[1], a.shape[2])


def add_double(v, es, lo, hi, base=0):
    def step(x, n, _):
        new = [v[x + i] + es[((x - base) >> 1) + (i >> 1)] for i in range(n)]
        for i in range(n):
            v[x + i] = new[i]
        return 0

    blocks(lo, hi, max(2, block_of(v) & ~1), step)


def coef_kernel(
    f_hbm, tags_hbm, table_hbm, rough_hbm, coef, to_next, to_prev, packed,
    tags, table, rough, s, sems,
):
    pairs = (
        (table_hbm, table),
        (tags_hbm, tags),
        (rough_hbm, rough),
        (f_hbm.at[24:32], to_next.at[0:8]),
        (f_hbm.at[0:8], to_prev.at[0:8]),
    )
    copies = [pltpu.make_async_copy(a, b, sems.at[i]) for i, (a, b) in enumerate(pairs)]
    for copy in copies:
        copy.start()
    for copy in copies[:3]:
        copy.wait()

    def step(x, n, _):
        new = []
        for i in range(n):
            tag = tags[x + i]
            picked = jnp.zeros(tag.shape, F32)
            for region in range(8):
                picked = jnp.where(tag == region, table[region], picked)
            new.append(picked * rough[x + i])
        for i in range(n):
            coef[x + i] = new[i]
        return 0

    blocks(0, 32, 8, step)
    sum_pairs(coef, 0, 16, s)
    c1 = dot(flat(pair_rows(s, 0, 16) * F32(0.25)), halver(128)).reshape(16, 16, 128)
    packed[...] = pack_halves(c1)
    to_next[8:17] = coef[23:32]
    to_prev[8:17] = coef[0:9]
    for copy in copies[3:]:
        copy.wait()


def rows_kernel(f, coef, left, right, to_next, to_prev):
    for out, row, extra in ((to_next, 24, 23), (to_prev, 0, 8)):
        sl = slice(row, row + 8)
        out[0:8] = left[0:8, sl]
        out[8:40] = f[:, sl]
        out[40:48] = right[0:8, sl]
        out[48:57] = left[8:17, sl]
        out[57:89] = coef[:, sl]
        out[89:98] = right[8:17, sl]
        for x in range(50):
            if x < 9:
                line = left[8 + x, extra : extra + 1, :]
            elif x < 41:
                line = coef[x - 9, extra : extra + 1, :]
            else:
                line = right[8 + x - 41, extra : extra + 1, :]
            out[98 + x // 8, x % 8 : x % 8 + 1, :] = line
        out[104, 2:8, :] = jnp.zeros((6, 128), F32)


def pack_halves(a):
    return a[0:8] + pltpu.roll(a[8:16], 64, 2)


def unpack(dst, own, left, right, above, below, flags=None):
    lanes = iota((48, 128), 1)
    rows = iota((48, 128), 0)
    for k in range(3):
        scale = None
        if flags is not None:
            gl, gr, bl, br = flags
            one = F32(1.0)
            scale = jnp.where(rows < 16, bl, jnp.where(rows < 32, one, br)) * (gl, one, gr)[k]
        for i in range(8):
            if k == 1:
                slab = jnp.concatenate([above[i], own[i], below[i]], 0)
            else:
                slab = (left, None, right)[k][i]
            if scale is not None:
                slab = slab * scale
            dst[16 * k + i] = jnp.where(lanes < 64, slab, F32(0.0))
            dst[16 * k + 8 + i] = jnp.where(lanes < 64, pltpu.roll(slab, 64, 1), F32(0.0))


def edge_flags(ng, nb):
    g, b = lax.axis_index("grp"), lax.axis_index("box")
    one, zero = F32(1.0), F32(0.0)
    return (
        jnp.where(g > 0, one, zero),
        jnp.where(g < ng - 1, one, zero),
        jnp.where(b > 0, one, zero),
        jnp.where(b < nb - 1, one, zero),
    )


def fine_restrict(v, f, op, s):
    resid_pairs(v, f, op, 8, 16, s)
    pairs = pair_rows(s, 8, 16)
    return dot(flat(pairs), halver(128)).reshape(16, 16, 128)


def start_kernel(
    ng, nb, f, coef, left, right, above, below, v, fx, wx, ws, wl, di, packed, cx, edge, s
):
    gl, gr, bl, br = edge_flags(ng, nb)
    fx[0:8, 8:40] = left[0:8]
    fx[8:40, 8:40] = f[...]
    fx[40:48, 8:40] = right[0:8]
    fx[:, 0:8] = above[0:48]
    fx[:, 40:48] = below[0:48]
    cx[0:9, 8:40] = left[8:17] * gl
    cx[9:41, 8:40] = coef[...]
    cx[41:50, 8:40] = right[8:17] * gr
    for rows, src, flag in ((slice(0, 8), above, bl), (slice(40, 48), below, br)):
        cx[0:9, rows] = src[48:57] * (gl * flag)
        cx[9:41, rows] = src[57:89] * flag
        cx[41:50, rows] = src[89:98] * (gr * flag)
    for i, (src, flag) in enumerate(((above, bl), (below, br))):
        lines = flat(src[98:105])
        x = iota(lines.shape, 0)
        scale = jnp.where(x < 9, gl * flag, jnp.where(x < 41, flag, gr * flag))
        edge[i] = lines * scale
    op = (wx, ws, wl, di)
    weights(cx, 1, op, 0, 48, 127, False, edge)
    first_sweep(v, fx, op, 0, 48)
    sweep(v, fx, op, 1, 47)
    f1 = fine_restrict(v, fx, op, s)

    packed[...] = pack_halves(f1)


def fold_rows(send):
    lanes = iota((2, 128), 1)
    even = jnp.concatenate([send[0:1], send[2:3]], 0)
    odd = jnp.concatenate([send[1:2], send[3:4]], 0)
    return jnp.where(lanes < 64, even, pltpu.roll(odd, 64, 1))


def mid_down(f1, v1, op1, f2, v2, op2, s, payload, extra):
    first_sweep(v1, f1, op1, 2, 46)
    sweep(v1, f1, op1, 3, 45)
    resid_pairs(v1, f1, op1, 4, 20, s)
    half = halver(128)
    f2[2:22] = dot(flat(pair_rows(s.at[0:20], 0, 24)), half).reshape(20, 24, 128)
    first_sweep(v2, f2, op2, 2, 22)
    sweep(v2, f2, op2, 3, 21)
    resid_pairs(v2, f2, op2, 8, 4, s.at[0:4, 0:24])
    send = collect(s, half, 0, F32(1.0))
    send = fold_rows(send) if extra is None else send + extra
    payload[...] = jnp.broadcast_to(send[None], payload.shape)


def collect(s, half, lane, scale):
    total = jnp.zeros((12, 128), F32)
    lanes = iota((12, 128), 1)
    for x in range(4):
        pairs = flat(pair_rows(s.at[x : x + 1], 0, 12))
        cut = jnp.where(lanes < 16, dot(pairs * scale, half), F32(0.0))
        shift = lane + 16 * x
        total = total + (pltpu.roll(cut, shift, 1) if shift else cut)
    return total[4:8]


def mid_kernel(
    ng, nb, own, left, right, above, below, cown, cleft, cright, cabove, cbelow,
    f1, v1, wx1, ws1, wl1, di1, f2, v2, wx2, ws2, wl2, di2, payload, c1, c2, s,
):
    unpack(f1, own, left, right, above, below)
    unpack(c1, cown, cleft, cright, cabove, cbelow, edge_flags(ng, nb))
    op1, op2 = (wx1, ws1, wl1, di1), (wx2, ws2, wl2, di2)
    weights(c1, 0, op1, 1, 47, 63, False)

    sum_pairs(c1, 0, 24, s)
    half = halver(128)
    c2[...] = dot(flat(pair_rows(s, 0, 24) * F32(0.25)), half).reshape(24, 24, 128)
    weights(c2, 0, op2, 1, 23, 31, False)
    for x in range(4):
        s[x, 0:24] = c2[8 + 2 * x] + c2[9 + 2 * x]
    extra = collect(s, half, 64, F32(0.25))
    mid_down(f1, v1, op1, f2, v2, op2, s, payload, extra)


def mid2_kernel(
    own, left, right, above, below, wx1, ws1, wl1, di1, wx2, ws2, wl2, di2,
    f1, v1, f2, v2, payload, s,
):
    unpack(f1, own, left, right, above, below)
    op1, op2 = (wx1, ws1, wl1, di1), (wx2, ws2, wl2, di2)
    mid_down(f1, v1, op1, f2, v2, op2, s, payload, None)


def apply3(p, wx, ws, wl, diag):
    zero = jnp.zeros_like(p[:1])
    q = wx * jnp.concatenate([p[1:], zero], 0)
    q = q + jnp.concatenate([zero, (wx * p)[:-1]], 0)
    q = q + (ws * up(p, 1) + down(ws * p, 1))
    q = q + (wl * up(p, 2) + down(wl * p, 2))
    return diag * p - q


def bottom(f4, c4, ny4):
    nx, nz, nl = c4.shape
    ch = c4 * F32(0.5)
    zero = jnp.zeros_like(ch[:1])
    rows, lanes, slabs = iota(c4.shape, 1), iota(c4.shape, 2), iota(c4.shape, 0)
    o = F32(0.0)
    x_up = ch + jnp.concatenate([ch[1:], zero], 0)
    x_dn = ch + jnp.concatenate([zero, ch[:-1]], 0)
    s_up = ch + jnp.where(rows == nz - 1, o, up(ch, 1))
    s_dn = ch + jnp.where(rows == 0, o, down(ch, 1))
    l_up = ch + jnp.where(lanes >= ny4 - 1, o, up(ch, 2))
    l_dn = ch + jnp.where(lanes == 0, o, down(ch, 2))
    diag = x_up + x_dn + s_up + s_dn + l_up + l_dn
    wx = jnp.where(slabs == nx - 1, o, x_up)
    ws = jnp.where(rows == nz - 1, o, s_up)
    wl = jnp.where(lanes >= ny4 - 1, o, l_up)

    def total(a):
        return jnp.sum(jnp.sum(a, axis=0))

    v = None
    r = p = f4
    rr = total(r * r)
    for i in range(NB):
        q = apply3(p, wx, ws, wl, diag)
        alpha = rr / total(p * q)
        v = alpha * p if v is None else v + alpha * p
        if i < NB - 1:
            r = r - alpha * q
            new = total(r * r)
            p = r + (new / rr) * p
            rr = new
    return v


def coarse(ng, nb, got, got_c, v3, f3, op3, c3, s3):
    n3, nl = 4 * ng, 4 * nb
    for g in range(ng):
        slabs = slice(4 + 4 * g, 8 + 4 * g)
        t = got_c[g * nl : (g + 1) * nl, :].T
        c3[slabs] = t[64:128].reshape(4, 16, nl)
        if got is None:
            f3[slabs] = t[0:64].reshape(4, 16, nl)
    if got is not None:
        k, y = iota((nl // 2, nl), 0), iota((nl // 2, nl), 1)
        even = jnp.where(y == 2 * k, F32(1.0), F32(0.0))
        odd = jnp.where(y == 2 * k + 1, F32(1.0), F32(0.0))
        ts = [got[g * (nl // 2) : (g + 1) * (nl // 2), :].T for g in range(ng)]
        lhs0 = jnp.concatenate([t[0:64] for t in ts], 0)
        lhs1 = jnp.concatenate([t[64:128] for t in ts], 0)
        f3[4 : 4 + n3] = (dot(lhs0, even) + dot(lhs1, odd)).reshape(n3, 16, nl)
    pad = jnp.zeros((4, 16, nl), F32)
    for ref in (v3, c3, op3[0]):
        ref[0:4] = pad
        ref[4 + n3 : 8 + n3] = pad
    weights(c3, 0, op3, 4, 4 + n3, nl - 1, True)
    lo, hi = 4, 4 + n3
    first_sweep(v3, f3, op3, lo, hi)
    sweep(v3, f3, op3, lo, hi)
    half = halver(nl)

    sum_pairs(c3, 4, n3 // 2, s3)
    c4 = dot(flat(pair_rows(s3, 0, 8) * F32(0.25)), half).reshape(n3 // 2, 8, nl)
    resid_pairs(v3, f3, op3, 4, n3 // 2, s3)
    f4 = dot(flat(pair_rows(s3, 0, 8)), half).reshape(n3 // 2, 8, nl)
    v4 = bottom(f4, c4, nl // 2)
    e = dot(flat(v4), doubler(nl)).reshape(n3 // 2, 8, nl)
    s3[:, pl.ds(0, 8, stride=2), :] = e
    s3[:, pl.ds(1, 8, stride=2), :] = e

    add_double(v3, s3, 4, 4 + n3, 4)
    sweep(v3, f3, op3, lo, hi)
    sweep(v3, f3, op3, lo, hi)


def coarse_to_mid(nb, v3, v2, s2, nl):
    g, b = lax.axis_index("grp"), lax.axis_index("box")
    for x in range(12):
        e = v3[4 * g + x]
        s2[x : x + 1, pl.ds(0, 16, stride=2), :] = e[None]
        s2[x : x + 1, pl.ds(1, 16, stride=2), :] = e[None]
    j, y = iota((24, nl), 0), iota((24, nl), 1)
    pick = jnp.where(y == 4 * b - 4 + (j >> 1), F32(1.0), F32(0.0))
    lanes = iota((24, 128), 1)
    zero = F32(0.0)
    for q in range(3):
        block = flat(s2[4 * q : 4 * q + 4])
        e = lax.dot_general(
            pick, block, (((1,), (1,)), ((), ())),
            precision=lax.Precision.HIGHEST, preferred_element_type=F32,
        )
        for i in range(4):
            part = e if i == 0 else pltpu.roll(e, 128 - 32 * i, 1)
            part = jnp.where(lanes < 32, part, zero)
            x = 2 * (4 * q + i)
            v2[x] = v2[x] + part
            v2[x + 1] = v2[x + 1] + part


def climb(ng, nb, got, got_c, v0, f0, op0, v1, f1, op1, v2, f2, op2, scr):
    v3, f3, c3, wx3, ws3, wl3, di3, s3, s2, es = scr
    op3 = (wx3, ws3, wl3, di3)
    coarse(ng, nb, got, got_c, v3, f3, op3, c3, s3)
    coarse_to_mid(nb, v3, v2, s2, 4 * nb)
    sweep(v2, f2, op2, 4, 20)
    sweep(v2, f2, op2, 5, 19)
    twice = doubler(128)
    e = dot(flat(v2[5:19]), twice).reshape(14, 24, 128)
    es[5:19, pl.ds(0, 24, stride=2), :] = e
    es[5:19, pl.ds(1, 24, stride=2), :] = e
    v1, f1 = v1.at[:, 8:40], f1.at[:, 8:40]
    op1 = tuple(ref.at[:, 8:40] for ref in op1)
    add_double(v1, es.at[:, 8:40], 10, 38)
    sweep(v1, f1, op1, 11, 37)
    sweep(v1, f1, op1, 12, 36)
    e = dot(flat(v1[12:36, 4:28, :]), twice).reshape(24, 24, 128)
    es[:, pl.ds(0, 24, stride=2), :] = e
    es[:, pl.ds(1, 24, stride=2), :] = e


def turn_kernel(ng, nb, *refs):
    got, f0, wx0, ws0, wl0, di0, f1, wx1, ws1, wl1, di1, f2, wx2, ws2, wl2, di2 = refs[:16]
    v0i, v1i, v2i = refs[16:19]
    v0, packed = refs[19:21]
    v1, v2, s = refs[21:24]
    scr = refs[24:]
    v1[...] = v1i[...]
    v2[...] = v2i[...]
    op0, op1, op2 = (wx0, ws0, wl0, di0), (wx1, ws1, wl1, di1), (wx2, ws2, wl2, di2)
    climb(ng, nb, None, got, v0, f0, op0, v1, f1, op1, v2, f2, op2, scr)
    add_double(v0, scr[-1], 0, 48)
    for lo in (2, 3, 4, 5):
        sweep(v0, f0, op0, lo, 48 - lo)
    f1n = fine_restrict(v0, f0, op0, s)
    packed[...] = pack_halves(f1n)


def end_kernel(ng, nb, *refs):
    got, got_c = refs[:2]
    f0, wx0, ws0, wl0, di0, f1, wx1, ws1, wl1, di1, f2, wx2, ws2, wl2, di2 = refs[2:17]
    v0i, v1i, v2i = refs[17:20]
    sol, res = refs[20:22]
    v0, v1, v2 = refs[22:25]
    scr = refs[25:]
    v0[...] = v0i[...]
    v1[...] = v1i[...]
    v2[...] = v2i[...]
    op0, op1, op2 = (wx0, ws0, wl0, di0), (wx1, ws1, wl1, di1), (wx2, ws2, wl2, di2)
    climb(ng, nb, got, got_c, v0, f0, op0, v1, f1, op1, v2, f2, op2, scr)
    add_double(v0, scr[-1], 4, 44)
    sweep(v0, f0, op0, 6, 42)
    sweep(v0, f0, op0, 7, 41)

    def step(x, n, _):
        rs = resid_slabs(v0, f0, op0, x + 8, n)
        for i in range(n):
            res[x + i] = rs[i][8:40]
        return 0

    sol[...] = v0[8:40, 8:40]
    blocks(0, 32, 8, step)


def ring(x, axis, n):
    before = lax.ppermute(x[0], axis, [(i, (i + 1) % n) for i in range(n)])
    after = lax.ppermute(x[1], axis, [(i, (i - 1) % n) for i in range(n)])
    return before, after


def tall_of(packed, nb):
    above, below = ring((packed, packed), "box", nb)
    return above, below, jnp.concatenate([above, packed, below], 1)


def around(packed, ng, nb):
    above, below, tall = tall_of(packed, nb)
    left, right = ring((tall, tall), "grp", ng)
    return packed, left, right, above, below


def gather_all(payload):
    got = lax.all_to_all(payload, ("grp", "box"), 0, 0, tiled=True)
    return got.reshape(got.shape[0] * got.shape[1], got.shape[2])


def make_body(ng, nb):
    big, mid, low = (48, 48, 128), (48, 48, 128), (24, 24, 128)
    n3, nl = 4 * ng, 4 * nb
    nd = ng * nb
    pay, pay2 = (nd, 4, 128), (nd, 2, 128)
    lev3 = (n3 + 8, 16, nl)
    climb_scratch = [lev3] * 7 + [(n3 // 2, 16, nl), (12, 32, nl), (24, 48, 128)]

    def fix(kernel):
        return lambda *refs: kernel(ng, nb, *refs)

    def body(f, tags, table, rough):
        coef, to_next, to_prev, cpack = call(
            coef_kernel, (f, tags, table, rough),
            [(32, 32, 128), (17, 32, 128), (17, 32, 128), (8, 16, 128)],
            scratch=[
                pltpu.VMEM((32, 32, 128), jnp.int32), pltpu.SMEM((8,), F32), (32, 32, 128),
                (16, 32, 128), pltpu.SemaphoreType.DMA((5,)),
            ],
            hbm=(0, 1, 2, 3),
        )
        left, right = ring((to_next, to_prev), "grp", ng)
        coarse_above, coarse_below, tall = tall_of(cpack, nb)
        left, right, tall = lax.optimization_barrier((left, right, tall))
        to_next, to_prev = call(rows_kernel, (f, coef, left, right), [(105, 8, 128)] * 2)
        above, below = ring((to_next, to_prev), "box", nb)
        coarse_left, coarse_right = ring((tall, tall), "grp", ng)
        above, below, coarse_left, coarse_right = lax.optimization_barrier(
            (above, below, coarse_left, coarse_right)
        )
        coarse_coef = (cpack, coarse_left, coarse_right, coarse_above, coarse_below)
        v0, f0, wx0, ws0, wl0, di0, packed = call(
            fix(start_kernel), (f, coef, left, right, above, below), [big] * 6 + [(8, 16, 128)],
            scratch=[(50, 48, 128), (2, 56, 128), (16, 48, 128)], touched=20_000_000,
        )
        l0 = (f0, wx0, ws0, wl0, di0)
        f1, v1, wx1, ws1, wl1, di1, f2, v2, wx2, ws2, wl2, di2, payload = call(
            fix(mid_kernel), around(packed, ng, nb) + coarse_coef, [mid] * 6 + [low] * 6 + [pay],
            scratch=[(48, 48, 128), (24, 24, 128), (24, 48, 128)], leave=(12,),
        )
        got_c = gather_all(payload)
        l1, l2 = (f1, wx1, ws1, wl1, di1), (f2, wx2, ws2, wl2, di2)
        v0, packed = call(
            fix(turn_kernel), (got_c,) + l0 + l1 + l2 + (v0, v1, v2), [big, (8, 16, 128)],
            aliases={16: 0}, scratch=[mid, low, (16, 48, 128)] + climb_scratch,
        )
        f1, v1, f2, v2, payload = call(
            mid2_kernel, around(packed, ng, nb) + l1[1:] + l2[1:],
            [mid, mid, low, low, pay2], scratch=[(24, 48, 128)], leave=(4,),
        )
        got = gather_all(payload)
        l1, l2 = (f1,) + l1[1:], (f2,) + l2[1:]
        return tuple(call(
            fix(end_kernel), (got, got_c) + l0 + l1 + l2 + (v0, v1, v2), [(32, 32, 128)] * 2,
            scratch=[big, mid, low] + climb_scratch, leave=(0, 1),
        ))

    return body


def solution(mesh):
    body = make_body(mesh.shape["grp"], mesh.shape["box"])
    return jax.shard_map(
        body,
        mesh=mesh,
        in_specs=(P("grp", "box", None), P("grp", "box", None), P(), P("grp", "box", None)),
        out_specs=(P("grp", "box", None), P("grp", "box", None)),
        check_vma=False,
    )
```

```python
import jax
import jax.numpy as jnp
from jax import lax
from jax.experimental import pallas as pl
from jax.experimental.pallas import tpu as pltpu
from jax.sharding import PartitionSpec as P

F32 = jnp.float32
NB = 4
INTERPRET = False


def params():
    return pltpu.CompilerParams(vmem_limit_bytes=24 << 20)


def call(kernel, ins, outs, scratch=(), leave=(), aliases=None, hbm=(), touched=0):
    def shape_of(i, s):
        if INTERPRET or i in leave:
            return jax.ShapeDtypeStruct(s, F32)
        return pltpu.VMEM(s, F32)

    def place(i, x):
        if INTERPRET:
            return x
        return pltpu.with_memory_space_constraint(x, pltpu.HBM if i in hbm else pltpu.VMEM)

    specs = [
        pl.BlockSpec(memory_space=pl.ANY if i in hbm else pltpu.VMEM) for i in range(len(ins))
    ]
    return pl.pallas_call(
        kernel,
        out_shape=[shape_of(i, s) for i, s in enumerate(outs)],
        in_specs=specs,
        out_specs=[pl.BlockSpec(memory_space=pltpu.VMEM) for _ in outs],
        scratch_shapes=[pltpu.VMEM(s, F32) if isinstance(s, tuple) else s for s in scratch],
        compiler_params=params(),
        input_output_aliases=aliases or {},
        interpret=INTERPRET,
        cost_estimate=pl.CostEstimate(
            flops=3 * touched, bytes_accessed=touched, transcendentals=0
        )
        if touched
        else None,
    )(*[place(i, x) for i, x in enumerate(ins)])


def iota(shape, dim):
    return lax.broadcasted_iota(jnp.int32, shape, dim)


def halver(n):
    k, j = iota((n, n), 0), iota((n, n), 1)
    return jnp.where((k >> 1) == j, F32(0.5), F32(0.0))


def doubler(n):
    j, k = iota((n, n), 0), iota((n, n), 1)
    return jnp.where((k >> 1) == j, F32(1.0), F32(0.0))


def dot(a, b):
    return lax.dot_general(
        a, b, (((1,), (0,)), ((), ())), precision=lax.Precision.HIGHEST, preferred_element_type=F32
    )


def up(v, axis):
    return pltpu.roll(v, v.shape[axis] - 1, axis)


def down(v, axis):
    return pltpu.roll(v, 1, axis)


def near_sum(vc, vn, carry, wxx, wss, wll):
    t = wxx * vn + carry
    t = t + (wss * up(vc, 0) + down(wss * vc, 0))
    return t + (wll * up(vc, 1) + down(wll * vc, 1))


def blocks(lo, hi, size, fn, state=0):
    count = (hi - lo) // size
    if count > 1:
        state = lax.fori_loop(0, count, lambda i, st: fn(lo + i * size, size, st), state)
    elif count == 1:
        state = fn(lo, size, state)
    rest = (hi - lo) - count * size
    if rest:
        state = fn(hi - rest, rest, state)
    return state


def block_of(ref):
    return max(1, 384 // ref.shape[1])


def sweep(v, f, op, lo, hi):
    wx, ws, wl, di = op

    def step(x, n, state):
        carry, vc = state
        vs = [vc] + [v[x + i + 1] for i in range(n)]
        new = []
        for i in range(n):
            wxx = wx[x + i]
            t = near_sum(vs[i], vs[i + 1], carry, wxx, ws[x + i], wl[x + i])
            new.append(F32(0.2) * vs[i] + di[x + i] * (f[x + i] + t))
            carry = wxx * vs[i]
        for i in range(n):
            v[x + i] = new[i]
        return carry, vs[n]

    blocks(lo, hi, block_of(v), step, (wx[lo - 1] * v[lo - 1], v[lo]))


def first_sweep(v, f, op, lo, hi):
    di = op[3]

    def step(x, n, _):
        new = [di[x + i] * f[x + i] for i in range(n)]
        for i in range(n):
            v[x + i] = new[i]
        return 0

    blocks(lo, hi, block_of(v), step)


def resid_slabs(v, f, op, x, n):
    wx, ws, wl, di = op
    vs = [v[x + i - 1] for i in range(n + 2)]
    wxs = [wx[x + i - 1] for i in range(n + 1)]
    out = []
    for i in range(n):
        vc = vs[i + 1]
        t = near_sum(vc, vs[i + 2], wxs[i] * vs[i], wxs[i + 1], ws[x + i], wl[x + i])
        dinv = di[x + i]
        inside = dinv > 0
        diag = jnp.where(inside, F32(0.8) / jnp.where(inside, dinv, F32(1.0)), F32(0.0))
        out.append(f[x + i] - (diag * vc - t))
    return out


def resid_pairs(v, f, op, lo, n, out):
    def step(j, m, _):
        rs = resid_slabs(v, f, op, lo + 2 * j, 2 * m)
        for i in range(m):
            out[j + i] = rs[2 * i] + rs[2 * i + 1]
        return 0

    blocks(0, n, max(1, block_of(v) // 2), step)


def sum_pairs(src, lo, n, out):
    def step(j, m, _):
        new = [src[lo + 2 * (j + i)] + src[lo + 2 * (j + i) + 1] for i in range(m)]
        for i in range(m):
            out[j + i] = new[i]
        return 0

    blocks(0, n, max(1, block_of(out) // 2), step)


def weights(c, cbase, op, lo, hi, lane_last, sub_last, edge=None):
    wx, ws, wl, di = op
    ny, nl = c.shape[1:]
    half, zero = F32(0.5), F32(0.0)

    def step(x, n, _):
        x = x + cbase
        rows, lanes = iota((ny, nl), 0), iota((ny, nl), 1)
        hs = [c[x + i - 1] * half for i in range(n + 2)]
        new = []
        for i in range(n):
            ch = hs[i + 1]
            cp, cm = ch + hs[i + 2], ch + hs[i]
            s_next, s_prev = up(ch, 0), down(ch, 0)
            if sub_last:
                s_next = jnp.where(rows == ny - 1, zero, s_next)
                s_prev = jnp.where(rows == 0, zero, s_prev)
            if edge is not None:
                s_next = jnp.where(rows == ny - 1, edge[1, pl.ds(x + i, 1), :] * half, s_next)
                s_prev = jnp.where(rows == 0, edge[0, pl.ds(x + i, 1), :] * half, s_prev)
            l_next = jnp.where(lanes >= lane_last, zero, up(ch, 1))
            l_prev = jnp.where(lanes == 0, zero, down(ch, 1))
            s_up, l_up = ch + s_next, ch + l_next
            diag = (cp + cm) + (s_up + (ch + s_prev)) + (l_up + (ch + l_prev))
            inside = ch > 0
            dinv = jnp.where(inside, F32(0.8) / jnp.where(inside, diag, F32(1.0)), zero)
            s_up = jnp.where(rows == ny - 1, zero, s_up) if sub_last else s_up
            new.append((cp, s_up, jnp.where(lanes >= lane_last, zero, l_up), dinv))
        for i in range(n):
            for ref, value in zip(op, new[i]):
                ref[x - cbase + i] = value
        return 0

    blocks(lo, hi, max(1, block_of(c) // 2), step)


def pair_rows(s, start, n):
    return s[:, pl.ds(start, n, stride=2), :] + s[:, pl.ds(start + 1, n, stride=2), :]


def flat(a):
    return a.reshape(a.shape[0] * a.shape[1], a.shape[2])


def add_double(v, es, lo, hi, base=0):
    def step(x, n, _):
        new = [v[x + i] + es[((x - base) >> 1) + (i >> 1)] for i in range(n)]
        for i in range(n):
            v[x + i] = new[i]
        return 0

    blocks(lo, hi, max(2, block_of(v) & ~1), step)


def coef_kernel(
    f_hbm, tags_hbm, table_hbm, rough_hbm, coef, to_next, to_prev, packed,
    tags, table, rough, s, sems,
):
    pairs = (
        (table_hbm, table),
        (tags_hbm, tags),
        (rough_hbm, rough),
        (f_hbm.at[24:32], to_next.at[0:8]),
        (f_hbm.at[0:8], to_prev.at[0:8]),
    )
    copies = [pltpu.make_async_copy(a, b, sems.at[i]) for i, (a, b) in enumerate(pairs)]
    for copy in copies:
        copy.start()
    for copy in copies[:3]:
        copy.wait()

    def step(x, n, _):
        new = []
        for i in range(n):
            tag = tags[x + i]
            picked = jnp.zeros(tag.shape, F32)
            for region in range(8):
                picked = jnp.where(tag == region, table[region], picked)
            new.append(picked * rough[x + i])
        for i in range(n):
            coef[x + i] = new[i]
        return 0

    blocks(0, 32, 8, step)
    sum_pairs(coef, 0, 16, s)
    c1 = dot(flat(pair_rows(s, 0, 16) * F32(0.25)), halver(128)).reshape(16, 16, 128)
    packed[...] = pack_halves(c1)
    to_next[8:17] = coef[23:32]
    to_prev[8:17] = coef[0:9]
    for copy in copies[3:]:
        copy.wait()


def rows_kernel(f, coef, left, right, to_next, to_prev):
    for out, row, extra in ((to_next, 24, 23), (to_prev, 0, 8)):
        sl = slice(row, row + 8)
        out[0:8] = left[0:8, sl]
        out[8:40] = f[:, sl]
        out[40:48] = right[0:8, sl]
        out[48:57] = left[8:17, sl]
        out[57:89] = coef[:, sl]
        out[89:98] = right[8:17, sl]
        for x in range(50):
            if x < 9:
                line = left[8 + x, extra : extra + 1, :]
            elif x < 41:
                line = coef[x - 9, extra : extra + 1, :]
            else:
                line = right[8 + x - 41, extra : extra + 1, :]
            out[98 + x // 8, x % 8 : x % 8 + 1, :] = line
        out[104, 2:8, :] = jnp.zeros((6, 128), F32)


def pack_halves(a):
    return a[0:8] + pltpu.roll(a[8:16], 64, 2)


def unpack(dst, own, left, right, above, below, flags=None):
    lanes = iota((48, 128), 1)
    rows = iota((48, 128), 0)
    for k in range(3):
        scale = None
        if flags is not None:
            gl, gr, bl, br = flags
            one = F32(1.0)
            scale = jnp.where(rows < 16, bl, jnp.where(rows < 32, one, br)) * (gl, one, gr)[k]
        for i in range(8):
            if k == 1:
                slab = jnp.concatenate([above[i], own[i], below[i]], 0)
            else:
                slab = (left, None, right)[k][i]
            if scale is not None:
                slab = slab * scale
            dst[16 * k + i] = jnp.where(lanes < 64, slab, F32(0.0))
            dst[16 * k + 8 + i] = jnp.where(lanes < 64, pltpu.roll(slab, 64, 1), F32(0.0))


def edge_flags(ng, nb):
    g, b = lax.axis_index("grp"), lax.axis_index("box")
    one, zero = F32(1.0), F32(0.0)
    return (
        jnp.where(g > 0, one, zero),
        jnp.where(g < ng - 1, one, zero),
        jnp.where(b > 0, one, zero),
        jnp.where(b < nb - 1, one, zero),
    )


def fine_restrict(v, f, op, s):
    resid_pairs(v, f, op, 8, 16, s)
    pairs = pair_rows(s, 8, 16)
    return dot(flat(pairs), halver(128)).reshape(16, 16, 128)


def start_kernel(
    ng, nb, f, coef, left, right, above, below, v, fx, wx, ws, wl, di, packed, cx, edge, s
):
    gl, gr, bl, br = edge_flags(ng, nb)
    fx[0:8, 8:40] = left[0:8]
    fx[8:40, 8:40] = f[...]
    fx[40:48, 8:40] = right[0:8]
    fx[:, 0:8] = above[0:48]
    fx[:, 40:48] = below[0:48]
    cx[0:9, 8:40] = left[8:17] * gl
    cx[9:41, 8:40] = coef[...]
    cx[41:50, 8:40] = right[8:17] * gr
    for rows, src, flag in ((slice(0, 8), above, bl), (slice(40, 48), below, br)):
        cx[0:9, rows] = src[48:57] * (gl * flag)
        cx[9:41, rows] = src[57:89] * flag
        cx[41:50, rows] = src[89:98] * (gr * flag)
    for i, (src, flag) in enumerate(((above, bl), (below, br))):
        lines = flat(src[98:105])
        x = iota(lines.shape, 0)
        scale = jnp.where(x < 9, gl * flag, jnp.where(x < 41, flag, gr * flag))
        edge[i] = lines * scale
    op = (wx, ws, wl, di)
    weights(cx, 1, op, 0, 48, 127, False, edge)
    first_sweep(v, fx, op, 0, 48)
    sweep(v, fx, op, 1, 47)
    f1 = fine_restrict(v, fx, op, s)

    packed[...] = pack_halves(f1)


def fold_rows(send):
    lanes = iota((2, 128), 1)
    even = jnp.concatenate([send[0:1], send[2:3]], 0)
    odd = jnp.concatenate([send[1:2], send[3:4]], 0)
    return jnp.where(lanes < 64, even, pltpu.roll(odd, 64, 1))


def mid_down(f1, v1, op1, f2, v2, op2, s, payload, extra):
    first_sweep(v1, f1, op1, 2, 46)
    sweep(v1, f1, op1, 3, 45)
    resid_pairs(v1, f1, op1, 4, 20, s)
    half = halver(128)
    f2[2:22] = dot(flat(pair_rows(s.at[0:20], 0, 24)), half).reshape(20, 24, 128)
    first_sweep(v2, f2, op2, 2, 22)
    sweep(v2, f2, op2, 3, 21)
    resid_pairs(v2, f2, op2, 8, 4, s.at[0:4, 0:24])
    send = collect(s, half, 0, F32(1.0))
    send = fold_rows(send) if extra is None else send + extra
    payload[...] = jnp.broadcast_to(send[None], payload.shape)


def collect(s, half, lane, scale):
    total = jnp.zeros((12, 128), F32)
    lanes = iota((12, 128), 1)
    for x in range(4):
        pairs = flat(pair_rows(s.at[x : x + 1], 0, 12))
        cut = jnp.where(lanes < 16, dot(pairs * scale, half), F32(0.0))
        shift = lane + 16 * x
        total = total + (pltpu.roll(cut, shift, 1) if shift else cut)
    return total[4:8]


def mid_weights_kernel(
    ng, nb, cown, cleft, cright, cabove, cbelow,
    wx1, ws1, wl1, di1, wx2, ws2, wl2, di2, coarser, c1, c2, s,
):
    unpack(c1, cown, cleft, cright, cabove, cbelow, edge_flags(ng, nb))
    weights(c1, 0, (wx1, ws1, wl1, di1), 1, 47, 63, False)
    sum_pairs(c1, 0, 24, s)
    half = halver(128)
    c2[...] = dot(flat(pair_rows(s, 0, 24) * F32(0.25)), half).reshape(24, 24, 128)
    weights(c2, 0, (wx2, ws2, wl2, di2), 1, 23, 31, False)
    for x in range(4):
        s[x, 0:24] = c2[8 + 2 * x] + c2[9 + 2 * x]
    send = collect(s, half, 64, F32(0.25))
    coarser[...] = send


def mid_kernel(
    own, left, right, above, below, wx1, ws1, wl1, di1, wx2, ws2, wl2, di2, coarser,
    f1, v1, f2, v2, payload, s,
):
    unpack(f1, own, left, right, above, below)
    op1, op2 = (wx1, ws1, wl1, di1), (wx2, ws2, wl2, di2)
    mid_down(f1, v1, op1, f2, v2, op2, s, payload, coarser[...])


def mid2_kernel(
    own, left, right, above, below, wx1, ws1, wl1, di1, wx2, ws2, wl2, di2,
    f1, v1, f2, v2, payload, s,
):
    unpack(f1, own, left, right, above, below)
    op1, op2 = (wx1, ws1, wl1, di1), (wx2, ws2, wl2, di2)
    mid_down(f1, v1, op1, f2, v2, op2, s, payload, None)


def apply3(p, wx, ws, wl, diag):
    zero = jnp.zeros_like(p[:1])
    q = wx * jnp.concatenate([p[1:], zero], 0)
    q = q + jnp.concatenate([zero, (wx * p)[:-1]], 0)
    q = q + (ws * up(p, 1) + down(ws * p, 1))
    q = q + (wl * up(p, 2) + down(wl * p, 2))
    return diag * p - q


def bottom(f4, c4, ny4):
    nx, nz, nl = c4.shape
    ch = c4 * F32(0.5)
    zero = jnp.zeros_like(ch[:1])
    rows, lanes, slabs = iota(c4.shape, 1), iota(c4.shape, 2), iota(c4.shape, 0)
    o = F32(0.0)
    x_up = ch + jnp.concatenate([ch[1:], zero], 0)
    x_dn = ch + jnp.concatenate([zero, ch[:-1]], 0)
    s_up = ch + jnp.where(rows == nz - 1, o, up(ch, 1))
    s_dn = ch + jnp.where(rows == 0, o, down(ch, 1))
    l_up = ch + jnp.where(lanes >= ny4 - 1, o, up(ch, 2))
    l_dn = ch + jnp.where(lanes == 0, o, down(ch, 2))
    diag = x_up + x_dn + s_up + s_dn + l_up + l_dn
    wx = jnp.where(slabs == nx - 1, o, x_up)
    ws = jnp.where(rows == nz - 1, o, s_up)
    wl = jnp.where(lanes >= ny4 - 1, o, l_up)

    def total(a):
        return jnp.sum(jnp.sum(a, axis=0))

    v = None
    r = p = f4
    rr = total(r * r)
    for i in range(NB):
        q = apply3(p, wx, ws, wl, diag)
        alpha = rr / total(p * q)
        v = alpha * p if v is None else v + alpha * p
        if i < NB - 1:
            r = r - alpha * q
            new = total(r * r)
            p = r + (new / rr) * p
            rr = new
    return v


def coarse(ng, nb, got, got_c, v3, f3, op3, c3, s3):
    n3, nl = 4 * ng, 4 * nb
    for g in range(ng):
        slabs = slice(4 + 4 * g, 8 + 4 * g)
        t = got_c[g * nl : (g + 1) * nl, :].T
        c3[slabs] = t[64:128].reshape(4, 16, nl)
        if got is None:
            f3[slabs] = t[0:64].reshape(4, 16, nl)
    if got is not None:
        k, y = iota((nl // 2, nl), 0), iota((nl // 2, nl), 1)
        even = jnp.where(y == 2 * k, F32(1.0), F32(0.0))
        odd = jnp.where(y == 2 * k + 1, F32(1.0), F32(0.0))
        ts = [got[g * (nl // 2) : (g + 1) * (nl // 2), :].T for g in range(ng)]
        lhs0 = jnp.concatenate([t[0:64] for t in ts], 0)
        lhs1 = jnp.concatenate([t[64:128] for t in ts], 0)
        f3[4 : 4 + n3] = (dot(lhs0, even) + dot(lhs1, odd)).reshape(n3, 16, nl)
    pad = jnp.zeros((4, 16, nl), F32)
    for ref in (v3, c3, op3[0]):
        ref[0:4] = pad
        ref[4 + n3 : 8 + n3] = pad
    weights(c3, 0, op3, 4, 4 + n3, nl - 1, True)
    lo, hi = 4, 4 + n3
    first_sweep(v3, f3, op3, lo, hi)
    sweep(v3, f3, op3, lo, hi)
    half = halver(nl)

    sum_pairs(c3, 4, n3 // 2, s3)
    c4 = dot(flat(pair_rows(s3, 0, 8) * F32(0.25)), half).reshape(n3 // 2, 8, nl)
    resid_pairs(v3, f3, op3, 4, n3 // 2, s3)
    f4 = dot(flat(pair_rows(s3, 0, 8)), half).reshape(n3 // 2, 8, nl)
    v4 = bottom(f4, c4, nl // 2)
    e = dot(flat(v4), doubler(nl)).reshape(n3 // 2, 8, nl)
    s3[:, pl.ds(0, 8, stride=2), :] = e
    s3[:, pl.ds(1, 8, stride=2), :] = e

    add_double(v3, s3, 4, 4 + n3, 4)
    sweep(v3, f3, op3, lo, hi)
    sweep(v3, f3, op3, lo, hi)


def coarse_to_mid(nb, v3, v2, s2, nl):
    g, b = lax.axis_index("grp"), lax.axis_index("box")
    for x in range(12):
        e = v3[4 * g + x]
        s2[x : x + 1, pl.ds(0, 16, stride=2), :] = e[None]
        s2[x : x + 1, pl.ds(1, 16, stride=2), :] = e[None]
    j, y = iota((24, nl), 0), iota((24, nl), 1)
    pick = jnp.where(y == 4 * b - 4 + (j >> 1), F32(1.0), F32(0.0))
    lanes = iota((24, 128), 1)
    zero = F32(0.0)
    for q in range(3):
        block = flat(s2[4 * q : 4 * q + 4])
        e = lax.dot_general(
            pick, block, (((1,), (1,)), ((), ())),
            precision=lax.Precision.HIGHEST, preferred_element_type=F32,
        )
        for i in range(4):
            part = e if i == 0 else pltpu.roll(e, 128 - 32 * i, 1)
            part = jnp.where(lanes < 32, part, zero)
            x = 2 * (4 * q + i)
            v2[x] = v2[x] + part
            v2[x + 1] = v2[x + 1] + part


def climb(ng, nb, got, got_c, v0, f0, op0, v1, f1, op1, v2, f2, op2, scr):
    v3, f3, c3, wx3, ws3, wl3, di3, s3, s2, es = scr
    op3 = (wx3, ws3, wl3, di3)
    coarse(ng, nb, got, got_c, v3, f3, op3, c3, s3)
    coarse_to_mid(nb, v3, v2, s2, 4 * nb)
    sweep(v2, f2, op2, 4, 20)
    sweep(v2, f2, op2, 5, 19)
    twice = doubler(128)
    e = dot(flat(v2[5:19]), twice).reshape(14, 24, 128)
    es[5:19, pl.ds(0, 24, stride=2), :] = e
    es[5:19, pl.ds(1, 24, stride=2), :] = e
    v1, f1 = v1.at[:, 8:40], f1.at[:, 8:40]
    op1 = tuple(ref.at[:, 8:40] for ref in op1)
    add_double(v1, es.at[:, 8:40], 10, 38)
    sweep(v1, f1, op1, 11, 37)
    sweep(v1, f1, op1, 12, 36)
    e = dot(flat(v1[12:36, 4:28, :]), twice).reshape(24, 24, 128)
    es[:, pl.ds(0, 24, stride=2), :] = e
    es[:, pl.ds(1, 24, stride=2), :] = e


def turn_kernel(ng, nb, *refs):
    got, f0, wx0, ws0, wl0, di0, f1, wx1, ws1, wl1, di1, f2, wx2, ws2, wl2, di2 = refs[:16]
    v0i, v1i, v2i = refs[16:19]
    v0, packed = refs[19:21]
    v1, v2, s = refs[21:24]
    scr = refs[24:]
    v1[...] = v1i[...]
    v2[...] = v2i[...]
    op0, op1, op2 = (wx0, ws0, wl0, di0), (wx1, ws1, wl1, di1), (wx2, ws2, wl2, di2)
    climb(ng, nb, None, got, v0, f0, op0, v1, f1, op1, v2, f2, op2, scr)
    add_double(v0, scr[-1], 0, 48)
    for lo in (2, 3, 4, 5):
        sweep(v0, f0, op0, lo, 48 - lo)
    f1n = fine_restrict(v0, f0, op0, s)
    packed[...] = pack_halves(f1n)


def end_kernel(ng, nb, *refs):
    got, got_c = refs[:2]
    f0, wx0, ws0, wl0, di0, f1, wx1, ws1, wl1, di1, f2, wx2, ws2, wl2, di2 = refs[2:17]
    v0i, v1i, v2i = refs[17:20]
    sol, res = refs[20:22]
    v0, v1, v2 = refs[22:25]
    scr = refs[25:]
    v0[...] = v0i[...]
    v1[...] = v1i[...]
    v2[...] = v2i[...]
    op0, op1, op2 = (wx0, ws0, wl0, di0), (wx1, ws1, wl1, di1), (wx2, ws2, wl2, di2)
    climb(ng, nb, got, got_c, v0, f0, op0, v1, f1, op1, v2, f2, op2, scr)
    add_double(v0, scr[-1], 4, 44)
    sweep(v0, f0, op0, 6, 42)
    sweep(v0, f0, op0, 7, 41)

    def step(x, n, _):
        rs = resid_slabs(v0, f0, op0, x + 8, n)
        for i in range(n):
            res[x + i] = rs[i][8:40]
        return 0

    sol[...] = v0[8:40, 8:40]
    blocks(0, 32, 8, step)


def ring(x, axis, n):
    before = lax.ppermute(x[0], axis, [(i, (i + 1) % n) for i in range(n)])
    after = lax.ppermute(x[1], axis, [(i, (i - 1) % n) for i in range(n)])
    return before, after


def tall_of(packed, nb):
    above, below = ring((packed, packed), "box", nb)
    return above, below, jnp.concatenate([above, packed, below], 1)


def around(packed, ng, nb):
    above, below, tall = tall_of(packed, nb)
    left, right = ring((tall, tall), "grp", ng)
    return packed, left, right, above, below


def gather_all(payload):
    got = lax.all_to_all(payload, ("grp", "box"), 0, 0, tiled=True)
    return got.reshape(got.shape[0] * got.shape[1], got.shape[2])


def make_body(ng, nb):
    big, mid, low = (48, 48, 128), (48, 48, 128), (24, 24, 128)
    n3, nl = 4 * ng, 4 * nb
    nd = ng * nb
    pay, pay2 = (nd, 4, 128), (nd, 2, 128)
    lev3 = (n3 + 8, 16, nl)
    climb_scratch = [lev3] * 7 + [(n3 // 2, 16, nl), (12, 32, nl), (24, 48, 128)]

    def fix(kernel):
        return lambda *refs: kernel(ng, nb, *refs)

    def body(f, tags, table, rough):
        coef, to_next, to_prev, cpack = call(
            coef_kernel, (f, tags, table, rough),
            [(32, 32, 128), (17, 32, 128), (17, 32, 128), (8, 16, 128)],
            scratch=[
                pltpu.VMEM((32, 32, 128), jnp.int32), pltpu.SMEM((8,), F32), (32, 32, 128),
                (16, 32, 128), pltpu.SemaphoreType.DMA((5,)),
            ],
            hbm=(0, 1, 2, 3),
        )
        left, right = ring((to_next, to_prev), "grp", ng)
        coarse_above, coarse_below, tall = tall_of(cpack, nb)
        left, right, tall = lax.optimization_barrier((left, right, tall))
        to_next, to_prev = call(rows_kernel, (f, coef, left, right), [(105, 8, 128)] * 2)
        above, below = ring((to_next, to_prev), "box", nb)
        coarse_left, coarse_right = ring((tall, tall), "grp", ng)
        above, below, coarse_left, coarse_right = lax.optimization_barrier(
            (above, below, coarse_left, coarse_right)
        )
        coarse_coef = (cpack, coarse_left, coarse_right, coarse_above, coarse_below)
        v0, f0, wx0, ws0, wl0, di0, packed = call(
            fix(start_kernel), (f, coef, left, right, above, below), [big] * 6 + [(8, 16, 128)],
            scratch=[(50, 48, 128), (2, 56, 128), (16, 48, 128)], touched=20_000_000,
        )
        l0 = (f0, wx0, ws0, wl0, di0)
        *ops, coarser = call(
            fix(mid_weights_kernel), coarse_coef, [mid] * 4 + [low] * 4 + [(4, 128)],
            scratch=[(48, 48, 128), (24, 24, 128), (24, 48, 128)],
        )
        f1, v1, f2, v2, payload = call(
            mid_kernel, around(packed, ng, nb) + tuple(ops) + (coarser,),
            [mid, mid, low, low, pay], scratch=[(24, 48, 128)], leave=(4,),
        )
        got_c = gather_all(payload)
        l1, l2 = (f1, *ops[:4]), (f2, *ops[4:])
        v0, packed = call(
            fix(turn_kernel), (got_c,) + l0 + l1 + l2 + (v0, v1, v2), [big, (8, 16, 128)],
            aliases={16: 0}, scratch=[mid, low, (16, 48, 128)] + climb_scratch,
        )
        f1, v1, f2, v2, payload = call(
            mid2_kernel, around(packed, ng, nb) + l1[1:] + l2[1:],
            [mid, mid, low, low, pay2], scratch=[(24, 48, 128)], leave=(4,),
        )
        got = gather_all(payload)
        l1, l2 = (f1,) + l1[1:], (f2,) + l2[1:]
        return tuple(call(
            fix(end_kernel), (got, got_c) + l0 + l1 + l2 + (v0, v1, v2), [(32, 32, 128)] * 2,
            scratch=[big, mid, low] + climb_scratch, leave=(0, 1),
        ))

    return body


def solution(mesh):
    body = make_body(mesh.shape["grp"], mesh.shape["box"])
    return jax.shard_map(
        body,
        mesh=mesh,
        in_specs=(P("grp", "box", None), P("grp", "box", None), P(), P("grp", "box", None)),
        out_specs=(P("grp", "box", None), P("grp", "box", None)),
        check_vma=False,
    )
```

```python
import jax
import jax.numpy as jnp
from jax import lax
from jax.experimental import pallas as pl
from jax.experimental.pallas import tpu as pltpu
from jax.sharding import PartitionSpec as P

F32 = jnp.float32
NB = 4
INTERPRET = False


def params():
    return pltpu.CompilerParams(vmem_limit_bytes=24 << 20)


def call(kernel, ins, outs, scratch=(), leave=(), aliases=None, hbm=(), touched=0):
    def shape_of(i, s):
        if INTERPRET or i in leave:
            return jax.ShapeDtypeStruct(s, F32)
        return pltpu.VMEM(s, F32)

    def place(i, x):
        if INTERPRET:
            return x
        return pltpu.with_memory_space_constraint(x, pltpu.HBM if i in hbm else pltpu.VMEM)

    specs = [
        pl.BlockSpec(memory_space=pl.ANY if i in hbm else pltpu.VMEM) for i in range(len(ins))
    ]
    return pl.pallas_call(
        kernel,
        out_shape=[shape_of(i, s) for i, s in enumerate(outs)],
        in_specs=specs,
        out_specs=[pl.BlockSpec(memory_space=pltpu.VMEM) for _ in outs],
        scratch_shapes=[pltpu.VMEM(s, F32) if isinstance(s, tuple) else s for s in scratch],
        compiler_params=params(),
        input_output_aliases=aliases or {},
        interpret=INTERPRET,
        cost_estimate=pl.CostEstimate(
            flops=3 * touched, bytes_accessed=touched, transcendentals=0
        )
        if touched
        else None,
    )(*[place(i, x) for i, x in enumerate(ins)])


def iota(shape, dim):
    return lax.broadcasted_iota(jnp.int32, shape, dim)


def halver(n):
    k, j = iota((n, n), 0), iota((n, n), 1)
    return jnp.where((k >> 1) == j, F32(0.5), F32(0.0))


def doubler(n):
    j, k = iota((n, n), 0), iota((n, n), 1)
    return jnp.where((k >> 1) == j, F32(1.0), F32(0.0))


def halver_at(h):
    k, j = iota((128, 128), 0), iota((128, 128), 1)
    return jnp.where((k >> 1) + 64 * h == j, F32(0.5), F32(0.0))


def doubler_at(h):
    j, k = iota((128, 128), 0), iota((128, 128), 1)
    return jnp.where((k >> 1) + 64 * h == j, F32(1.0), F32(0.0))


def folder():
    k, j = iota((128, 128), 0), iota((128, 128), 1)
    return jnp.where(((k & 63) >> 1) == j, F32(0.5), F32(0.0))


def spreader():
    j, k = iota((128, 128), 0), iota((128, 128), 1)
    return jnp.where(((k & 63) >> 1) == j, F32(1.0), F32(0.0))


def dot(a, b):
    return lax.dot_general(
        a, b, (((1,), (0,)), ((), ())), precision=lax.Precision.HIGHEST, preferred_element_type=F32
    )


def up(v, axis):
    return pltpu.roll(v, v.shape[axis] - 1, axis)


def down(v, axis):
    return pltpu.roll(v, 1, axis)


def two_next(here, after):
    low = iota(here.shape, 1) < 64
    return pltpu.roll(jnp.where(low, after, here), 64, 1)


def two_prev(here, before):
    low = iota(here.shape, 1) < 64
    return pltpu.roll(jnp.where(low, here, before), 64, 1)


def near_sum(vc, vn, carry, wxx, wss, wll):
    t = wxx * vn + carry
    t = t + (wss * up(vc, 0) + down(wss * vc, 0))
    return t + (wll * up(vc, 1) + down(wll * vc, 1))


def blocks(lo, hi, size, fn, state=0):
    count = (hi - lo) // size
    if count > 1:
        state = lax.fori_loop(0, count, lambda i, st: fn(lo + i * size, size, st), state)
    elif count == 1:
        state = fn(lo, size, state)
    rest = (hi - lo) - count * size
    if rest:
        state = fn(hi - rest, rest, state)
    return state


def block_of(ref):
    return max(1, 384 // ref.shape[1])


def sweep(v, f, op, lo, hi, two=False):
    wx, ws, wl, di = op

    def step(x, n, state):
        carry, vc = state
        vs = [vc] + [v[x + i + 1] for i in range(n)]
        new = []
        for i in range(n):
            wxx = wx[x + i]
            after, before = vs[i + 1], carry
            carry = wxx * vs[i]
            if two:
                after, before = two_next(vs[i], after), two_prev(carry, before)
            t = near_sum(vs[i], after, before, wxx, ws[x + i], wl[x + i])
            new.append(F32(0.2) * vs[i] + di[x + i] * (f[x + i] + t))
        for i in range(n):
            v[x + i] = new[i]
        return carry, vs[n]

    blocks(lo, hi, block_of(v), step, (wx[lo - 1] * v[lo - 1], v[lo]))


def first_sweep(v, f, op, lo, hi):
    di = op[3]

    def step(x, n, _):
        new = [di[x + i] * f[x + i] for i in range(n)]
        for i in range(n):
            v[x + i] = new[i]
        return 0

    blocks(lo, hi, block_of(v), step)


def resid_slabs(v, f, op, x, n, two=False):
    wx, ws, wl, di = op
    vs = [v[x + i - 1] for i in range(n + 2)]
    wxs = [wx[x + i - 1] for i in range(n + 1)]
    out = []
    for i in range(n):
        vc = vs[i + 1]
        after, before = vs[i + 2], wxs[i] * vs[i]
        if two:
            after, before = two_next(vc, after), two_prev(wxs[i + 1] * vc, before)
        t = near_sum(vc, after, before, wxs[i + 1], ws[x + i], wl[x + i])
        dinv = di[x + i]
        inside = dinv > 0
        diag = jnp.where(inside, F32(0.8) / jnp.where(inside, dinv, F32(1.0)), F32(0.0))
        out.append(f[x + i] - (diag * vc - t))
    return out


def resid_pairs(v, f, op, lo, n, out):
    def step(j, m, _):
        rs = resid_slabs(v, f, op, lo + 2 * j, 2 * m)
        for i in range(m):
            out[j + i] = rs[2 * i] + rs[2 * i + 1]
        return 0

    blocks(0, n, max(1, block_of(v) // 2), step)


def resid_each(v, f, op, lo, n, out):
    def step(j, m, _):
        rs = resid_slabs(v, f, op, lo + j, m, True)
        for i in range(m):
            out[j + i] = rs[i]
        return 0

    blocks(0, n, block_of(v), step)


def sum_pairs(src, lo, n, out):
    def step(j, m, _):
        new = [src[lo + 2 * (j + i)] + src[lo + 2 * (j + i) + 1] for i in range(m)]
        for i in range(m):
            out[j + i] = new[i]
        return 0

    blocks(0, n, max(1, block_of(out) // 2), step)


def weights(c, cbase, op, lo, hi, lane_last, sub_last, edge=None, two=False):
    wx, ws, wl, di = op
    ny, nl = c.shape[1:]
    half, zero = F32(0.5), F32(0.0)

    def step(x, n, _):
        x = x + cbase
        rows, lanes = iota((ny, nl), 0), iota((ny, nl), 1)
        last, first = lanes >= lane_last, lanes == 0
        if two:
            last, first = (lanes & 63) == 63, (lanes & 63) == 0
        hs = [c[x + i - 1] * half for i in range(n + 2)]
        new = []
        for i in range(n):
            ch = hs[i + 1]
            after, before = hs[i + 2], hs[i]
            if two:
                after, before = two_next(ch, after), two_prev(ch, before)
            cp, cm = ch + after, ch + before
            s_next, s_prev = up(ch, 0), down(ch, 0)
            if sub_last:
                s_next = jnp.where(rows == ny - 1, zero, s_next)
                s_prev = jnp.where(rows == 0, zero, s_prev)
            if edge is not None:
                s_next = jnp.where(rows == ny - 1, edge[1, pl.ds(x + i, 1), :] * half, s_next)
                s_prev = jnp.where(rows == 0, edge[0, pl.ds(x + i, 1), :] * half, s_prev)
            l_next = jnp.where(last, zero, up(ch, 1))
            l_prev = jnp.where(first, zero, down(ch, 1))
            s_up, l_up = ch + s_next, ch + l_next
            diag = (cp + cm) + (s_up + (ch + s_prev)) + (l_up + (ch + l_prev))
            inside = ch > 0
            dinv = jnp.where(inside, F32(0.8) / jnp.where(inside, diag, F32(1.0)), zero)
            s_up = jnp.where(rows == ny - 1, zero, s_up) if sub_last else s_up
            new.append((cp, s_up, jnp.where(last, zero, l_up), dinv))
        for i in range(n):
            for ref, value in zip(op, new[i]):
                ref[x - cbase + i] = value
        return 0

    blocks(lo, hi, max(1, block_of(c) // 2), step)


def pair_rows(s, start, n):
    return s[:, pl.ds(start, n, stride=2), :] + s[:, pl.ds(start + 1, n, stride=2), :]


def flat(a):
    return a.reshape(a.shape[0] * a.shape[1], a.shape[2])


def add_double(v, es, lo, hi, base=0):
    def step(x, n, _):
        new = [v[x + i] + es[((x - base) >> 1) + (i >> 1)] for i in range(n)]
        for i in range(n):
            v[x + i] = new[i]
        return 0

    blocks(lo, hi, max(2, block_of(v) & ~1), step)


def coef_kernel(
    f_hbm, tags_hbm, table_hbm, rough_hbm, coef, to_next, to_prev, packed,
    tags, table, rough, s, sems,
):
    pairs = (
        (table_hbm, table),
        (tags_hbm, tags),
        (rough_hbm, rough),
        (f_hbm.at[24:32], to_next.at[0:8]),
        (f_hbm.at[0:8], to_prev.at[0:8]),
    )
    copies = [pltpu.make_async_copy(a, b, sems.at[i]) for i, (a, b) in enumerate(pairs)]
    for copy in copies:
        copy.start()
    for copy in copies[:3]:
        copy.wait()

    def step(x, n, _):
        new = []
        for i in range(n):
            tag = tags[x + i]
            picked = jnp.zeros(tag.shape, F32)
            for region in range(8):
                picked = jnp.where(tag == region, table[region], picked)
            new.append(picked * rough[x + i])
        for i in range(n):
            coef[x + i] = new[i]
        return 0

    blocks(0, 32, 8, step)
    sum_pairs(coef, 0, 16, s)
    packed[...] = to_level1(pair_rows(s, 0, 16) * F32(0.25))
    to_next[8:17] = coef[23:32]
    to_prev[8:17] = coef[0:9]
    for copy in copies[3:]:
        copy.wait()


def rows_kernel(f, coef, left, right, to_next, to_prev):
    for out, row, extra in ((to_next, 24, 23), (to_prev, 0, 8)):
        sl = slice(row, row + 8)
        out[0:8] = left[0:8, sl]
        out[8:40] = f[:, sl]
        out[40:48] = right[0:8, sl]
        out[48:57] = left[8:17, sl]
        out[57:89] = coef[:, sl]
        out[89:98] = right[8:17, sl]
        for x in range(50):
            if x < 9:
                line = left[8 + x, extra : extra + 1, :]
            elif x < 41:
                line = coef[x - 9, extra : extra + 1, :]
            else:
                line = right[8 + x - 41, extra : extra + 1, :]
            out[98 + x // 8, x % 8 : x % 8 + 1, :] = line
        out[104, 2:8, :] = jnp.zeros((6, 128), F32)


def to_level1(pairs):
    halves = pairs.reshape(8, 2, 16, 128)
    even, odd = halves[:, 0].reshape(128, 128), halves[:, 1].reshape(128, 128)
    return (dot(even, halver_at(0)) + dot(odd, halver_at(1))).reshape(8, 16, 128)


def assemble(dst, own, left, right, above, below, flags=None):
    one = F32(1.0)
    gl, gr, bl, br = flags or (one, one, one, one)
    rows = iota((48, 128), 0)
    for k, side in enumerate((left, None, right)):
        if flags is not None:
            scale = jnp.where(rows < 16, bl, jnp.where(rows < 32, one, br)) * (gl, one, gr)[k]
        for i in range(8):
            slab = jnp.concatenate([above[i], own[i], below[i]], 0) if side is None else side[i]
            dst[8 * k + i] = slab if flags is None else slab * scale


def edge_flags(ng, nb):
    g, b = lax.axis_index("grp"), lax.axis_index("box")
    one, zero = F32(1.0), F32(0.0)
    return (
        jnp.where(g > 0, one, zero),
        jnp.where(g < ng - 1, one, zero),
        jnp.where(b > 0, one, zero),
        jnp.where(b < nb - 1, one, zero),
    )


def fine_restrict(v, f, op, s):
    resid_pairs(v, f, op, 8, 16, s)
    return to_level1(pair_rows(s, 8, 16))


def start_kernel(
    ng, nb, f, coef, left, right, above, below, v, fx, wx, ws, wl, di, packed, cx, edge, s
):
    gl, gr, bl, br = edge_flags(ng, nb)
    fx[0:8, 8:40] = left[0:8]
    fx[8:40, 8:40] = f[...]
    fx[40:48, 8:40] = right[0:8]
    fx[:, 0:8] = above[0:48]
    fx[:, 40:48] = below[0:48]
    cx[0:9, 8:40] = left[8:17] * gl
    cx[9:41, 8:40] = coef[...]
    cx[41:50, 8:40] = right[8:17] * gr
    for rows, src, flag in ((slice(0, 8), above, bl), (slice(40, 48), below, br)):
        cx[0:9, rows] = src[48:57] * (gl * flag)
        cx[9:41, rows] = src[57:89] * flag
        cx[41:50, rows] = src[89:98] * (gr * flag)
    for i, (src, flag) in enumerate(((above, bl), (below, br))):
        lines = flat(src[98:105])
        x = iota(lines.shape, 0)
        scale = jnp.where(x < 9, gl * flag, jnp.where(x < 41, flag, gr * flag))
        edge[i] = lines * scale
    op = (wx, ws, wl, di)
    weights(cx, 1, op, 0, 48, 127, False, edge)
    first_sweep(v, fx, op, 0, 48)
    sweep(v, fx, op, 1, 47)
    packed[...] = fine_restrict(v, fx, op, s)


def fold_rows(send):
    lanes = iota((2, 128), 1)
    even = jnp.concatenate([send[0:1], send[2:3]], 0)
    odd = jnp.concatenate([send[1:2], send[3:4]], 0)
    return jnp.where(lanes < 64, even, pltpu.roll(odd, 64, 1))


def mid_down(f1, v1, op1, f2, v2, op2, s, payload, extra):
    v1[0] = v1[23] = jnp.zeros((48, 128), F32)
    first_sweep(v1, f1, op1, 1, 23)
    sweep(v1, f1, op1, 1, 23, True)
    resid_each(v1, f1, op1, 2, 20, s)
    half = halver(128)
    f2[2:22] = dot(flat(pair_rows(s.at[0:20], 0, 24)), folder()).reshape(20, 24, 128)
    first_sweep(v2, f2, op2, 2, 22)
    sweep(v2, f2, op2, 3, 21)
    resid_pairs(v2, f2, op2, 8, 4, s.at[0:4, 0:24])
    send = collect(s, half, 0, F32(1.0))
    send = fold_rows(send) if extra is None else send + extra
    payload[...] = jnp.broadcast_to(send[None], payload.shape)


def collect(s, half, lane, scale):
    total = jnp.zeros((12, 128), F32)
    lanes = iota((12, 128), 1)
    for x in range(4):
        pairs = flat(pair_rows(s.at[x : x + 1], 0, 12))
        cut = jnp.where(lanes < 16, dot(pairs * scale, half), F32(0.0))
        shift = lane + 16 * x
        total = total + (pltpu.roll(cut, shift, 1) if shift else cut)
    return total[4:8]


def mid_weights_kernel(
    ng, nb, cown, cleft, cright, cabove, cbelow,
    wx1, ws1, wl1, di1, wx2, ws2, wl2, di2, coarser, c1, c2, s,
):
    assemble(c1, cown, cleft, cright, cabove, cbelow, edge_flags(ng, nb))
    wx1[0] = jnp.zeros((48, 128), F32)
    weights(c1, 0, (wx1, ws1, wl1, di1), 1, 23, 127, False, None, True)
    half = halver(128)
    c2[...] = dot(flat(pair_rows(c1, 0, 24) * F32(0.25)), folder()).reshape(24, 24, 128)
    weights(c2, 0, (wx2, ws2, wl2, di2), 1, 23, 31, False)
    for x in range(4):
        s[x, 0:24] = c2[8 + 2 * x] + c2[9 + 2 * x]
    send = collect(s, half, 64, F32(0.25))
    coarser[...] = send


def mid_kernel(
    own, left, right, above, below, wx1, ws1, wl1, di1, wx2, ws2, wl2, di2, coarser,
    f1, v1, f2, v2, payload, s,
):
    assemble(f1, own, left, right, above, below)
    op1, op2 = (wx1, ws1, wl1, di1), (wx2, ws2, wl2, di2)
    mid_down(f1, v1, op1, f2, v2, op2, s, payload, coarser[...])


def mid2_kernel(
    own, left, right, above, below, wx1, ws1, wl1, di1, wx2, ws2, wl2, di2,
    f1, v1, f2, v2, payload, s,
):
    assemble(f1, own, left, right, above, below)
    op1, op2 = (wx1, ws1, wl1, di1), (wx2, ws2, wl2, di2)
    mid_down(f1, v1, op1, f2, v2, op2, s, payload, None)


def apply3(p, wx, ws, wl, diag):
    zero = jnp.zeros_like(p[:1])
    q = wx * jnp.concatenate([p[1:], zero], 0)
    q = q + jnp.concatenate([zero, (wx * p)[:-1]], 0)
    q = q + (ws * up(p, 1) + down(ws * p, 1))
    q = q + (wl * up(p, 2) + down(wl * p, 2))
    return diag * p - q


def bottom(f4, c4, ny4):
    nx, nz, nl = c4.shape
    ch = c4 * F32(0.5)
    zero = jnp.zeros_like(ch[:1])
    rows, lanes, slabs = iota(c4.shape, 1), iota(c4.shape, 2), iota(c4.shape, 0)
    o = F32(0.0)
    x_up = ch + jnp.concatenate([ch[1:], zero], 0)
    x_dn = ch + jnp.concatenate([zero, ch[:-1]], 0)
    s_up = ch + jnp.where(rows == nz - 1, o, up(ch, 1))
    s_dn = ch + jnp.where(rows == 0, o, down(ch, 1))
    l_up = ch + jnp.where(lanes >= ny4 - 1, o, up(ch, 2))
    l_dn = ch + jnp.where(lanes == 0, o, down(ch, 2))
    diag = x_up + x_dn + s_up + s_dn + l_up + l_dn
    wx = jnp.where(slabs == nx - 1, o, x_up)
    ws = jnp.where(rows == nz - 1, o, s_up)
    wl = jnp.where(lanes >= ny4 - 1, o, l_up)

    def total(a):
        return jnp.sum(jnp.sum(a, axis=0))

    v = None
    r = p = f4
    rr = total(r * r)
    for i in range(NB):
        q = apply3(p, wx, ws, wl, diag)
        alpha = rr / total(p * q)
        v = alpha * p if v is None else v + alpha * p
        if i < NB - 1:
            r = r - alpha * q
            new = total(r * r)
            p = r + (new / rr) * p
            rr = new
    return v


def coarse(ng, nb, got, got_c, v3, f3, op3, c3, s3):
    n3, nl = 4 * ng, 4 * nb
    for g in range(ng):
        slabs = slice(4 + 4 * g, 8 + 4 * g)
        t = got_c[g * nl : (g + 1) * nl, :].T
        c3[slabs] = t[64:128].reshape(4, 16, nl)
        if got is None:
            f3[slabs] = t[0:64].reshape(4, 16, nl)
    if got is not None:
        k, y = iota((nl // 2, nl), 0), iota((nl // 2, nl), 1)
        even = jnp.where(y == 2 * k, F32(1.0), F32(0.0))
        odd = jnp.where(y == 2 * k + 1, F32(1.0), F32(0.0))
        ts = [got[g * (nl // 2) : (g + 1) * (nl // 2), :].T for g in range(ng)]
        lhs0 = jnp.concatenate([t[0:64] for t in ts], 0)
        lhs1 = jnp.concatenate([t[64:128] for t in ts], 0)
        f3[4 : 4 + n3] = (dot(lhs0, even) + dot(lhs1, odd)).reshape(n3, 16, nl)
    pad = jnp.zeros((4, 16, nl), F32)
    for ref in (v3, c3, op3[0]):
        ref[0:4] = pad
        ref[4 + n3 : 8 + n3] = pad
    weights(c3, 0, op3, 4, 4 + n3, nl - 1, True)
    lo, hi = 4, 4 + n3
    first_sweep(v3, f3, op3, lo, hi)
    sweep(v3, f3, op3, lo, hi)
    half = halver(nl)

    sum_pairs(c3, 4, n3 // 2, s3)
    c4 = dot(flat(pair_rows(s3, 0, 8) * F32(0.25)), half).reshape(n3 // 2, 8, nl)
    resid_pairs(v3, f3, op3, 4, n3 // 2, s3)
    f4 = dot(flat(pair_rows(s3, 0, 8)), half).reshape(n3 // 2, 8, nl)
    v4 = bottom(f4, c4, nl // 2)
    e = dot(flat(v4), doubler(nl)).reshape(n3 // 2, 8, nl)
    s3[:, pl.ds(0, 8, stride=2), :] = e
    s3[:, pl.ds(1, 8, stride=2), :] = e

    add_double(v3, s3, 4, 4 + n3, 4)
    sweep(v3, f3, op3, lo, hi)
    sweep(v3, f3, op3, lo, hi)


def coarse_to_mid(nb, v3, v2, s2, nl):
    g, b = lax.axis_index("grp"), lax.axis_index("box")
    for x in range(12):
        e = v3[4 * g + x]
        s2[x : x + 1, pl.ds(0, 16, stride=2), :] = e[None]
        s2[x : x + 1, pl.ds(1, 16, stride=2), :] = e[None]
    j, y = iota((24, nl), 0), iota((24, nl), 1)
    pick = jnp.where(y == 4 * b - 4 + (j >> 1), F32(1.0), F32(0.0))
    lanes = iota((24, 128), 1)
    zero = F32(0.0)
    for q in range(3):
        block = flat(s2[4 * q : 4 * q + 4])
        e = lax.dot_general(
            pick, block, (((1,), (1,)), ((), ())),
            precision=lax.Precision.HIGHEST, preferred_element_type=F32,
        )
        for i in range(4):
            part = e if i == 0 else pltpu.roll(e, 128 - 32 * i, 1)
            part = jnp.where(lanes < 32, part, zero)
            x = 2 * (4 * q + i)
            v2[x] = v2[x] + part
            v2[x + 1] = v2[x + 1] + part


def climb(ng, nb, got, got_c, v0, f0, op0, v1, f1, op1, v2, f2, op2, scr):
    v3, f3, c3, wx3, ws3, wl3, di3, s3, s2, es = scr
    op3 = (wx3, ws3, wl3, di3)
    coarse(ng, nb, got, got_c, v3, f3, op3, c3, s3)
    coarse_to_mid(nb, v3, v2, s2, 4 * nb)
    sweep(v2, f2, op2, 4, 20)
    sweep(v2, f2, op2, 5, 19)
    e = dot(flat(v2[5:19]), spreader()).reshape(14, 24, 128)
    es[5:19, pl.ds(0, 24, stride=2), :] = e
    es[5:19, pl.ds(1, 24, stride=2), :] = e
    v1, f1 = v1.at[:, 8:40], f1.at[:, 8:40]
    op1 = tuple(ref.at[:, 8:40] for ref in op1)
    for i in range(5, 19):
        v1[i] = v1[i] + es[i, 8:40]
    sweep(v1, f1, op1, 5, 19, True)
    sweep(v1, f1, op1, 6, 18, True)
    rows = flat(v1[6:18, 4:28, :])
    e = [dot(rows, doubler_at(h)).reshape(12, 1, 24, 128) for h in (0, 1)]
    e = jnp.concatenate(e, 1).reshape(24, 24, 128)
    es[:, pl.ds(0, 24, stride=2), :] = e
    es[:, pl.ds(1, 24, stride=2), :] = e


def turn_kernel(ng, nb, *refs):
    got, f0, wx0, ws0, wl0, di0, f1, wx1, ws1, wl1, di1, f2, wx2, ws2, wl2, di2 = refs[:16]
    v0i, v1i, v2i = refs[16:19]
    v0, packed = refs[19:21]
    v1, v2, s = refs[21:24]
    scr = refs[24:]
    v1[...] = v1i[...]
    v2[...] = v2i[...]
    op0, op1, op2 = (wx0, ws0, wl0, di0), (wx1, ws1, wl1, di1), (wx2, ws2, wl2, di2)
    climb(ng, nb, None, got, v0, f0, op0, v1, f1, op1, v2, f2, op2, scr)
    add_double(v0, scr[-1], 0, 48)
    for lo in (2, 3, 4, 5):
        sweep(v0, f0, op0, lo, 48 - lo)
    packed[...] = fine_restrict(v0, f0, op0, s)


def end_kernel(ng, nb, *refs):
    got, got_c = refs[:2]
    f0, wx0, ws0, wl0, di0, f1, wx1, ws1, wl1, di1, f2, wx2, ws2, wl2, di2 = refs[2:17]
    v0i, v1i, v2i = refs[17:20]
    sol, res = refs[20:22]
    v0, v1, v2 = refs[22:25]
    scr = refs[25:]
    v0[...] = v0i[...]
    v1[...] = v1i[...]
    v2[...] = v2i[...]
    op0, op1, op2 = (wx0, ws0, wl0, di0), (wx1, ws1, wl1, di1), (wx2, ws2, wl2, di2)
    climb(ng, nb, got, got_c, v0, f0, op0, v1, f1, op1, v2, f2, op2, scr)
    add_double(v0, scr[-1], 4, 44)
    sweep(v0, f0, op0, 6, 42)
    sweep(v0, f0, op0, 7, 41)

    def step(x, n, _):
        rs = resid_slabs(v0, f0, op0, x + 8, n)
        for i in range(n):
            res[x + i] = rs[i][8:40]
        return 0

    sol[...] = v0[8:40, 8:40]
    blocks(0, 32, 8, step)


def ring(x, axis, n):
    before = lax.ppermute(x[0], axis, [(i, (i + 1) % n) for i in range(n)])
    after = lax.ppermute(x[1], axis, [(i, (i - 1) % n) for i in range(n)])
    return before, after


def tall_of(packed, nb):
    above, below = ring((packed, packed), "box", nb)
    return above, below, jnp.concatenate([above, packed, below], 1)


def around(packed, ng, nb):
    above, below, tall = tall_of(packed, nb)
    left, right = ring((tall, tall), "grp", ng)
    return packed, left, right, above, below


def gather_all(payload):
    got = lax.all_to_all(payload, ("grp", "box"), 0, 0, tiled=True)
    return got.reshape(got.shape[0] * got.shape[1], got.shape[2])


def make_body(ng, nb):
    big, mid, low = (48, 48, 128), (24, 48, 128), (24, 24, 128)
    n3, nl = 4 * ng, 4 * nb
    nd = ng * nb
    pay, pay2 = (nd, 4, 128), (nd, 2, 128)
    lev3 = (n3 + 8, 16, nl)
    climb_scratch = [lev3] * 7 + [(n3 // 2, 16, nl), (12, 32, nl), (24, 48, 128)]

    def fix(kernel):
        return lambda *refs: kernel(ng, nb, *refs)

    def body(f, tags, table, rough):
        coef, to_next, to_prev, cpack = call(
            coef_kernel, (f, tags, table, rough),
            [(32, 32, 128), (17, 32, 128), (17, 32, 128), (8, 16, 128)],
            scratch=[
                pltpu.VMEM((32, 32, 128), jnp.int32), pltpu.SMEM((8,), F32), (32, 32, 128),
                (16, 32, 128), pltpu.SemaphoreType.DMA((5,)),
            ],
            hbm=(0, 1, 2, 3),
        )
        left, right = ring((to_next, to_prev), "grp", ng)
        to_next, to_prev = call(rows_kernel, (f, coef, left, right), [(105, 8, 128)] * 2)
        above, below = ring((to_next, to_prev), "box", nb)
        coarse_above, coarse_below, tall = tall_of(cpack, nb)
        above, below, tall = lax.optimization_barrier((above, below, tall))
        coarse_left, coarse_right = ring((tall, tall), "grp", ng)
        coarse_coef = (cpack, coarse_left, coarse_right, coarse_above, coarse_below)
        v0, f0, wx0, ws0, wl0, di0, packed = call(
            fix(start_kernel), (f, coef, left, right, above, below), [big] * 6 + [(8, 16, 128)],
            scratch=[(50, 48, 128), (2, 56, 128), (16, 48, 128)], touched=20_000_000,
        )
        l0 = (f0, wx0, ws0, wl0, di0)
        *ops, coarser = call(
            fix(mid_weights_kernel), coarse_coef, [mid] * 4 + [low] * 4 + [(4, 128)],
            scratch=[mid, low, mid],
        )
        f1, v1, f2, v2, payload = call(
            mid_kernel, around(packed, ng, nb) + tuple(ops) + (coarser,),
            [mid, mid, low, low, pay], scratch=[(24, 48, 128)], leave=(4,),
        )
        got_c = gather_all(payload)
        l1, l2 = (f1, *ops[:4]), (f2, *ops[4:])
        v0, packed = call(
            fix(turn_kernel), (got_c,) + l0 + l1 + l2 + (v0, v1, v2), [big, (8, 16, 128)],
            aliases={16: 0}, scratch=[mid, low, (16, 48, 128)] + climb_scratch,
        )
        f1, v1, f2, v2, payload = call(
            mid2_kernel, around(packed, ng, nb) + l1[1:] + l2[1:],
            [mid, mid, low, low, pay2], scratch=[(24, 48, 128)], leave=(4,),
        )
        got = gather_all(payload)
        l1, l2 = (f1,) + l1[1:], (f2,) + l2[1:]
        return tuple(call(
            fix(end_kernel), (got, got_c) + l0 + l1 + l2 + (v0, v1, v2), [(32, 32, 128)] * 2,
            scratch=[big, mid, low] + climb_scratch, leave=(0, 1),
        ))

    return body


def solution(mesh):
    body = make_body(mesh.shape["grp"], mesh.shape["box"])
    return jax.shard_map(
        body,
        mesh=mesh,
        in_specs=(P("grp", "box", None), P("grp", "box", None), P(), P("grp", "box", None)),
        out_specs=(P("grp", "box", None), P("grp", "box", None)),
        check_vma=False,
    )
```

```python
import jax
import jax.numpy as jnp
from jax import lax
from jax.experimental import pallas as pl
from jax.experimental.pallas import tpu as pltpu
from jax.sharding import PartitionSpec as P

F32 = jnp.float32
NB = 4
INTERPRET = False


def params():
    return pltpu.CompilerParams(vmem_limit_bytes=24 << 20)


def call(kernel, ins, outs, scratch=(), leave=(), aliases=None, hbm=(), touched=0):
    def shape_of(i, s):
        if INTERPRET or i in leave:
            return jax.ShapeDtypeStruct(s, F32)
        return pltpu.VMEM(s, F32)

    def place(i, x):
        if INTERPRET:
            return x
        return pltpu.with_memory_space_constraint(x, pltpu.HBM if i in hbm else pltpu.VMEM)

    specs = [
        pl.BlockSpec(memory_space=pl.ANY if i in hbm else pltpu.VMEM) for i in range(len(ins))
    ]
    return pl.pallas_call(
        kernel,
        out_shape=[shape_of(i, s) for i, s in enumerate(outs)],
        in_specs=specs,
        out_specs=[pl.BlockSpec(memory_space=pltpu.VMEM) for _ in outs],
        scratch_shapes=[pltpu.VMEM(s, F32) if isinstance(s, tuple) else s for s in scratch],
        compiler_params=params(),
        input_output_aliases=aliases or {},
        interpret=INTERPRET,
        cost_estimate=pl.CostEstimate(
            flops=3 * touched, bytes_accessed=touched, transcendentals=0
        )
        if touched
        else None,
    )(*[place(i, x) for i, x in enumerate(ins)])


def iota(shape, dim):
    return lax.broadcasted_iota(jnp.int32, shape, dim)


def halver(n):
    k, j = iota((n, n), 0), iota((n, n), 1)
    return jnp.where((k >> 1) == j, F32(0.5), F32(0.0))


def doubler(n):
    j, k = iota((n, n), 0), iota((n, n), 1)
    return jnp.where((k >> 1) == j, F32(1.0), F32(0.0))


def halver_at(h):
    k, j = iota((128, 128), 0), iota((128, 128), 1)
    return jnp.where((k >> 1) + 64 * h == j, F32(0.5), F32(0.0))


def doubler_at(h):
    j, k = iota((128, 128), 0), iota((128, 128), 1)
    return jnp.where((k >> 1) + 64 * h == j, F32(1.0), F32(0.0))


def folder():
    k, j = iota((128, 128), 0), iota((128, 128), 1)
    return jnp.where(((k & 63) >> 1) == j, F32(0.5), F32(0.0))


def spreader():
    j, k = iota((128, 128), 0), iota((128, 128), 1)
    return jnp.where(((k & 63) >> 1) == j, F32(1.0), F32(0.0))


def dot(a, b):
    return lax.dot_general(
        a, b, (((1,), (0,)), ((), ())), precision=lax.Precision.HIGHEST, preferred_element_type=F32
    )


def up(v, axis):
    return pltpu.roll(v, v.shape[axis] - 1, axis)


def down(v, axis):
    return pltpu.roll(v, 1, axis)


def two_next(here, after):
    low = iota(here.shape, 1) < 64
    return pltpu.roll(jnp.where(low, after, here), 64, 1)


def two_prev(here, before):
    low = iota(here.shape, 1) < 64
    return pltpu.roll(jnp.where(low, here, before), 64, 1)


def near_sum(vc, vn, carry, wxx, wss, wll):
    t = wxx * vn + carry
    t = t + (wss * up(vc, 0) + down(wss * vc, 0))
    return t + (wll * up(vc, 1) + down(wll * vc, 1))


def blocks(lo, hi, size, fn, state=0):
    count = (hi - lo) // size
    if count > 1:
        state = lax.fori_loop(0, count, lambda i, st: fn(lo + i * size, size, st), state)
    elif count == 1:
        state = fn(lo, size, state)
    rest = (hi - lo) - count * size
    if rest:
        state = fn(hi - rest, rest, state)
    return state


def block_of(ref):
    return max(1, 384 // ref.shape[1])


def sweep(v, f, op, lo, hi, two=False):
    wx, ws, wl, di = op

    def step(x, n, state):
        carry, vc = state
        vs = [vc] + [v[x + i + 1] for i in range(n)]
        new = []
        for i in range(n):
            wxx = wx[x + i]
            after, before = vs[i + 1], carry
            carry = wxx * vs[i]
            if two:
                after, before = two_next(vs[i], after), two_prev(carry, before)
            t = near_sum(vs[i], after, before, wxx, ws[x + i], wl[x + i])
            new.append(F32(0.2) * vs[i] + di[x + i] * (f[x + i] + t))
        for i in range(n):
            v[x + i] = new[i]
        return carry, vs[n]

    blocks(lo, hi, block_of(v), step, (wx[lo - 1] * v[lo - 1], v[lo]))


def first_sweep(v, f, op, lo, hi):
    di = op[3]

    def step(x, n, _):
        new = [di[x + i] * f[x + i] for i in range(n)]
        for i in range(n):
            v[x + i] = new[i]
        return 0

    blocks(lo, hi, block_of(v), step)


def resid_slabs(v, f, op, x, n, two=False):
    wx, ws, wl, di = op
    vs = [v[x + i - 1] for i in range(n + 2)]
    wxs = [wx[x + i - 1] for i in range(n + 1)]
    out = []
    for i in range(n):
        vc = vs[i + 1]
        after, before = vs[i + 2], wxs[i] * vs[i]
        if two:
            after, before = two_next(vc, after), two_prev(wxs[i + 1] * vc, before)
        t = near_sum(vc, after, before, wxs[i + 1], ws[x + i], wl[x + i])
        dinv = di[x + i]
        inside = dinv > 0
        diag = jnp.where(inside, F32(0.8) / jnp.where(inside, dinv, F32(1.0)), F32(0.0))
        out.append(f[x + i] - (diag * vc - t))
    return out


def resid_pairs(v, f, op, lo, n, out):
    def step(j, m, _):
        rs = resid_slabs(v, f, op, lo + 2 * j, 2 * m)
        for i in range(m):
            out[j + i] = rs[2 * i] + rs[2 * i + 1]
        return 0

    blocks(0, n, max(1, block_of(v) // 2), step)


def resid_each(v, f, op, lo, n, out):
    def step(j, m, _):
        rs = resid_slabs(v, f, op, lo + j, m, True)
        for i in range(m):
            out[j + i] = rs[i]
        return 0

    blocks(0, n, block_of(v), step)


def sum_pairs(src, lo, n, out):
    def step(j, m, _):
        new = [src[lo + 2 * (j + i)] + src[lo + 2 * (j + i) + 1] for i in range(m)]
        for i in range(m):
            out[j + i] = new[i]
        return 0

    blocks(0, n, max(1, block_of(out) // 2), step)


def weights(c, cbase, op, lo, hi, lane_last, sub_last, edge=None, two=False):
    wx, ws, wl, di = op
    ny, nl = c.shape[1:]
    half, zero = F32(0.5), F32(0.0)

    def step(x, n, _):
        x = x + cbase
        rows, lanes = iota((ny, nl), 0), iota((ny, nl), 1)
        last, first = lanes >= lane_last, lanes == 0
        if two:
            last, first = (lanes & 63) == 63, (lanes & 63) == 0
        hs = [c[x + i - 1] * half for i in range(n + 2)]
        new = []
        for i in range(n):
            ch = hs[i + 1]
            after, before = hs[i + 2], hs[i]
            if two:
                after, before = two_next(ch, after), two_prev(ch, before)
            cp, cm = ch + after, ch + before
            s_next, s_prev = up(ch, 0), down(ch, 0)
            if sub_last:
                s_next = jnp.where(rows == ny - 1, zero, s_next)
                s_prev = jnp.where(rows == 0, zero, s_prev)
            if edge is not None:
                s_next = jnp.where(rows == ny - 1, edge[1, pl.ds(x + i, 1), :] * half, s_next)
                s_prev = jnp.where(rows == 0, edge[0, pl.ds(x + i, 1), :] * half, s_prev)
            l_next = jnp.where(last, zero, up(ch, 1))
            l_prev = jnp.where(first, zero, down(ch, 1))
            s_up, l_up = ch + s_next, ch + l_next
            diag = (cp + cm) + (s_up + (ch + s_prev)) + (l_up + (ch + l_prev))
            inside = ch > 0
            dinv = jnp.where(inside, F32(0.8) / jnp.where(inside, diag, F32(1.0)), zero)
            s_up = jnp.where(rows == ny - 1, zero, s_up) if sub_last else s_up
            new.append((cp, s_up, jnp.where(last, zero, l_up), dinv))
        for i in range(n):
            for ref, value in zip(op, new[i]):
                ref[x - cbase + i] = value
        return 0

    blocks(lo, hi, max(1, block_of(c) // 2), step)


def pair_rows(s, start, n):
    return s[:, pl.ds(start, n, stride=2), :] + s[:, pl.ds(start + 1, n, stride=2), :]


def flat(a):
    return a.reshape(a.shape[0] * a.shape[1], a.shape[2])


def add_double(v, es, lo, hi, base=0):
    def step(x, n, _):
        new = [v[x + i] + es[((x - base) >> 1) + (i >> 1)] for i in range(n)]
        for i in range(n):
            v[x + i] = new[i]
        return 0

    blocks(lo, hi, max(2, block_of(v) & ~1), step)


def coef_kernel(
    f_hbm, tags_hbm, table_hbm, rough_hbm, coef, to_next, to_prev, packed,
    tags, table, rough, s, sems,
):
    pairs = (
        (table_hbm, table),
        (tags_hbm, tags),
        (rough_hbm, rough),
        (f_hbm.at[:, 24:32], to_next.at[0:32]),
        (f_hbm.at[:, 0:8], to_prev.at[0:32]),
    )
    copies = [pltpu.make_async_copy(a, b, sems.at[i]) for i, (a, b) in enumerate(pairs)]
    for copy in copies:
        copy.start()
    for copy in copies[:3]:
        copy.wait()

    def step(x, n, _):
        new = []
        for i in range(n):
            tag = tags[x + i]
            picked = jnp.zeros(tag.shape, F32)
            for region in range(8):
                picked = jnp.where(tag == region, table[region], picked)
            new.append(picked * rough[x + i])
        for i in range(n):
            coef[x + i] = new[i]
        return 0

    blocks(0, 32, 8, step)
    sum_pairs(coef, 0, 16, s)
    c1 = to_level1(pair_rows(s, 0, 16) * F32(0.25))
    packed[...] = c1
    for out, row, extra in ((to_next, 24, 23), (to_prev, 0, 8)):
        out[32:64] = coef[:, row : row + 8]
        for x in range(32):
            out[64 + x // 8, x % 8 : x % 8 + 1, :] = coef[x, extra : extra + 1, :]
        out[68:84] = c1.reshape(16, 8, 128)
    for copy in copies[3:]:
        copy.wait()


def slabs_kernel(f, coef, packed, above, below, to_next, to_prev):
    for out, fs, cs in (
        (to_next, slice(24, 32), slice(23, 32)),
        (to_prev, slice(0, 8), slice(0, 9)),
    ):
        out[0:8, 8:40] = f[fs]
        out[8:17, 8:40] = coef[cs]
        out[17] = jnp.zeros((48, 128), F32)
        for rows, src, line in ((slice(0, 8), above, 0), (slice(40, 48), below, 16)):
            out[0:8, rows] = src[fs]
            out[8:17, rows] = src[32 + cs.start : 32 + cs.stop]
            out[17, line : line + 9] = flat(src[64:68])[cs]
        for i in range(8):
            out[18 + i] = tall_slab(packed, above, below, i)


def tall_slab(packed, above, below, i):
    parts = [above[68 + 2 * i], above[69 + 2 * i], packed[i], below[68 + 2 * i], below[69 + 2 * i]]
    return jnp.concatenate(parts, 0)


def to_level1(pairs):
    halves = pairs.reshape(8, 2, 16, 128)
    even, odd = halves[:, 0].reshape(128, 128), halves[:, 1].reshape(128, 128)
    return (dot(even, halver_at(0)) + dot(odd, halver_at(1))).reshape(8, 16, 128)


def assemble(dst, own, left, right, above, below):
    for i in range(8):
        dst[i] = left[i]
        dst[8 + i] = jnp.concatenate([above[i], own[i], below[i]], 0)
        dst[16 + i] = right[i]


def edge_flags(ng, nb):
    g, b = lax.axis_index("grp"), lax.axis_index("box")
    one, zero = F32(1.0), F32(0.0)
    return (
        jnp.where(g > 0, one, zero),
        jnp.where(g < ng - 1, one, zero),
        jnp.where(b > 0, one, zero),
        jnp.where(b < nb - 1, one, zero),
    )


def fine_restrict(v, f, op, s):
    resid_pairs(v, f, op, 8, 16, s)
    return to_level1(pair_rows(s, 8, 16))


def start_kernel(
    ng, nb, f, coef, left, right, above, below, v, fx, wx, ws, wl, di, packed, cx, edge, s
):
    gl, gr, bl, br = edge_flags(ng, nb)
    fx[0:8] = left[0:8]
    fx[8:40, 8:40] = f[...]
    fx[8:40, 0:8] = above[0:32]
    fx[8:40, 40:48] = below[0:32]
    fx[40:48] = right[0:8]
    rows = iota((48, 128), 0)
    tall = jnp.where(rows < 8, bl, jnp.where(rows < 40, F32(1.0), br))
    cx[0:9] = left[8:17] * (tall * gl)[None]
    cx[9:41, 8:40] = coef[...]
    cx[9:41, 0:8] = above[32:64] * bl
    cx[9:41, 40:48] = below[32:64] * br
    cx[41:50] = right[8:17] * (tall * gr)[None]
    for i, (src, flag) in enumerate(((above, bl), (below, br))):
        line = 16 * i
        edge[i, 0:9] = left[17, line : line + 9] * (gl * flag)
        edge[i, 9:41] = flat(src[64:68]) * flag
        edge[i, 41:50] = right[17, line : line + 9] * (gr * flag)
    op = (wx, ws, wl, di)
    weights(cx, 1, op, 0, 48, 127, False, edge)
    first_sweep(v, fx, op, 0, 48)
    sweep(v, fx, op, 1, 47)
    packed[...] = fine_restrict(v, fx, op, s)


def fold_rows(send):
    lanes = iota((2, 128), 1)
    even = jnp.concatenate([send[0:1], send[2:3]], 0)
    odd = jnp.concatenate([send[1:2], send[3:4]], 0)
    return jnp.where(lanes < 64, even, pltpu.roll(odd, 64, 1))


def mid_down(f1, v1, op1, f2, v2, op2, s, payload, extra):
    v1[0] = v1[23] = jnp.zeros((48, 128), F32)
    first_sweep(v1, f1, op1, 1, 23)
    sweep(v1, f1, op1, 1, 23, True)
    resid_each(v1, f1, op1, 2, 20, s)
    half = halver(128)
    f2[2:22] = dot(flat(pair_rows(s.at[0:20], 0, 24)), folder()).reshape(20, 24, 128)
    first_sweep(v2, f2, op2, 2, 22)
    sweep(v2, f2, op2, 3, 21)
    resid_pairs(v2, f2, op2, 8, 4, s.at[0:4, 0:24])
    send = collect(s, half, 0, F32(1.0))
    send = fold_rows(send) if extra is None else send + extra
    payload[...] = jnp.broadcast_to(send[None], payload.shape)


def collect(s, half, lane, scale):
    total = jnp.zeros((12, 128), F32)
    lanes = iota((12, 128), 1)
    for x in range(4):
        pairs = flat(pair_rows(s.at[x : x + 1], 0, 12))
        cut = jnp.where(lanes < 16, dot(pairs * scale, half), F32(0.0))
        shift = lane + 16 * x
        total = total + (pltpu.roll(cut, shift, 1) if shift else cut)
    return total[4:8]


def mid_weights_kernel(
    ng, nb, packed, left, right, above, below,
    wx1, ws1, wl1, di1, wx2, ws2, wl2, di2, coarser, c1, c2, s,
):
    gl, gr, bl, br = edge_flags(ng, nb)
    rows = iota((48, 128), 0)
    scale = jnp.where(rows < 16, bl, jnp.where(rows < 32, F32(1.0), br))
    for i in range(8):
        c1[i] = left[18 + i] * (scale * gl)
        c1[8 + i] = tall_slab(packed, above, below, i) * scale
        c1[16 + i] = right[18 + i] * (scale * gr)
    wx1[0] = jnp.zeros((48, 128), F32)
    weights(c1, 0, (wx1, ws1, wl1, di1), 1, 23, 127, False, None, True)
    half = halver(128)
    c2[...] = dot(flat(pair_rows(c1, 0, 24) * F32(0.25)), folder()).reshape(24, 24, 128)
    weights(c2, 0, (wx2, ws2, wl2, di2), 1, 23, 31, False)
    for x in range(4):
        s[x, 0:24] = c2[8 + 2 * x] + c2[9 + 2 * x]
    send = collect(s, half, 64, F32(0.25))
    coarser[...] = send


def mid_kernel(
    own, left, right, above, below, wx1, ws1, wl1, di1, wx2, ws2, wl2, di2, coarser,
    f1, v1, f2, v2, payload, s,
):
    assemble(f1, own, left, right, above, below)
    op1, op2 = (wx1, ws1, wl1, di1), (wx2, ws2, wl2, di2)
    mid_down(f1, v1, op1, f2, v2, op2, s, payload, coarser[...])


def mid2_kernel(
    own, left, right, above, below, wx1, ws1, wl1, di1, wx2, ws2, wl2, di2,
    f1, v1, f2, v2, payload, s,
):
    assemble(f1, own, left, right, above, below)
    op1, op2 = (wx1, ws1, wl1, di1), (wx2, ws2, wl2, di2)
    mid_down(f1, v1, op1, f2, v2, op2, s, payload, None)


def apply3(p, wx, ws, wl, diag):
    zero = jnp.zeros_like(p[:1])
    q = wx * jnp.concatenate([p[1:], zero], 0)
    q = q + jnp.concatenate([zero, (wx * p)[:-1]], 0)
    q = q + (ws * up(p, 1) + down(ws * p, 1))
    q = q + (wl * up(p, 2) + down(wl * p, 2))
    return diag * p - q


def bottom(f4, c4, ny4):
    nx, nz, nl = c4.shape
    ch = c4 * F32(0.5)
    zero = jnp.zeros_like(ch[:1])
    rows, lanes, slabs = iota(c4.shape, 1), iota(c4.shape, 2), iota(c4.shape, 0)
    o = F32(0.0)
    x_up = ch + jnp.concatenate([ch[1:], zero], 0)
    x_dn = ch + jnp.concatenate([zero, ch[:-1]], 0)
    s_up = ch + jnp.where(rows == nz - 1, o, up(ch, 1))
    s_dn = ch + jnp.where(rows == 0, o, down(ch, 1))
    l_up = ch + jnp.where(lanes >= ny4 - 1, o, up(ch, 2))
    l_dn = ch + jnp.where(lanes == 0, o, down(ch, 2))
    diag = x_up + x_dn + s_up + s_dn + l_up + l_dn
    wx = jnp.where(slabs == nx - 1, o, x_up)
    ws = jnp.where(rows == nz - 1, o, s_up)
    wl = jnp.where(lanes >= ny4 - 1, o, l_up)

    def total(a):
        for axis in range(3):
            a = jnp.sum(a, axis=axis, keepdims=True)
        return a

    v = None
    r = p = f4
    rr = total(r * r)
    for i in range(NB):
        q = apply3(p, wx, ws, wl, diag)
        alpha = rr / total(p * q)
        v = alpha * p if v is None else v + alpha * p
        if i < NB - 1:
            r = r - alpha * q
            new = total(r * r)
            p = r + (new / rr) * p
            rr = new
    return v


def coarse(ng, nb, got, got_c, v3, f3, op3, c3, s3):
    n3, nl = 4 * ng, 4 * nb
    for g in range(ng):
        slabs = slice(4 + 4 * g, 8 + 4 * g)
        t = got_c[g * nl : (g + 1) * nl, :].T
        c3[slabs] = t[64:128].reshape(4, 16, nl)
        if got is None:
            f3[slabs] = t[0:64].reshape(4, 16, nl)
    if got is not None:
        k, y = iota((nl // 2, nl), 0), iota((nl // 2, nl), 1)
        even = jnp.where(y == 2 * k, F32(1.0), F32(0.0))
        odd = jnp.where(y == 2 * k + 1, F32(1.0), F32(0.0))
        ts = [got[g * (nl // 2) : (g + 1) * (nl // 2), :].T for g in range(ng)]
        lhs0 = jnp.concatenate([t[0:64] for t in ts], 0)
        lhs1 = jnp.concatenate([t[64:128] for t in ts], 0)
        f3[4 : 4 + n3] = (dot(lhs0, even) + dot(lhs1, odd)).reshape(n3, 16, nl)
    pad = jnp.zeros((4, 16, nl), F32)
    for ref in (v3, c3, op3[0]):
        ref[0:4] = pad
        ref[4 + n3 : 8 + n3] = pad
    weights(c3, 0, op3, 4, 4 + n3, nl - 1, True)
    lo, hi = 4, 4 + n3
    first_sweep(v3, f3, op3, lo, hi)
    sweep(v3, f3, op3, lo, hi)
    half = halver(nl)

    sum_pairs(c3, 4, n3 // 2, s3)
    c4 = dot(flat(pair_rows(s3, 0, 8) * F32(0.25)), half).reshape(n3 // 2, 8, nl)
    resid_pairs(v3, f3, op3, 4, n3 // 2, s3)
    f4 = dot(flat(pair_rows(s3, 0, 8)), half).reshape(n3 // 2, 8, nl)
    v4 = bottom(f4, c4, nl // 2)
    e = dot(flat(v4), doubler(nl)).reshape(n3 // 2, 8, nl)
    s3[:, pl.ds(0, 8, stride=2), :] = e
    s3[:, pl.ds(1, 8, stride=2), :] = e

    add_double(v3, s3, 4, 4 + n3, 4)
    sweep(v3, f3, op3, lo, hi)
    sweep(v3, f3, op3, lo, hi)


def coarse_to_mid(nb, v3, v2, s2, nl):
    g, b = lax.axis_index("grp"), lax.axis_index("box")
    for x in range(12):
        e = v3[4 * g + x]
        s2[x : x + 1, pl.ds(0, 16, stride=2), :] = e[None]
        s2[x : x + 1, pl.ds(1, 16, stride=2), :] = e[None]
    j, y = iota((24, nl), 0), iota((24, nl), 1)
    pick = jnp.where(y == 4 * b - 4 + (j >> 1), F32(1.0), F32(0.0))
    lanes = iota((24, 128), 1)
    zero = F32(0.0)
    for q in range(3):
        block = flat(s2[4 * q : 4 * q + 4])
        e = lax.dot_general(
            pick, block, (((1,), (1,)), ((), ())),
            precision=lax.Precision.HIGHEST, preferred_element_type=F32,
        )
        for i in range(4):
            part = e if i == 0 else pltpu.roll(e, 128 - 32 * i, 1)
            part = jnp.where(lanes < 32, part, zero)
            x = 2 * (4 * q + i)
            v2[x] = v2[x] + part
            v2[x + 1] = v2[x + 1] + part


def climb(ng, nb, got, got_c, v0, f0, op0, v1, f1, op1, v2, f2, op2, scr):
    v3, f3, c3, wx3, ws3, wl3, di3, s3, s2, es = scr
    op3 = (wx3, ws3, wl3, di3)
    coarse(ng, nb, got, got_c, v3, f3, op3, c3, s3)
    coarse_to_mid(nb, v3, v2, s2, 4 * nb)
    sweep(v2, f2, op2, 4, 20)
    sweep(v2, f2, op2, 5, 19)
    e = dot(flat(v2[5:19]), spreader()).reshape(14, 24, 128)
    es[5:19, pl.ds(0, 24, stride=2), :] = e
    es[5:19, pl.ds(1, 24, stride=2), :] = e
    v1, f1 = v1.at[:, 8:40], f1.at[:, 8:40]
    op1 = tuple(ref.at[:, 8:40] for ref in op1)
    for i in range(5, 19):
        v1[i] = v1[i] + es[i, 8:40]
    sweep(v1, f1, op1, 5, 19, True)
    sweep(v1, f1, op1, 6, 18, True)
    rows = flat(v1[6:18, 4:28, :])
    e = [dot(rows, doubler_at(h)).reshape(12, 1, 24, 128) for h in (0, 1)]
    e = jnp.concatenate(e, 1).reshape(24, 24, 128)
    es[:, pl.ds(0, 24, stride=2), :] = e
    es[:, pl.ds(1, 24, stride=2), :] = e


def turn_kernel(ng, nb, *refs):
    got, f0, wx0, ws0, wl0, di0, f1, wx1, ws1, wl1, di1, f2, wx2, ws2, wl2, di2 = refs[:16]
    v0i, v1i, v2i = refs[16:19]
    v0, packed = refs[19:21]
    v1, v2, s = refs[21:24]
    scr = refs[24:]
    v1[...] = v1i[...]
    v2[...] = v2i[...]
    op0, op1, op2 = (wx0, ws0, wl0, di0), (wx1, ws1, wl1, di1), (wx2, ws2, wl2, di2)
    climb(ng, nb, None, got, v0, f0, op0, v1, f1, op1, v2, f2, op2, scr)
    add_double(v0, scr[-1], 0, 48)
    for lo in (2, 3, 4, 5):
        sweep(v0, f0, op0, lo, 48 - lo)
    packed[...] = fine_restrict(v0, f0, op0, s)


def end_kernel(ng, nb, *refs):
    got, got_c = refs[:2]
    f0, wx0, ws0, wl0, di0, f1, wx1, ws1, wl1, di1, f2, wx2, ws2, wl2, di2 = refs[2:17]
    v0i, v1i, v2i = refs[17:20]
    sol, res = refs[20:22]
    v0, v1, v2 = refs[22:25]
    scr = refs[25:]
    v0[...] = v0i[...]
    v1[...] = v1i[...]
    v2[...] = v2i[...]
    op0, op1, op2 = (wx0, ws0, wl0, di0), (wx1, ws1, wl1, di1), (wx2, ws2, wl2, di2)
    climb(ng, nb, got, got_c, v0, f0, op0, v1, f1, op1, v2, f2, op2, scr)
    add_double(v0, scr[-1], 4, 44)
    sweep(v0, f0, op0, 6, 42)
    sweep(v0, f0, op0, 7, 41)

    def step(x, n, _):
        rs = resid_slabs(v0, f0, op0, x + 8, n)
        for i in range(n):
            res[x + i] = rs[i][8:40]
        return 0

    sol[...] = v0[8:40, 8:40]
    blocks(0, 32, 8, step)


def ring(x, axis, n):
    before = lax.ppermute(x[0], axis, [(i, (i + 1) % n) for i in range(n)])
    after = lax.ppermute(x[1], axis, [(i, (i - 1) % n) for i in range(n)])
    return before, after


def tall_of(packed, nb):
    above, below = ring((packed, packed), "box", nb)
    return above, below, jnp.concatenate([above, packed, below], 1)


def around(packed, ng, nb):
    above, below, tall = tall_of(packed, nb)
    left, right = ring((tall, tall), "grp", ng)
    return packed, left, right, above, below


def gather_all(payload):
    got = lax.all_to_all(payload, ("grp", "box"), 0, 0, tiled=True)
    return got.reshape(got.shape[0] * got.shape[1], got.shape[2])


def make_body(ng, nb):
    big, mid, low = (48, 48, 128), (24, 48, 128), (24, 24, 128)
    n3, nl = 4 * ng, 4 * nb
    nd = ng * nb
    pay, pay2 = (nd, 4, 128), (nd, 2, 128)
    lev3 = (n3 + 8, 16, nl)
    climb_scratch = [lev3] * 7 + [(n3 // 2, 16, nl), (12, 32, nl), (24, 48, 128)]

    def fix(kernel):
        return lambda *refs: kernel(ng, nb, *refs)

    def body(f, tags, table, rough):
        coef, to_next, to_prev, cpack = call(
            coef_kernel, (f, tags, table, rough),
            [(32, 32, 128), (84, 8, 128), (84, 8, 128), (8, 16, 128)],
            scratch=[
                pltpu.VMEM((32, 32, 128), jnp.int32), pltpu.SMEM((8,), F32), (32, 32, 128),
                (16, 32, 128), pltpu.SemaphoreType.DMA((5,)),
            ],
            hbm=(0, 1, 2, 3),
        )
        above, below = ring((to_next, to_prev), "box", nb)
        to_next, to_prev = call(
            slabs_kernel, (f, coef, cpack, above, below), [(26, 48, 128)] * 2
        )
        left, right = ring((to_next, to_prev), "grp", ng)
        v0, f0, wx0, ws0, wl0, di0, packed = call(
            fix(start_kernel), (f, coef, left, right, above, below), [big] * 6 + [(8, 16, 128)],
            scratch=[(50, 48, 128), (2, 56, 128), (16, 48, 128)], touched=20_000_000,
        )
        l0 = (f0, wx0, ws0, wl0, di0)
        *ops, coarser = call(
            fix(mid_weights_kernel), (cpack, left, right, above, below), [mid] * 4 + [low] * 4 + [(4, 128)],
            scratch=[mid, low, mid],
        )
        f1, v1, f2, v2, payload = call(
            mid_kernel, around(packed, ng, nb) + tuple(ops) + (coarser,),
            [mid, mid, low, low, pay], scratch=[(24, 48, 128)], leave=(4,),
        )
        got_c = gather_all(payload)
        l1, l2 = (f1, *ops[:4]), (f2, *ops[4:])
        v0, packed = call(
            fix(turn_kernel), (got_c,) + l0 + l1 + l2 + (v0, v1, v2), [big, (8, 16, 128)],
            aliases={16: 0}, scratch=[mid, low, (16, 48, 128)] + climb_scratch,
        )
        f1, v1, f2, v2, payload = call(
            mid2_kernel, around(packed, ng, nb) + l1[1:] + l2[1:],
            [mid, mid, low, low, pay2], scratch=[(24, 48, 128)], leave=(4,),
        )
        got = gather_all(payload)
        l1, l2 = (f1,) + l1[1:], (f2,) + l2[1:]
        return tuple(call(
            fix(end_kernel), (got, got_c) + l0 + l1 + l2 + (v0, v1, v2), [(32, 32, 128)] * 2,
            scratch=[big, mid, low] + climb_scratch, leave=(0, 1),
        ))

    return body


def solution(mesh):
    body = make_body(mesh.shape["grp"], mesh.shape["box"])
    return jax.shard_map(
        body,
        mesh=mesh,
        in_specs=(P("grp", "box", None), P("grp", "box", None), P(), P("grp", "box", None)),
        out_specs=(P("grp", "box", None), P("grp", "box", None)),
        check_vma=False,
    )
```

```python
import jax
import jax.numpy as jnp
from jax import lax
from jax.experimental import pallas as pl
from jax.experimental.pallas import tpu as pltpu
from jax.sharding import PartitionSpec as P

F32 = jnp.float32
NB = 4
INTERPRET = False


def params():
    return pltpu.CompilerParams(vmem_limit_bytes=24 << 20)


def call(kernel, ins, outs, scratch=(), leave=(), aliases=None, hbm=(), touched=0):
    def shape_of(i, s):
        if INTERPRET or i in leave:
            return jax.ShapeDtypeStruct(s, F32)
        return pltpu.VMEM(s, F32)

    def place(i, x):
        if INTERPRET:
            return x
        return pltpu.with_memory_space_constraint(x, pltpu.HBM if i in hbm else pltpu.VMEM)

    specs = [
        pl.BlockSpec(memory_space=pl.ANY if i in hbm else pltpu.VMEM) for i in range(len(ins))
    ]
    return pl.pallas_call(
        kernel,
        out_shape=[shape_of(i, s) for i, s in enumerate(outs)],
        in_specs=specs,
        out_specs=[pl.BlockSpec(memory_space=pltpu.VMEM) for _ in outs],
        scratch_shapes=[pltpu.VMEM(s, F32) if isinstance(s, tuple) else s for s in scratch],
        compiler_params=params(),
        input_output_aliases=aliases or {},
        interpret=INTERPRET,
        cost_estimate=pl.CostEstimate(
            flops=3 * touched, bytes_accessed=touched, transcendentals=0
        )
        if touched
        else None,
    )(*[place(i, x) for i, x in enumerate(ins)])


def iota(shape, dim):
    return lax.broadcasted_iota(jnp.int32, shape, dim)


def halver(n):
    k, j = iota((n, n), 0), iota((n, n), 1)
    return jnp.where((k >> 1) == j, F32(0.5), F32(0.0))


def doubler(n):
    j, k = iota((n, n), 0), iota((n, n), 1)
    return jnp.where((k >> 1) == j, F32(1.0), F32(0.0))


def halver_at(h):
    k, j = iota((128, 128), 0), iota((128, 128), 1)
    return jnp.where((k >> 1) + 64 * h == j, F32(0.5), F32(0.0))


def doubler_at(h):
    j, k = iota((128, 128), 0), iota((128, 128), 1)
    return jnp.where((k >> 1) + 64 * h == j, F32(1.0), F32(0.0))


def folder():
    k, j = iota((128, 128), 0), iota((128, 128), 1)
    return jnp.where(((k & 63) >> 1) == j, F32(0.5), F32(0.0))


def spreader():
    j, k = iota((128, 128), 0), iota((128, 128), 1)
    return jnp.where(((k & 63) >> 1) == j, F32(1.0), F32(0.0))


def dot(a, b):
    return lax.dot_general(
        a, b, (((1,), (0,)), ((), ())), precision=lax.Precision.HIGHEST, preferred_element_type=F32
    )


def up(v, axis):
    return pltpu.roll(v, v.shape[axis] - 1, axis)


def down(v, axis):
    return pltpu.roll(v, 1, axis)


def two_next(here, after):
    low = iota(here.shape, 1) < 64
    return pltpu.roll(jnp.where(low, after, here), 64, 1)


def two_prev(here, before):
    low = iota(here.shape, 1) < 64
    return pltpu.roll(jnp.where(low, here, before), 64, 1)


def near_sum(vc, vn, carry, wxx, wss, wll):
    t = wxx * vn + carry
    t = t + (wss * up(vc, 0) + down(wss * vc, 0))
    return t + (wll * up(vc, 1) + down(wll * vc, 1))


def blocks(lo, hi, size, fn, state=0):
    count = (hi - lo) // size
    if count > 1:
        state = lax.fori_loop(0, count, lambda i, st: fn(lo + i * size, size, st), state)
    elif count == 1:
        state = fn(lo, size, state)
    rest = (hi - lo) - count * size
    if rest:
        state = fn(hi - rest, rest, state)
    return state


def block_of(ref):
    return max(1, 384 // ref.shape[1])


def sweep(v, f, op, lo, hi, two=False):
    wx, ws, wl, di = op

    def step(x, n, state):
        carry, vc = state
        vs = [vc] + [v[x + i + 1] for i in range(n)]
        new = []
        for i in range(n):
            wxx = wx[x + i]
            after, before = vs[i + 1], carry
            carry = wxx * vs[i]
            if two:
                after, before = two_next(vs[i], after), two_prev(carry, before)
            t = near_sum(vs[i], after, before, wxx, ws[x + i], wl[x + i])
            new.append(F32(0.2) * vs[i] + di[x + i] * (f[x + i] + t))
        for i in range(n):
            v[x + i] = new[i]
        return carry, vs[n]

    blocks(lo, hi, block_of(v), step, (wx[lo - 1] * v[lo - 1], v[lo]))


def first_sweep(v, f, op, lo, hi):
    di = op[3]

    def step(x, n, _):
        new = [di[x + i] * f[x + i] for i in range(n)]
        for i in range(n):
            v[x + i] = new[i]
        return 0

    blocks(lo, hi, block_of(v), step)


def resid_slabs(v, f, op, x, n, two=False):
    wx, ws, wl, di = op
    vs = [v[x + i - 1] for i in range(n + 2)]
    wxs = [wx[x + i - 1] for i in range(n + 1)]
    out = []
    for i in range(n):
        vc = vs[i + 1]
        after, before = vs[i + 2], wxs[i] * vs[i]
        if two:
            after, before = two_next(vc, after), two_prev(wxs[i + 1] * vc, before)
        t = near_sum(vc, after, before, wxs[i + 1], ws[x + i], wl[x + i])
        dinv = di[x + i]
        inside = dinv > 0
        diag = jnp.where(inside, F32(0.8) / jnp.where(inside, dinv, F32(1.0)), F32(0.0))
        out.append(f[x + i] - (diag * vc - t))
    return out


def resid_pairs(v, f, op, lo, n, out):
    def step(j, m, _):
        rs = resid_slabs(v, f, op, lo + 2 * j, 2 * m)
        for i in range(m):
            out[j + i] = rs[2 * i] + rs[2 * i + 1]
        return 0

    blocks(0, n, max(1, block_of(v) // 2), step)


def resid_each(v, f, op, lo, n, out):
    def step(j, m, _):
        rs = resid_slabs(v, f, op, lo + j, m, True)
        for i in range(m):
            out[j + i] = rs[i]
        return 0

    blocks(0, n, block_of(v), step)


def sum_pairs(src, lo, n, out):
    def step(j, m, _):
        new = [src[lo + 2 * (j + i)] + src[lo + 2 * (j + i) + 1] for i in range(m)]
        for i in range(m):
            out[j + i] = new[i]
        return 0

    blocks(0, n, max(1, block_of(out) // 2), step)


def weights(c, cbase, op, lo, hi, lane_last, sub_last, edge=None, two=False):
    wx, ws, wl, di = op
    ny, nl = c.shape[1:]
    half, zero = F32(0.5), F32(0.0)

    def step(x, n, _):
        x = x + cbase
        rows, lanes = iota((ny, nl), 0), iota((ny, nl), 1)
        last, first = lanes >= lane_last, lanes == 0
        if two:
            last, first = (lanes & 63) == 63, (lanes & 63) == 0
        hs = [c[x + i - 1] * half for i in range(n + 2)]
        new = []
        for i in range(n):
            ch = hs[i + 1]
            after, before = hs[i + 2], hs[i]
            if two:
                after, before = two_next(ch, after), two_prev(ch, before)
            cp, cm = ch + after, ch + before
            s_next, s_prev = up(ch, 0), down(ch, 0)
            if sub_last:
                s_next = jnp.where(rows == ny - 1, zero, s_next)
                s_prev = jnp.where(rows == 0, zero, s_prev)
            if edge is not None:
                s_next = jnp.where(rows == ny - 1, edge[1, pl.ds(x + i, 1), :] * half, s_next)
                s_prev = jnp.where(rows == 0, edge[0, pl.ds(x + i, 1), :] * half, s_prev)
            l_next = jnp.where(last, zero, up(ch, 1))
            l_prev = jnp.where(first, zero, down(ch, 1))
            s_up, l_up = ch + s_next, ch + l_next
            diag = (cp + cm) + (s_up + (ch + s_prev)) + (l_up + (ch + l_prev))
            inside = ch > 0
            dinv = jnp.where(inside, F32(0.8) / jnp.where(inside, diag, F32(1.0)), zero)
            s_up = jnp.where(rows == ny - 1, zero, s_up) if sub_last else s_up
            new.append((cp, s_up, jnp.where(last, zero, l_up), dinv))
        for i in range(n):
            for ref, value in zip(op, new[i]):
                ref[x - cbase + i] = value
        return 0

    blocks(lo, hi, max(1, block_of(c) // 2), step)


def pair_rows(s, start, n):
    return s[:, pl.ds(start, n, stride=2), :] + s[:, pl.ds(start + 1, n, stride=2), :]


def flat(a):
    return a.reshape(a.shape[0] * a.shape[1], a.shape[2])


def add_double(v, es, lo, hi, base=0):
    def step(x, n, _):
        new = [v[x + i] + es[((x - base) >> 1) + (i >> 1)] for i in range(n)]
        for i in range(n):
            v[x + i] = new[i]
        return 0

    blocks(lo, hi, max(2, block_of(v) & ~1), step)


def coef_kernel(
    f_hbm, tags_hbm, table_hbm, rough_hbm, coef, to_next, to_prev, x_next, x_prev, packed,
    tags, table, rough, s, sems,
):
    pairs = (
        (table_hbm, table),
        (tags_hbm, tags),
        (rough_hbm, rough),
        (f_hbm.at[:, 24:32], to_next.at[0:32]),
        (f_hbm.at[:, 0:8], to_prev.at[0:32]),
        (f_hbm.at[24:32], x_next.at[0:8]),
        (f_hbm.at[0:8], x_prev.at[0:8]),
    )
    copies = [pltpu.make_async_copy(a, b, sems.at[i]) for i, (a, b) in enumerate(pairs)]
    for copy in copies:
        copy.start()
    for copy in copies[:3]:
        copy.wait()

    def step(x, n, _):
        new = []
        for i in range(n):
            tag = tags[x + i]
            picked = jnp.zeros(tag.shape, F32)
            for region in range(8):
                picked = jnp.where(tag == region, table[region], picked)
            new.append(picked * rough[x + i])
        for i in range(n):
            coef[x + i] = new[i]
        return 0

    blocks(0, 32, 8, step)
    sum_pairs(coef, 0, 16, s)
    c1 = to_level1(pair_rows(s, 0, 16) * F32(0.25))
    packed[...] = c1
    for out, row, extra in ((to_next, 24, 23), (to_prev, 0, 8)):
        out[32:64] = coef[:, row : row + 8]
        for x in range(32):
            out[64 + x // 8, x % 8 : x % 8 + 1, :] = coef[x, extra : extra + 1, :]
        out[68:84] = c1.reshape(16, 8, 128)
    for out, first in ((x_next, 23), (x_prev, 0)):
        out[8:17] = coef[first : first + 9]
        out[17:21] = c1.reshape(4, 32, 128)
    for copy in copies[3:]:
        copy.wait()


def corners_kernel(above, below, to_next, to_prev):
    for out, fs, cs in (
        (to_next, slice(24, 32), slice(23, 32)),
        (to_prev, slice(0, 8), slice(0, 9)),
    ):
        for i, src in enumerate((above, below)):
            rows = slice(8 * i, 8 * i + 8)
            out[0:8, rows] = src[fs]
            out[8:17, rows] = src[32 + cs.start : 32 + cs.stop]
            out[17 + i] = jnp.zeros((16, 128), F32)
            out[17 + i, 0:9] = flat(src[64:68])[cs]
            out[19 + 8 * i : 27 + 8 * i] = src[68:84].reshape(8, 16, 128)


def to_level1(pairs):
    halves = pairs.reshape(8, 2, 16, 128)
    even, odd = halves[:, 0].reshape(128, 128), halves[:, 1].reshape(128, 128)
    return (dot(even, halver_at(0)) + dot(odd, halver_at(1))).reshape(8, 16, 128)


def assemble(dst, own, left, right, above, below):
    for i in range(8):
        dst[i] = left[i]
        dst[8 + i] = jnp.concatenate([above[i], own[i], below[i]], 0)
        dst[16 + i] = right[i]


def edge_flags(ng, nb):
    g, b = lax.axis_index("grp"), lax.axis_index("box")
    one, zero = F32(1.0), F32(0.0)
    return (
        jnp.where(g > 0, one, zero),
        jnp.where(g < ng - 1, one, zero),
        jnp.where(b > 0, one, zero),
        jnp.where(b < nb - 1, one, zero),
    )


def fine_restrict(v, f, op, s):
    resid_pairs(v, f, op, 8, 16, s)
    return to_level1(pair_rows(s, 8, 16))


def start_kernel(
    ng, nb, f, coef, left, right, above, below, cleft, cright, v, fx, wx, ws, wl, di, packed, cx, edge, s
):
    gl, gr, bl, br = edge_flags(ng, nb)
    fx[8:40, 8:40] = f[...]
    fx[8:40, 0:8] = above[0:32]
    fx[8:40, 40:48] = below[0:32]
    cx[9:41, 8:40] = coef[...]
    cx[9:41, 0:8] = above[32:64] * bl
    cx[9:41, 40:48] = below[32:64] * br
    for x, side, corner, flag in ((0, left, cleft, gl), (40, right, cright, gr)):
        fx[x : x + 8, 8:40] = side[0:8]
        fx[x : x + 8, 0:8] = corner[0:8, 0:8]
        fx[x : x + 8, 40:48] = corner[0:8, 8:16]
        x = 41 if x else 0
        cx[x : x + 9, 8:40] = side[8:17] * flag
        cx[x : x + 9, 0:8] = corner[8:17, 0:8] * (flag * bl)
        cx[x : x + 9, 40:48] = corner[8:17, 8:16] * (flag * br)
        edge[0, x : x + 9] = corner[17, 0:9] * (flag * bl)
        edge[1, x : x + 9] = corner[18, 0:9] * (flag * br)
    edge[0, 9:41] = flat(above[64:68]) * bl
    edge[1, 9:41] = flat(below[64:68]) * br
    op = (wx, ws, wl, di)
    weights(cx, 1, op, 0, 48, 127, False, edge)
    first_sweep(v, fx, op, 0, 48)
    sweep(v, fx, op, 1, 47)
    packed[...] = fine_restrict(v, fx, op, s)


def fold_rows(send):
    lanes = iota((2, 128), 1)
    even = jnp.concatenate([send[0:1], send[2:3]], 0)
    odd = jnp.concatenate([send[1:2], send[3:4]], 0)
    return jnp.where(lanes < 64, even, pltpu.roll(odd, 64, 1))


def mid_down(f1, v1, op1, f2, v2, op2, s, payload, extra):
    v1[0] = v1[23] = jnp.zeros((48, 128), F32)
    first_sweep(v1, f1, op1, 1, 23)
    sweep(v1, f1, op1, 1, 23, True)
    resid_each(v1, f1, op1, 2, 20, s)
    half = halver(128)
    f2[2:22] = dot(flat(pair_rows(s.at[0:20], 0, 24)), folder()).reshape(20, 24, 128)
    first_sweep(v2, f2, op2, 2, 22)
    sweep(v2, f2, op2, 3, 21)
    resid_pairs(v2, f2, op2, 8, 4, s.at[0:4, 0:24])
    send = collect(s, half, 0, F32(1.0))
    send = fold_rows(send) if extra is None else send + extra
    payload[...] = jnp.broadcast_to(send[None], payload.shape)


def collect(s, half, lane, scale):
    total = jnp.zeros((12, 128), F32)
    lanes = iota((12, 128), 1)
    for x in range(4):
        pairs = flat(pair_rows(s.at[x : x + 1], 0, 12))
        cut = jnp.where(lanes < 16, dot(pairs * scale, half), F32(0.0))
        shift = lane + 16 * x
        total = total + (pltpu.roll(cut, shift, 1) if shift else cut)
    return total[4:8]


def mid_weights_kernel(
    ng, nb, packed, left, right, above, below, cleft, cright,
    wx1, ws1, wl1, di1, wx2, ws2, wl2, di2, coarser, c1, c2, s,
):
    gl, gr, bl, br = edge_flags(ng, nb)
    rows = iota((48, 128), 0)
    scale = jnp.where(rows < 16, bl, jnp.where(rows < 32, F32(1.0), br))
    for i in range(8):
        parts = [above[68 + 2 * i], above[69 + 2 * i], packed[i]]
        parts += [below[68 + 2 * i], below[69 + 2 * i]]
        c1[8 + i] = jnp.concatenate(parts, 0) * scale
        own = slice(16 * (i % 2), 16 * (i % 2) + 16)
        for at, side, corner, flag in ((0, left, cleft, gl), (16, right, cright, gr)):
            parts = [corner[19 + i], side[17 + i // 2, own], corner[27 + i]]
            c1[at + i] = jnp.concatenate(parts, 0) * (scale * flag)
    wx1[0] = jnp.zeros((48, 128), F32)
    weights(c1, 0, (wx1, ws1, wl1, di1), 1, 23, 127, False, None, True)
    half = halver(128)
    c2[...] = dot(flat(pair_rows(c1, 0, 24) * F32(0.25)), folder()).reshape(24, 24, 128)
    weights(c2, 0, (wx2, ws2, wl2, di2), 1, 23, 31, False)
    for x in range(4):
        s[x, 0:24] = c2[8 + 2 * x] + c2[9 + 2 * x]
    send = collect(s, half, 64, F32(0.25))
    coarser[...] = send


def mid_kernel(
    own, left, right, above, below, wx1, ws1, wl1, di1, wx2, ws2, wl2, di2, coarser,
    f1, v1, f2, v2, payload, s,
):
    assemble(f1, own, left, right, above, below)
    op1, op2 = (wx1, ws1, wl1, di1), (wx2, ws2, wl2, di2)
    mid_down(f1, v1, op1, f2, v2, op2, s, payload, coarser[...])


def mid2_kernel(
    own, left, right, above, below, wx1, ws1, wl1, di1, wx2, ws2, wl2, di2,
    f1, v1, f2, v2, payload, s,
):
    assemble(f1, own, left, right, above, below)
    op1, op2 = (wx1, ws1, wl1, di1), (wx2, ws2, wl2, di2)
    mid_down(f1, v1, op1, f2, v2, op2, s, payload, None)


def apply3(p, wx, ws, wl, diag):
    zero = jnp.zeros_like(p[:1])
    q = wx * jnp.concatenate([p[1:], zero], 0)
    q = q + jnp.concatenate([zero, (wx * p)[:-1]], 0)
    q = q + (ws * up(p, 1) + down(ws * p, 1))
    q = q + (wl * up(p, 2) + down(wl * p, 2))
    return diag * p - q


def bottom(f4, c4, ny4):
    nx, nz, nl = c4.shape
    ch = c4 * F32(0.5)
    zero = jnp.zeros_like(ch[:1])
    rows, lanes, slabs = iota(c4.shape, 1), iota(c4.shape, 2), iota(c4.shape, 0)
    o = F32(0.0)
    x_up = ch + jnp.concatenate([ch[1:], zero], 0)
    x_dn = ch + jnp.concatenate([zero, ch[:-1]], 0)
    s_up = ch + jnp.where(rows == nz - 1, o, up(ch, 1))
    s_dn = ch + jnp.where(rows == 0, o, down(ch, 1))
    l_up = ch + jnp.where(lanes >= ny4 - 1, o, up(ch, 2))
    l_dn = ch + jnp.where(lanes == 0, o, down(ch, 2))
    diag = x_up + x_dn + s_up + s_dn + l_up + l_dn
    wx = jnp.where(slabs == nx - 1, o, x_up)
    ws = jnp.where(rows == nz - 1, o, s_up)
    wl = jnp.where(lanes >= ny4 - 1, o, l_up)

    def total(a):
        for axis in range(3):
            a = jnp.sum(a, axis=axis, keepdims=True)
        return a

    v = None
    r = p = f4
    rr = total(r * r)
    for i in range(NB):
        q = apply3(p, wx, ws, wl, diag)
        alpha = rr / total(p * q)
        v = alpha * p if v is None else v + alpha * p
        if i < NB - 1:
            r = r - alpha * q
            new = total(r * r)
            p = r + (new / rr) * p
            rr = new
    return v


def coarse(ng, nb, got, got_c, v3, f3, op3, c3, s3):
    n3, nl = 4 * ng, 4 * nb
    for g in range(ng):
        slabs = slice(4 + 4 * g, 8 + 4 * g)
        t = got_c[g * nl : (g + 1) * nl, :].T
        c3[slabs] = t[64:128].reshape(4, 16, nl)
        if got is None:
            f3[slabs] = t[0:64].reshape(4, 16, nl)
    if got is not None:
        k, y = iota((nl // 2, nl), 0), iota((nl // 2, nl), 1)
        even = jnp.where(y == 2 * k, F32(1.0), F32(0.0))
        odd = jnp.where(y == 2 * k + 1, F32(1.0), F32(0.0))
        ts = [got[g * (nl // 2) : (g + 1) * (nl // 2), :].T for g in range(ng)]
        lhs0 = jnp.concatenate([t[0:64] for t in ts], 0)
        lhs1 = jnp.concatenate([t[64:128] for t in ts], 0)
        f3[4 : 4 + n3] = (dot(lhs0, even) + dot(lhs1, odd)).reshape(n3, 16, nl)
    pad = jnp.zeros((4, 16, nl), F32)
    for ref in (v3, c3, op3[0]):
        ref[0:4] = pad
        ref[4 + n3 : 8 + n3] = pad
    weights(c3, 0, op3, 4, 4 + n3, nl - 1, True)
    lo, hi = 4, 4 + n3
    first_sweep(v3, f3, op3, lo, hi)
    sweep(v3, f3, op3, lo, hi)
    half = halver(nl)

    sum_pairs(c3, 4, n3 // 2, s3)
    c4 = dot(flat(pair_rows(s3, 0, 8) * F32(0.25)), half).reshape(n3 // 2, 8, nl)
    resid_pairs(v3, f3, op3, 4, n3 // 2, s3)
    f4 = dot(flat(pair_rows(s3, 0, 8)), half).reshape(n3 // 2, 8, nl)
    v4 = bottom(f4, c4, nl // 2)
    e = dot(flat(v4), doubler(nl)).reshape(n3 // 2, 8, nl)
    s3[:, pl.ds(0, 8, stride=2), :] = e
    s3[:, pl.ds(1, 8, stride=2), :] = e

    add_double(v3, s3, 4, 4 + n3, 4)
    sweep(v3, f3, op3, lo, hi)
    sweep(v3, f3, op3, lo, hi)


def coarse_to_mid(nb, v3, v2, s2, nl):
    g, b = lax.axis_index("grp"), lax.axis_index("box")
    for x in range(12):
        e = v3[4 * g + x]
        s2[x : x + 1, pl.ds(0, 16, stride=2), :] = e[None]
        s2[x : x + 1, pl.ds(1, 16, stride=2), :] = e[None]
    j, y = iota((24, nl), 0), iota((24, nl), 1)
    pick = jnp.where(y == 4 * b - 4 + (j >> 1), F32(1.0), F32(0.0))
    lanes = iota((24, 128), 1)
    zero = F32(0.0)
    for q in range(3):
        block = flat(s2[4 * q : 4 * q + 4])
        e = lax.dot_general(
            pick, block, (((1,), (1,)), ((), ())),
            precision=lax.Precision.HIGHEST, preferred_element_type=F32,
        )
        for i in range(4):
            part = e if i == 0 else pltpu.roll(e, 128 - 32 * i, 1)
            part = jnp.where(lanes < 32, part, zero)
            x = 2 * (4 * q + i)
            v2[x] = v2[x] + part
            v2[x + 1] = v2[x + 1] + part


def climb(ng, nb, got, got_c, v0, f0, op0, v1, f1, op1, v2, f2, op2, scr):
    v3, f3, c3, wx3, ws3, wl3, di3, s3, s2, es = scr
    op3 = (wx3, ws3, wl3, di3)
    coarse(ng, nb, got, got_c, v3, f3, op3, c3, s3)
    coarse_to_mid(nb, v3, v2, s2, 4 * nb)
    sweep(v2, f2, op2, 4, 20)
    sweep(v2, f2, op2, 5, 19)
    e = dot(flat(v2[5:19]), spreader()).reshape(14, 24, 128)
    es[5:19, pl.ds(0, 24, stride=2), :] = e
    es[5:19, pl.ds(1, 24, stride=2), :] = e
    v1, f1 = v1.at[:, 8:40], f1.at[:, 8:40]
    op1 = tuple(ref.at[:, 8:40] for ref in op1)
    for i in range(5, 19):
        v1[i] = v1[i] + es[i, 8:40]
    sweep(v1, f1, op1, 5, 19, True)
    sweep(v1, f1, op1, 6, 18, True)
    rows = flat(v1[6:18, 4:28, :])
    e = [dot(rows, doubler_at(h)).reshape(12, 1, 24, 128) for h in (0, 1)]
    e = jnp.concatenate(e, 1).reshape(24, 24, 128)
    es[:, pl.ds(0, 24, stride=2), :] = e
    es[:, pl.ds(1, 24, stride=2), :] = e


def turn_kernel(ng, nb, *refs):
    got, f0, wx0, ws0, wl0, di0, f1, wx1, ws1, wl1, di1, f2, wx2, ws2, wl2, di2 = refs[:16]
    v0i, v1i, v2i = refs[16:19]
    v0, packed = refs[19:21]
    v1, v2, s = refs[21:24]
    scr = refs[24:]
    v1[...] = v1i[...]
    v2[...] = v2i[...]
    op0, op1, op2 = (wx0, ws0, wl0, di0), (wx1, ws1, wl1, di1), (wx2, ws2, wl2, di2)
    climb(ng, nb, None, got, v0, f0, op0, v1, f1, op1, v2, f2, op2, scr)
    add_double(v0, scr[-1], 0, 48)
    for lo in (2, 3, 4, 5):
        sweep(v0, f0, op0, lo, 48 - lo)
    packed[...] = fine_restrict(v0, f0, op0, s)


def end_kernel(ng, nb, *refs):
    got, got_c = refs[:2]
    f0, wx0, ws0, wl0, di0, f1, wx1, ws1, wl1, di1, f2, wx2, ws2, wl2, di2 = refs[2:17]
    v0i, v1i, v2i = refs[17:20]
    sol, res = refs[20:22]
    v0, v1, v2 = refs[22:25]
    scr = refs[25:]
    v0[...] = v0i[...]
    v1[...] = v1i[...]
    v2[...] = v2i[...]
    op0, op1, op2 = (wx0, ws0, wl0, di0), (wx1, ws1, wl1, di1), (wx2, ws2, wl2, di2)
    climb(ng, nb, got, got_c, v0, f0, op0, v1, f1, op1, v2, f2, op2, scr)
    add_double(v0, scr[-1], 4, 44)
    sweep(v0, f0, op0, 6, 42)
    sweep(v0, f0, op0, 7, 41)

    def step(x, n, _):
        rs = resid_slabs(v0, f0, op0, x + 8, n)
        for i in range(n):
            res[x + i] = rs[i][8:40]
        return 0

    sol[...] = v0[8:40, 8:40]
    blocks(0, 32, 8, step)


def ring(x, axis, n):
    before = lax.ppermute(x[0], axis, [(i, (i + 1) % n) for i in range(n)])
    after = lax.ppermute(x[1], axis, [(i, (i - 1) % n) for i in range(n)])
    return before, after


def tall_of(packed, nb):
    above, below = ring((packed, packed), "box", nb)
    return above, below, jnp.concatenate([above, packed, below], 1)


def around(packed, ng, nb):
    above, below, tall = tall_of(packed, nb)
    left, right = ring((tall, tall), "grp", ng)
    return packed, left, right, above, below


def gather_all(payload):
    got = lax.all_to_all(payload, ("grp", "box"), 0, 0, tiled=True)
    return got.reshape(got.shape[0] * got.shape[1], got.shape[2])


def make_body(ng, nb):
    big, mid, low = (48, 48, 128), (24, 48, 128), (24, 24, 128)
    n3, nl = 4 * ng, 4 * nb
    nd = ng * nb
    pay, pay2 = (nd, 4, 128), (nd, 2, 128)
    lev3 = (n3 + 8, 16, nl)
    climb_scratch = [lev3] * 7 + [(n3 // 2, 16, nl), (12, 32, nl), (24, 48, 128)]

    def fix(kernel):
        return lambda *refs: kernel(ng, nb, *refs)

    def body(f, tags, table, rough):
        coef, to_next, to_prev, x_next, x_prev, cpack = call(
            coef_kernel, (f, tags, table, rough),
            [(32, 32, 128)] + [(84, 8, 128)] * 2 + [(21, 32, 128)] * 2 + [(8, 16, 128)],
            scratch=[
                pltpu.VMEM((32, 32, 128), jnp.int32), pltpu.SMEM((8,), F32), (32, 32, 128),
                (16, 32, 128), pltpu.SemaphoreType.DMA((7,)),
            ],
            hbm=(0, 1, 2, 3),
        )
        above, below = ring((to_next, to_prev), "box", nb)
        left, right = ring((x_next, x_prev), "grp", ng)
        corners = call(corners_kernel, (above, below), [(35, 16, 128)] * 2)
        halo = (left, right, above, below) + ring(corners, "grp", ng)
        v0, f0, wx0, ws0, wl0, di0, packed = call(
            fix(start_kernel), (f, coef) + halo, [big] * 6 + [(8, 16, 128)],
            scratch=[(50, 48, 128), (2, 56, 128), (16, 48, 128)], touched=20_000_000,
        )
        l0 = (f0, wx0, ws0, wl0, di0)
        *ops, coarser = call(
            fix(mid_weights_kernel), (cpack,) + halo, [mid] * 4 + [low] * 4 + [(4, 128)],
            scratch=[mid, low, mid],
        )
        f1, v1, f2, v2, payload = call(
            mid_kernel, around(packed, ng, nb) + tuple(ops) + (coarser,),
            [mid, mid, low, low, pay], scratch=[(24, 48, 128)], leave=(4,),
        )
        got_c = gather_all(payload)
        l1, l2 = (f1, *ops[:4]), (f2, *ops[4:])
        v0, packed = call(
            fix(turn_kernel), (got_c,) + l0 + l1 + l2 + (v0, v1, v2), [big, (8, 16, 128)],
            aliases={16: 0}, scratch=[mid, low, (16, 48, 128)] + climb_scratch,
        )
        f1, v1, f2, v2, payload = call(
            mid2_kernel, around(packed, ng, nb) + l1[1:] + l2[1:],
            [mid, mid, low, low, pay2], scratch=[(24, 48, 128)], leave=(4,),
        )
        got = gather_all(payload)
        l1, l2 = (f1,) + l1[1:], (f2,) + l2[1:]
        return tuple(call(
            fix(end_kernel), (got, got_c) + l0 + l1 + l2 + (v0, v1, v2), [(32, 32, 128)] * 2,
            scratch=[big, mid, low] + climb_scratch, leave=(0, 1),
        ))

    return body


def solution(mesh):
    body = make_body(mesh.shape["grp"], mesh.shape["box"])
    return jax.shard_map(
        body,
        mesh=mesh,
        in_specs=(P("grp", "box", None), P("grp", "box", None), P(), P("grp", "box", None)),
        out_specs=(P("grp", "box", None), P("grp", "box", None)),
        check_vma=False,
    )
```

```python
import jax
import jax.numpy as jnp
from jax import lax
from jax.experimental import pallas as pl
from jax.experimental.pallas import tpu as pltpu
from jax.sharding import PartitionSpec as P

F32 = jnp.float32
NB = 4
INTERPRET = False


def params():
    return pltpu.CompilerParams(vmem_limit_bytes=24 << 20)


def call(kernel, ins, outs, scratch=(), leave=(), aliases=None, hbm=(), touched=0):
    def shape_of(i, s):
        if INTERPRET or i in leave:
            return jax.ShapeDtypeStruct(s, F32)
        return pltpu.VMEM(s, F32)

    def place(i, x):
        if INTERPRET:
            return x
        return pltpu.with_memory_space_constraint(x, pltpu.HBM if i in hbm else pltpu.VMEM)

    specs = [
        pl.BlockSpec(memory_space=pl.ANY if i in hbm else pltpu.VMEM) for i in range(len(ins))
    ]
    return pl.pallas_call(
        kernel,
        out_shape=[shape_of(i, s) for i, s in enumerate(outs)],
        in_specs=specs,
        out_specs=[pl.BlockSpec(memory_space=pltpu.VMEM) for _ in outs],
        scratch_shapes=[pltpu.VMEM(s, F32) if isinstance(s, tuple) else s for s in scratch],
        compiler_params=params(),
        input_output_aliases=aliases or {},
        interpret=INTERPRET,
        cost_estimate=pl.CostEstimate(
            flops=3 * touched, bytes_accessed=touched, transcendentals=0
        )
        if touched
        else None,
    )(*[place(i, x) for i, x in enumerate(ins)])


def iota(shape, dim):
    return lax.broadcasted_iota(jnp.int32, shape, dim)


def halver(n):
    k, j = iota((n, n), 0), iota((n, n), 1)
    return jnp.where((k >> 1) == j, F32(0.5), F32(0.0))


def doubler(n):
    j, k = iota((n, n), 0), iota((n, n), 1)
    return jnp.where((k >> 1) == j, F32(1.0), F32(0.0))


def halver_at(h):
    k, j = iota((128, 128), 0), iota((128, 128), 1)
    return jnp.where((k >> 1) + 64 * h == j, F32(0.5), F32(0.0))


def doubler_at(h):
    j, k = iota((128, 128), 0), iota((128, 128), 1)
    return jnp.where((k >> 1) + 64 * h == j, F32(1.0), F32(0.0))


def folder():
    k, j = iota((128, 128), 0), iota((128, 128), 1)
    return jnp.where(((k & 63) >> 1) == j, F32(0.5), F32(0.0))


def spreader():
    j, k = iota((128, 128), 0), iota((128, 128), 1)
    return jnp.where(((k & 63) >> 1) == j, F32(1.0), F32(0.0))


def dot(a, b):
    return lax.dot_general(
        a, b, (((1,), (0,)), ((), ())), precision=lax.Precision.HIGHEST, preferred_element_type=F32
    )


def up(v, axis):
    return pltpu.roll(v, v.shape[axis] - 1, axis)


def down(v, axis):
    return pltpu.roll(v, 1, axis)


def two_next(here, after):
    low = iota(here.shape, 1) < 64
    return pltpu.roll(jnp.where(low, after, here), 64, 1)


def two_prev(here, before):
    low = iota(here.shape, 1) < 64
    return pltpu.roll(jnp.where(low, here, before), 64, 1)


def near_sum(vc, vn, carry, wxx, wss, wll):
    t = wxx * vn + carry
    t = t + (wss * up(vc, 0) + down(wss * vc, 0))
    return t + (wll * up(vc, 1) + down(wll * vc, 1))


def blocks(lo, hi, size, fn, state=0):
    count = (hi - lo) // size
    if count > 1:
        state = lax.fori_loop(0, count, lambda i, st: fn(lo + i * size, size, st), state)
    elif count == 1:
        state = fn(lo, size, state)
    rest = (hi - lo) - count * size
    if rest:
        state = fn(hi - rest, rest, state)
    return state


def block_of(ref):
    return max(1, 384 // ref.shape[1])


def sweep(v, f, op, lo, hi, two=False):
    wx, ws, wl, di = op

    def step(x, n, state):
        carry, vc = state
        vs = [vc] + [v[x + i + 1] for i in range(n)]
        new = []
        for i in range(n):
            wxx = wx[x + i]
            after, before = vs[i + 1], carry
            carry = wxx * vs[i]
            if two:
                after, before = two_next(vs[i], after), two_prev(carry, before)
            t = near_sum(vs[i], after, before, wxx, ws[x + i], wl[x + i])
            new.append(F32(0.2) * vs[i] + di[x + i] * (f[x + i] + t))
        for i in range(n):
            v[x + i] = new[i]
        return carry, vs[n]

    blocks(lo, hi, block_of(v), step, (wx[lo - 1] * v[lo - 1], v[lo]))


def first_sweep(v, f, op, lo, hi):
    di = op[3]

    def step(x, n, _):
        new = [di[x + i] * f[x + i] for i in range(n)]
        for i in range(n):
            v[x + i] = new[i]
        return 0

    blocks(lo, hi, block_of(v), step)


def resid_slabs(v, f, op, x, n, two=False):
    wx, ws, wl, di = op
    vs = [v[x + i - 1] for i in range(n + 2)]
    wxs = [wx[x + i - 1] for i in range(n + 1)]
    out = []
    for i in range(n):
        vc = vs[i + 1]
        after, before = vs[i + 2], wxs[i] * vs[i]
        if two:
            after, before = two_next(vc, after), two_prev(wxs[i + 1] * vc, before)
        t = near_sum(vc, after, before, wxs[i + 1], ws[x + i], wl[x + i])
        dinv = di[x + i]
        inside = dinv > 0
        diag = jnp.where(inside, F32(0.8) / jnp.where(inside, dinv, F32(1.0)), F32(0.0))
        out.append(f[x + i] - (diag * vc - t))
    return out


def resid_pairs(v, f, op, lo, n, out):
    def step(j, m, _):
        rs = resid_slabs(v, f, op, lo + 2 * j, 2 * m)
        for i in range(m):
            out[j + i] = rs[2 * i] + rs[2 * i + 1]
        return 0

    blocks(0, n, max(1, block_of(v) // 2), step)


def resid_each(v, f, op, lo, n, out):
    def step(j, m, _):
        rs = resid_slabs(v, f, op, lo + j, m, True)
        for i in range(m):
            out[j + i] = rs[i]
        return 0

    blocks(0, n, block_of(v), step)


def sum_pairs(src, lo, n, out):
    def step(j, m, _):
        new = [src[lo + 2 * (j + i)] + src[lo + 2 * (j + i) + 1] for i in range(m)]
        for i in range(m):
            out[j + i] = new[i]
        return 0

    blocks(0, n, max(1, block_of(out) // 2), step)


def weights(c, cbase, op, lo, hi, lane_last, sub_last, edge=None, two=False):
    wx, ws, wl, di = op
    ny, nl = c.shape[1:]
    half, zero = F32(0.5), F32(0.0)

    def step(x, n, _):
        x = x + cbase
        rows, lanes = iota((ny, nl), 0), iota((ny, nl), 1)
        last, first = lanes >= lane_last, lanes == 0
        if two:
            last, first = (lanes & 63) == 63, (lanes & 63) == 0
        hs = [c[x + i - 1] * half for i in range(n + 2)]
        new = []
        for i in range(n):
            ch = hs[i + 1]
            after, before = hs[i + 2], hs[i]
            if two:
                after, before = two_next(ch, after), two_prev(ch, before)
            cp, cm = ch + after, ch + before
            s_next, s_prev = up(ch, 0), down(ch, 0)
            if sub_last:
                s_next = jnp.where(rows == ny - 1, zero, s_next)
                s_prev = jnp.where(rows == 0, zero, s_prev)
            if edge is not None:
                s_next = jnp.where(rows == ny - 1, edge[1, pl.ds(x + i, 1), :] * half, s_next)
                s_prev = jnp.where(rows == 0, edge[0, pl.ds(x + i, 1), :] * half, s_prev)
            l_next = jnp.where(last, zero, up(ch, 1))
            l_prev = jnp.where(first, zero, down(ch, 1))
            s_up, l_up = ch + s_next, ch + l_next
            diag = (cp + cm) + (s_up + (ch + s_prev)) + (l_up + (ch + l_prev))
            inside = ch > 0
            dinv = jnp.where(inside, F32(0.8) / jnp.where(inside, diag, F32(1.0)), zero)
            s_up = jnp.where(rows == ny - 1, zero, s_up) if sub_last else s_up
            new.append((cp, s_up, jnp.where(last, zero, l_up), dinv))
        for i in range(n):
            for ref, value in zip(op, new[i]):
                ref[x - cbase + i] = value
        return 0

    blocks(lo, hi, max(1, block_of(c) // 2), step)


def pair_rows(s, start, n):
    return s[:, pl.ds(start, n, stride=2), :] + s[:, pl.ds(start + 1, n, stride=2), :]


def flat(a):
    return a.reshape(a.shape[0] * a.shape[1], a.shape[2])


def add_double(v, es, lo, hi, base=0):
    def step(x, n, _):
        new = [v[x + i] + es[((x - base) >> 1) + (i >> 1)] for i in range(n)]
        for i in range(n):
            v[x + i] = new[i]
        return 0

    blocks(lo, hi, max(2, block_of(v) & ~1), step)


def coef_kernel(
    f_hbm, tags_hbm, table_hbm, rough_hbm, coef, to_next, to_prev, x_next, x_prev, packed,
    tags, table, rough, s, sems,
):
    pairs = (
        (table_hbm, table),
        (tags_hbm, tags),
        (rough_hbm, rough),
        (f_hbm.at[:, 24:32], to_next.at[0:32]),
        (f_hbm.at[:, 0:8], to_prev.at[0:32]),
        (f_hbm.at[24:32], x_next.at[0:8]),
        (f_hbm.at[0:8], x_prev.at[0:8]),
    )
    copies = [pltpu.make_async_copy(a, b, sems.at[i]) for i, (a, b) in enumerate(pairs)]
    for copy in copies:
        copy.start()
    for copy in copies[:3]:
        copy.wait()

    def step(x, n, _):
        new = []
        for i in range(n):
            tag = tags[x + i]
            picked = jnp.zeros(tag.shape, F32)
            for region in range(8):
                picked = jnp.where(tag == region, table[region], picked)
            new.append(picked * rough[x + i])
        for i in range(n):
            coef[x + i] = new[i]
        return 0

    blocks(0, 32, 8, step)
    sum_pairs(coef, 0, 16, s)
    c1 = to_level1(pair_rows(s, 0, 16) * F32(0.25))
    packed[...] = c1
    for out, row, extra in ((to_next, 24, 23), (to_prev, 0, 8)):
        out[32:64] = coef[:, row : row + 8]
        for x in range(32):
            out[64 + x // 8, x % 8 : x % 8 + 1, :] = coef[x, extra : extra + 1, :]
        out[68:84] = c1.reshape(16, 8, 128)
    for out, first in ((x_next, 23), (x_prev, 0)):
        out[8:17] = coef[first : first + 9]
        out[17:21] = c1.reshape(4, 32, 128)
    for copy in copies[3:]:
        copy.wait()


def corners_kernel(above, below, to_next, to_prev):
    for out, fs, cs in (
        (to_next, slice(24, 32), slice(23, 32)),
        (to_prev, slice(0, 8), slice(0, 9)),
    ):
        for i, src in enumerate((above, below)):
            rows = slice(8 * i, 8 * i + 8)
            out[0:8, rows] = src[fs]
            out[8:17, rows] = src[32 + cs.start : 32 + cs.stop]
            out[17 + i] = jnp.zeros((16, 128), F32)
            out[17 + i, 0:9] = flat(src[64:68])[cs]
            out[19 + 8 * i : 27 + 8 * i] = src[68:84].reshape(8, 16, 128)


def to_level1(pairs):
    halves = pairs.reshape(8, 2, 16, 128)
    even, odd = halves[:, 0].reshape(128, 128), halves[:, 1].reshape(128, 128)
    return (dot(even, halver_at(0)) + dot(odd, halver_at(1))).reshape(8, 16, 128)


def assemble(dst, own, left, right, above, below):
    for i in range(8):
        dst[i] = left[i]
        dst[8 + i] = jnp.concatenate([above[i], own[i], below[i]], 0)
        dst[16 + i] = right[i]


def edge_flags(ng, nb):
    g, b = lax.axis_index("grp"), lax.axis_index("box")
    one, zero = F32(1.0), F32(0.0)
    return (
        jnp.where(g > 0, one, zero),
        jnp.where(g < ng - 1, one, zero),
        jnp.where(b > 0, one, zero),
        jnp.where(b < nb - 1, one, zero),
    )


def fine_restrict(v, f, op, s):
    resid_pairs(v, f, op, 8, 16, s)
    return to_level1(pair_rows(s, 8, 16))


def inner_kernel(ng, nb, f, coef, above, below, v, fx, wx, ws, wl, di, cx, edge):
    gl, gr, bl, br = edge_flags(ng, nb)
    fx[8:40, 8:40] = f[...]
    fx[8:40, 0:8] = above[0:32]
    fx[8:40, 40:48] = below[0:32]
    cx[9:41, 8:40] = coef[...]
    cx[9:41, 0:8] = above[32:64] * bl
    cx[9:41, 40:48] = below[32:64] * br
    edge[0, 9:41] = flat(above[64:68]) * bl
    edge[1, 9:41] = flat(below[64:68]) * br
    op = (wx, ws, wl, di)
    weights(cx, 1, op, 9, 39, 127, False, edge)
    first_sweep(v, fx, op, 9, 39)


def start_kernel(ng, nb, left, right, cleft, cright, *refs):
    v, fx, wx, ws, wl, di, cx, edge, packed, s = refs[8:]
    gl, gr, bl, br = edge_flags(ng, nb)
    for x, side, corner, flag in ((0, left, cleft, gl), (40, right, cright, gr)):
        fx[x : x + 8, 8:40] = side[0:8]
        fx[x : x + 8, 0:8] = corner[0:8, 0:8]
        fx[x : x + 8, 40:48] = corner[0:8, 8:16]
        x = 41 if x else 0
        cx[x : x + 9, 8:40] = side[8:17] * flag
        cx[x : x + 9, 0:8] = corner[8:17, 0:8] * (flag * bl)
        cx[x : x + 9, 40:48] = corner[8:17, 8:16] * (flag * br)
        edge[0, x : x + 9] = corner[17, 0:9] * (flag * bl)
        edge[1, x : x + 9] = corner[18, 0:9] * (flag * br)
    op = (wx, ws, wl, di)
    for lo, hi in ((0, 9), (39, 48)):
        weights(cx, 1, op, lo, hi, 127, False, edge)
        first_sweep(v, fx, op, lo, hi)
    sweep(v, fx, op, 1, 47)
    packed[...] = fine_restrict(v, fx, op, s)


def fold_rows(send):
    lanes = iota((2, 128), 1)
    even = jnp.concatenate([send[0:1], send[2:3]], 0)
    odd = jnp.concatenate([send[1:2], send[3:4]], 0)
    return jnp.where(lanes < 64, even, pltpu.roll(odd, 64, 1))


def mid_down(f1, v1, op1, f2, v2, op2, s, payload, extra):
    v1[0] = v1[23] = jnp.zeros((48, 128), F32)
    first_sweep(v1, f1, op1, 1, 23)
    sweep(v1, f1, op1, 1, 23, True)
    resid_each(v1, f1, op1, 2, 20, s)
    half = halver(128)
    f2[2:22] = dot(flat(pair_rows(s.at[0:20], 0, 24)), folder()).reshape(20, 24, 128)
    first_sweep(v2, f2, op2, 2, 22)
    sweep(v2, f2, op2, 3, 21)
    resid_pairs(v2, f2, op2, 8, 4, s.at[0:4, 0:24])
    send = collect(s, half, 0, F32(1.0))
    send = fold_rows(send) if extra is None else send + extra
    payload[...] = jnp.broadcast_to(send[None], payload.shape)


def collect(s, half, lane, scale):
    total = jnp.zeros((12, 128), F32)
    lanes = iota((12, 128), 1)
    for x in range(4):
        pairs = flat(pair_rows(s.at[x : x + 1], 0, 12))
        cut = jnp.where(lanes < 16, dot(pairs * scale, half), F32(0.0))
        shift = lane + 16 * x
        total = total + (pltpu.roll(cut, shift, 1) if shift else cut)
    return total[4:8]


def mid_weights_kernel(
    ng, nb, packed, left, right, above, below, cleft, cright,
    wx1, ws1, wl1, di1, wx2, ws2, wl2, di2, coarser, c1, c2, s,
):
    gl, gr, bl, br = edge_flags(ng, nb)
    rows = iota((48, 128), 0)
    scale = jnp.where(rows < 16, bl, jnp.where(rows < 32, F32(1.0), br))
    for i in range(8):
        parts = [above[68 + 2 * i], above[69 + 2 * i], packed[i]]
        parts += [below[68 + 2 * i], below[69 + 2 * i]]
        c1[8 + i] = jnp.concatenate(parts, 0) * scale
        own = slice(16 * (i % 2), 16 * (i % 2) + 16)
        for at, side, corner, flag in ((0, left, cleft, gl), (16, right, cright, gr)):
            parts = [corner[19 + i], side[17 + i // 2, own], corner[27 + i]]
            c1[at + i] = jnp.concatenate(parts, 0) * (scale * flag)
    wx1[0] = jnp.zeros((48, 128), F32)
    weights(c1, 0, (wx1, ws1, wl1, di1), 1, 23, 127, False, None, True)
    half = halver(128)
    c2[...] = dot(flat(pair_rows(c1, 0, 24) * F32(0.25)), folder()).reshape(24, 24, 128)
    weights(c2, 0, (wx2, ws2, wl2, di2), 1, 23, 31, False)
    for x in range(4):
        s[x, 0:24] = c2[8 + 2 * x] + c2[9 + 2 * x]
    send = collect(s, half, 64, F32(0.25))
    coarser[...] = send


def mid_kernel(
    own, left, right, above, below, wx1, ws1, wl1, di1, wx2, ws2, wl2, di2, coarser,
    f1, v1, f2, v2, payload, s,
):
    assemble(f1, own, left, right, above, below)
    op1, op2 = (wx1, ws1, wl1, di1), (wx2, ws2, wl2, di2)
    mid_down(f1, v1, op1, f2, v2, op2, s, payload, coarser[...])


def mid2_kernel(
    own, left, right, above, below, wx1, ws1, wl1, di1, wx2, ws2, wl2, di2,
    f1, v1, f2, v2, payload, s,
):
    assemble(f1, own, left, right, above, below)
    op1, op2 = (wx1, ws1, wl1, di1), (wx2, ws2, wl2, di2)
    mid_down(f1, v1, op1, f2, v2, op2, s, payload, None)


def apply3(p, wx, ws, wl, diag):
    zero = jnp.zeros_like(p[:1])
    q = wx * jnp.concatenate([p[1:], zero], 0)
    q = q + jnp.concatenate([zero, (wx * p)[:-1]], 0)
    q = q + (ws * up(p, 1) + down(ws * p, 1))
    q = q + (wl * up(p, 2) + down(wl * p, 2))
    return diag * p - q


def bottom(f4, c4, ny4):
    nx, nz, nl = c4.shape
    ch = c4 * F32(0.5)
    zero = jnp.zeros_like(ch[:1])
    rows, lanes, slabs = iota(c4.shape, 1), iota(c4.shape, 2), iota(c4.shape, 0)
    o = F32(0.0)
    x_up = ch + jnp.concatenate([ch[1:], zero], 0)
    x_dn = ch + jnp.concatenate([zero, ch[:-1]], 0)
    s_up = ch + jnp.where(rows == nz - 1, o, up(ch, 1))
    s_dn = ch + jnp.where(rows == 0, o, down(ch, 1))
    l_up = ch + jnp.where(lanes >= ny4 - 1, o, up(ch, 2))
    l_dn = ch + jnp.where(lanes == 0, o, down(ch, 2))
    diag = x_up + x_dn + s_up + s_dn + l_up + l_dn
    wx = jnp.where(slabs == nx - 1, o, x_up)
    ws = jnp.where(rows == nz - 1, o, s_up)
    wl = jnp.where(lanes >= ny4 - 1, o, l_up)

    def total(a):
        for axis in range(3):
            a = jnp.sum(a, axis=axis, keepdims=True)
        return a

    v = None
    r = p = f4
    rr = total(r * r)
    for i in range(NB):
        q = apply3(p, wx, ws, wl, diag)
        alpha = rr / total(p * q)
        v = alpha * p if v is None else v + alpha * p
        if i < NB - 1:
            r = r - alpha * q
            new = total(r * r)
            p = r + (new / rr) * p
            rr = new
    return v


def coarse_weights(ng, nb, got, op3, c4, c3, s3):
    n3, nl = 4 * ng, 4 * nb
    for g in range(ng):
        t = got[g * nl : (g + 1) * nl, :].T
        c3[4 + 4 * g : 8 + 4 * g] = t[64:128].reshape(4, 16, nl)
    pad = jnp.zeros((4, 16, nl), F32)
    for ref in (c3, op3[0]):
        ref[0:4] = pad
        ref[4 + n3 : 8 + n3] = pad
    weights(c3, 0, op3, 4, 4 + n3, nl - 1, True)
    sum_pairs(c3, 4, n3 // 2, s3)
    c4[...] = dot(flat(pair_rows(s3, 0, 8) * F32(0.25)), halver(nl)).reshape(n3 // 2, 8, nl)


def coarse(ng, nb, got, v3, f3, op3, c4, s3):
    n3, nl = 4 * ng, 4 * nb
    if got.shape[0] == ng * nl:
        for g in range(ng):
            t = got[g * nl : (g + 1) * nl, :].T
            f3[4 + 4 * g : 8 + 4 * g] = t[0:64].reshape(4, 16, nl)
    else:
        k, y = iota((nl // 2, nl), 0), iota((nl // 2, nl), 1)
        even = jnp.where(y == 2 * k, F32(1.0), F32(0.0))
        odd = jnp.where(y == 2 * k + 1, F32(1.0), F32(0.0))
        ts = [got[g * (nl // 2) : (g + 1) * (nl // 2), :].T for g in range(ng)]
        lhs0 = jnp.concatenate([t[0:64] for t in ts], 0)
        lhs1 = jnp.concatenate([t[64:128] for t in ts], 0)
        f3[4 : 4 + n3] = (dot(lhs0, even) + dot(lhs1, odd)).reshape(n3, 16, nl)
    pad = jnp.zeros((4, 16, nl), F32)
    v3[0:4] = pad
    v3[4 + n3 : 8 + n3] = pad
    lo, hi = 4, 4 + n3
    first_sweep(v3, f3, op3, lo, hi)
    sweep(v3, f3, op3, lo, hi)
    half = halver(nl)

    resid_pairs(v3, f3, op3, 4, n3 // 2, s3)
    f4 = dot(flat(pair_rows(s3, 0, 8)), half).reshape(n3 // 2, 8, nl)
    v4 = bottom(f4, c4[...], nl // 2)
    e = dot(flat(v4), doubler(nl)).reshape(n3 // 2, 8, nl)
    s3[:, pl.ds(0, 8, stride=2), :] = e
    s3[:, pl.ds(1, 8, stride=2), :] = e

    add_double(v3, s3, 4, 4 + n3, 4)
    sweep(v3, f3, op3, lo, hi)
    sweep(v3, f3, op3, lo, hi)


def coarse_to_mid(nb, v3, v2, s2, nl):
    g, b = lax.axis_index("grp"), lax.axis_index("box")
    for x in range(12):
        e = v3[4 * g + x]
        s2[x : x + 1, pl.ds(0, 16, stride=2), :] = e[None]
        s2[x : x + 1, pl.ds(1, 16, stride=2), :] = e[None]
    j, y = iota((24, nl), 0), iota((24, nl), 1)
    pick = jnp.where(y == 4 * b - 4 + (j >> 1), F32(1.0), F32(0.0))
    lanes = iota((24, 128), 1)
    zero = F32(0.0)
    for q in range(3):
        block = flat(s2[4 * q : 4 * q + 4])
        e = lax.dot_general(
            pick, block, (((1,), (1,)), ((), ())),
            precision=lax.Precision.HIGHEST, preferred_element_type=F32,
        )
        for i in range(4):
            part = e if i == 0 else pltpu.roll(e, 128 - 32 * i, 1)
            part = jnp.where(lanes < 32, part, zero)
            x = 2 * (4 * q + i)
            v2[x] = v2[x] + part
            v2[x + 1] = v2[x + 1] + part


def climb(ng, nb, got, op3, c4, v1, f1, op1, v2, f2, op2, scr):
    v3, f3, s3, s2, es = scr
    coarse(ng, nb, got, v3, f3, op3, c4, s3)
    coarse_to_mid(nb, v3, v2, s2, 4 * nb)
    sweep(v2, f2, op2, 4, 20)
    sweep(v2, f2, op2, 5, 19)
    e = dot(flat(v2[5:19]), spreader()).reshape(14, 24, 128)
    es[5:19, pl.ds(0, 24, stride=2), :] = e
    es[5:19, pl.ds(1, 24, stride=2), :] = e
    v1, f1 = v1.at[:, 8:40], f1.at[:, 8:40]
    op1 = tuple(ref.at[:, 8:40] for ref in op1)
    for i in range(5, 19):
        v1[i] = v1[i] + es[i, 8:40]
    sweep(v1, f1, op1, 5, 19, True)
    sweep(v1, f1, op1, 6, 18, True)
    rows = flat(v1[6:18, 4:28, :])
    e = [dot(rows, doubler_at(h)).reshape(12, 1, 24, 128) for h in (0, 1)]
    e = jnp.concatenate(e, 1).reshape(24, 24, 128)
    es[:, pl.ds(0, 24, stride=2), :] = e
    es[:, pl.ds(1, 24, stride=2), :] = e


def turn_kernel(ng, nb, *refs):
    got, f0, wx0, ws0, wl0, di0, f1, wx1, ws1, wl1, di1, f2, wx2, ws2, wl2, di2 = refs[:16]
    v0i, v1i, v2i = refs[16:19]
    v0, packed = refs[19:21]
    op3, c4 = refs[21:25], refs[25]
    v1, v2, s, c3 = refs[26:30]
    scr = refs[30:]
    coarse_weights(ng, nb, got, op3, c4, c3, scr[2])
    v1[...] = v1i[...]
    v2[...] = v2i[...]
    op0, op1, op2 = (wx0, ws0, wl0, di0), (wx1, ws1, wl1, di1), (wx2, ws2, wl2, di2)
    climb(ng, nb, got, op3, c4, v1, f1, op1, v2, f2, op2, scr)
    add_double(v0, scr[-1], 0, 48)
    for lo in (2, 3, 4, 5):
        sweep(v0, f0, op0, lo, 48 - lo)
    packed[...] = fine_restrict(v0, f0, op0, s)


def end_kernel(ng, nb, *refs):
    got, op3, c4 = refs[0], refs[1:5], refs[5]
    f0, wx0, ws0, wl0, di0, f1, wx1, ws1, wl1, di1, f2, wx2, ws2, wl2, di2 = refs[6:21]
    v0i, v1i, v2i = refs[21:24]
    sol, res = refs[24:26]
    v0, v1, v2 = refs[26:29]
    scr = refs[29:]
    v0[...] = v0i[...]
    v1[...] = v1i[...]
    v2[...] = v2i[...]
    op0, op1, op2 = (wx0, ws0, wl0, di0), (wx1, ws1, wl1, di1), (wx2, ws2, wl2, di2)
    climb(ng, nb, got, op3, c4, v1, f1, op1, v2, f2, op2, scr)
    add_double(v0, scr[-1], 4, 44)
    sweep(v0, f0, op0, 6, 42)
    sweep(v0, f0, op0, 7, 41)

    def step(x, n, _):
        rs = resid_slabs(v0, f0, op0, x + 8, n)
        for i in range(n):
            res[x + i] = rs[i][8:40]
        return 0

    sol[...] = v0[8:40, 8:40]
    blocks(0, 32, 8, step)


def ring(x, axis, n):
    before = lax.ppermute(x[0], axis, [(i, (i + 1) % n) for i in range(n)])
    after = lax.ppermute(x[1], axis, [(i, (i - 1) % n) for i in range(n)])
    return before, after


def tall_of(packed, nb):
    above, below = ring((packed, packed), "box", nb)
    return above, below, jnp.concatenate([above, packed, below], 1)


def around(packed, ng, nb):
    above, below, tall = tall_of(packed, nb)
    left, right = ring((tall, tall), "grp", ng)
    return packed, left, right, above, below


def gather_all(payload):
    got = lax.all_to_all(payload, ("grp", "box"), 0, 0, tiled=True)
    return got.reshape(got.shape[0] * got.shape[1], got.shape[2])


def make_body(ng, nb):
    big, mid, low = (48, 48, 128), (24, 48, 128), (24, 24, 128)
    n3, nl = 4 * ng, 4 * nb
    nd = ng * nb
    pay, pay2 = (nd, 4, 128), (nd, 2, 128)
    lev3 = (n3 + 8, 16, nl)
    climb_scratch = [lev3] * 2 + [(n3 // 2, 16, nl), (12, 32, nl), (24, 48, 128)]

    def fix(kernel):
        return lambda *refs: kernel(ng, nb, *refs)

    def body(f, tags, table, rough):
        coef, to_next, to_prev, x_next, x_prev, cpack = call(
            coef_kernel, (f, tags, table, rough),
            [(32, 32, 128)] + [(84, 8, 128)] * 2 + [(21, 32, 128)] * 2 + [(8, 16, 128)],
            scratch=[
                pltpu.VMEM((32, 32, 128), jnp.int32), pltpu.SMEM((8,), F32), (32, 32, 128),
                (16, 32, 128), pltpu.SemaphoreType.DMA((7,)),
            ],
            hbm=(0, 1, 2, 3),
        )
        above, below = ring((to_next, to_prev), "box", nb)
        left, right = ring((x_next, x_prev), "grp", ng)
        corners = call(corners_kernel, (above, below), [(35, 16, 128)] * 2)
        halo = (left, right, above, below) + ring(corners, "grp", ng)
        inner = call(
            fix(inner_kernel), (f, coef, above, below), [big] * 6 + [(50, 48, 128), (2, 56, 128)],
        )
        v0, f0, wx0, ws0, wl0, di0, _, _, packed = call(
            fix(start_kernel), halo[:2] + halo[4:] + tuple(inner),
            [big] * 6 + [(50, 48, 128), (2, 56, 128), (8, 16, 128)],
            scratch=[(16, 48, 128)], aliases={4 + i: i for i in range(8)},
        )
        l0 = (f0, wx0, ws0, wl0, di0)
        *ops, coarser = call(
            fix(mid_weights_kernel), (cpack,) + halo, [mid] * 4 + [low] * 4 + [(4, 128)],
            scratch=[mid, low, mid],
        )
        f1, v1, f2, v2, payload = call(
            mid_kernel, around(packed, ng, nb) + tuple(ops) + (coarser,),
            [mid, mid, low, low, pay], scratch=[(24, 48, 128)], leave=(4,),
        )
        got_c = gather_all(payload)
        l1, l2 = (f1, *ops[:4]), (f2, *ops[4:])
        v0, packed, *level3 = call(
            fix(turn_kernel), (got_c,) + l0 + l1 + l2 + (v0, v1, v2),
            [big, (8, 16, 128)] + [lev3] * 4 + [(n3 // 2, 8, nl)],
            aliases={16: 0}, scratch=[mid, low, (16, 48, 128), lev3] + climb_scratch,
        )
        f1, v1, f2, v2, payload = call(
            mid2_kernel, around(packed, ng, nb) + l1[1:] + l2[1:],
            [mid, mid, low, low, pay2], scratch=[(24, 48, 128)], leave=(4,),
        )
        got = gather_all(payload)
        l1, l2 = (f1,) + l1[1:], (f2,) + l2[1:]
        return tuple(call(
            fix(end_kernel), (got, *level3) + l0 + l1 + l2 + (v0, v1, v2), [(32, 32, 128)] * 2,
            scratch=[big, mid, low] + climb_scratch, leave=(0, 1),
        ))

    return body


def solution(mesh):
    body = make_body(mesh.shape["grp"], mesh.shape["box"])
    return jax.shard_map(
        body,
        mesh=mesh,
        in_specs=(P("grp", "box", None), P("grp", "box", None), P(), P("grp", "box", None)),
        out_specs=(P("grp", "box", None), P("grp", "box", None)),
        check_vma=False,
    )
```

```python
import jax
import jax.numpy as jnp
from jax import lax
from jax.experimental import pallas as pl
from jax.experimental.pallas import tpu as pltpu
from jax.sharding import PartitionSpec as P

F32 = jnp.float32
NB = 4
INTERPRET = False


def params():
    return pltpu.CompilerParams(vmem_limit_bytes=24 << 20)


def call(kernel, ins, outs, scratch=(), leave=(), aliases=None, hbm=(), touched=0):
    def shape_of(i, s):
        if INTERPRET or i in leave:
            return jax.ShapeDtypeStruct(s, F32)
        return pltpu.VMEM(s, F32)

    def place(i, x):
        if INTERPRET:
            return x
        return pltpu.with_memory_space_constraint(x, pltpu.HBM if i in hbm else pltpu.VMEM)

    specs = [
        pl.BlockSpec(memory_space=pl.ANY if i in hbm else pltpu.VMEM) for i in range(len(ins))
    ]
    return pl.pallas_call(
        kernel,
        out_shape=[shape_of(i, s) for i, s in enumerate(outs)],
        in_specs=specs,
        out_specs=[pl.BlockSpec(memory_space=pltpu.VMEM) for _ in outs],
        scratch_shapes=[pltpu.VMEM(s, F32) if isinstance(s, tuple) else s for s in scratch],
        compiler_params=params(),
        input_output_aliases=aliases or {},
        interpret=INTERPRET,
        cost_estimate=pl.CostEstimate(
            flops=3 * touched, bytes_accessed=touched, transcendentals=0
        )
        if touched
        else None,
    )(*[place(i, x) for i, x in enumerate(ins)])


def iota(shape, dim):
    return lax.broadcasted_iota(jnp.int32, shape, dim)


def halver(n):
    k, j = iota((n, n), 0), iota((n, n), 1)
    return jnp.where((k >> 1) == j, F32(0.5), F32(0.0))


def doubler(n):
    j, k = iota((n, n), 0), iota((n, n), 1)
    return jnp.where((k >> 1) == j, F32(1.0), F32(0.0))


def halver_at(h):
    k, j = iota((128, 128), 0), iota((128, 128), 1)
    return jnp.where((k >> 1) + 64 * h == j, F32(0.5), F32(0.0))


def doubler_at(h):
    j, k = iota((128, 128), 0), iota((128, 128), 1)
    return jnp.where((k >> 1) + 64 * h == j, F32(1.0), F32(0.0))


def folder():
    k, j = iota((128, 128), 0), iota((128, 128), 1)
    return jnp.where(((k & 63) >> 1) == j, F32(0.5), F32(0.0))


def spreader():
    j, k = iota((128, 128), 0), iota((128, 128), 1)
    return jnp.where(((k & 63) >> 1) == j, F32(1.0), F32(0.0))


def dot(a, b):
    return lax.dot_general(
        a, b, (((1,), (0,)), ((), ())), precision=lax.Precision.HIGHEST, preferred_element_type=F32
    )


def up(v, axis):
    return pltpu.roll(v, v.shape[axis] - 1, axis)


def down(v, axis):
    return pltpu.roll(v, 1, axis)


def two_next(here, after):
    low = iota(here.shape, 1) < 64
    return pltpu.roll(jnp.where(low, after, here), 64, 1)


def two_prev(here, before):
    low = iota(here.shape, 1) < 64
    return pltpu.roll(jnp.where(low, here, before), 64, 1)


def near_sum(vc, vn, carry, wxx, wss, wll):
    t = wxx * vn + carry
    t = t + (wss * up(vc, 0) + down(wss * vc, 0))
    return t + (wll * up(vc, 1) + down(wll * vc, 1))


def blocks(lo, hi, size, fn, state=0):
    count = (hi - lo) // size
    if count > 1:
        state = lax.fori_loop(0, count, lambda i, st: fn(lo + i * size, size, st), state)
    elif count == 1:
        state = fn(lo, size, state)
    rest = (hi - lo) - count * size
    if rest:
        state = fn(hi - rest, rest, state)
    return state


def block_of(ref):
    return max(1, 384 // ref.shape[1])


def sweep(v, f, op, lo, hi, two=False):
    wx, ws, wl, di = op

    def step(x, n, state):
        carry, vc = state
        vs = [vc] + [v[x + i + 1] for i in range(n)]
        new = []
        for i in range(n):
            wxx = wx[x + i]
            after, before = vs[i + 1], carry
            carry = wxx * vs[i]
            if two:
                after, before = two_next(vs[i], after), two_prev(carry, before)
            t = near_sum(vs[i], after, before, wxx, ws[x + i], wl[x + i])
            new.append(F32(0.2) * vs[i] + di[x + i] * (f[x + i] + t))
        for i in range(n):
            v[x + i] = new[i]
        return carry, vs[n]

    blocks(lo, hi, block_of(v), step, (wx[lo - 1] * v[lo - 1], v[lo]))


def first_sweep(v, f, op, lo, hi):
    di = op[3]

    def step(x, n, _):
        new = [di[x + i] * f[x + i] for i in range(n)]
        for i in range(n):
            v[x + i] = new[i]
        return 0

    blocks(lo, hi, block_of(v), step)


def resid_slabs(v, f, op, x, n, two=False):
    wx, ws, wl, di = op
    vs = [v[x + i - 1] for i in range(n + 2)]
    wxs = [wx[x + i - 1] for i in range(n + 1)]
    out = []
    for i in range(n):
        vc = vs[i + 1]
        after, before = vs[i + 2], wxs[i] * vs[i]
        if two:
            after, before = two_next(vc, after), two_prev(wxs[i + 1] * vc, before)
        t = near_sum(vc, after, before, wxs[i + 1], ws[x + i], wl[x + i])
        dinv = di[x + i]
        inside = dinv > 0
        diag = jnp.where(inside, F32(0.8) / jnp.where(inside, dinv, F32(1.0)), F32(0.0))
        out.append(f[x + i] - (diag * vc - t))
    return out


def resid_pairs(v, f, op, lo, n, out):
    def step(j, m, _):
        rs = resid_slabs(v, f, op, lo + 2 * j, 2 * m)
        for i in range(m):
            out[j + i] = rs[2 * i] + rs[2 * i + 1]
        return 0

    blocks(0, n, max(1, block_of(v) // 2), step)


def resid_each(v, f, op, lo, n, out):
    def step(j, m, _):
        rs = resid_slabs(v, f, op, lo + j, m, True)
        for i in range(m):
            out[j + i] = rs[i]
        return 0

    blocks(0, n, block_of(v), step)


def sum_pairs(src, lo, n, out):
    def step(j, m, _):
        new = [src[lo + 2 * (j + i)] + src[lo + 2 * (j + i) + 1] for i in range(m)]
        for i in range(m):
            out[j + i] = new[i]
        return 0

    blocks(0, n, max(1, block_of(out) // 2), step)


def weights(c, cbase, op, lo, hi, lane_last, sub_last, edge=None, two=False):
    wx, ws, wl, di = op
    ny, nl = c.shape[1:]
    half, zero = F32(0.5), F32(0.0)

    def step(x, n, _):
        x = x + cbase
        rows, lanes = iota((ny, nl), 0), iota((ny, nl), 1)
        last, first = lanes >= lane_last, lanes == 0
        if two:
            last, first = (lanes & 63) == 63, (lanes & 63) == 0
        hs = [c[x + i - 1] * half for i in range(n + 2)]
        new = []
        for i in range(n):
            ch = hs[i + 1]
            after, before = hs[i + 2], hs[i]
            if two:
                after, before = two_next(ch, after), two_prev(ch, before)
            cp, cm = ch + after, ch + before
            s_next, s_prev = up(ch, 0), down(ch, 0)
            if sub_last:
                s_next = jnp.where(rows == ny - 1, zero, s_next)
                s_prev = jnp.where(rows == 0, zero, s_prev)
            if edge is not None:
                s_next = jnp.where(rows == ny - 1, edge[1, pl.ds(x + i, 1), :] * half, s_next)
                s_prev = jnp.where(rows == 0, edge[0, pl.ds(x + i, 1), :] * half, s_prev)
            l_next = jnp.where(last, zero, up(ch, 1))
            l_prev = jnp.where(first, zero, down(ch, 1))
            s_up, l_up = ch + s_next, ch + l_next
            diag = (cp + cm) + (s_up + (ch + s_prev)) + (l_up + (ch + l_prev))
            inside = ch > 0
            dinv = jnp.where(inside, F32(0.8) / jnp.where(inside, diag, F32(1.0)), zero)
            s_up = jnp.where(rows == ny - 1, zero, s_up) if sub_last else s_up
            new.append((cp, s_up, jnp.where(last, zero, l_up), dinv))
        for i in range(n):
            for ref, value in zip(op, new[i]):
                ref[x - cbase + i] = value
        return 0

    blocks(lo, hi, max(1, block_of(c) // 2), step)


def pair_rows(s, start, n):
    return s[:, pl.ds(start, n, stride=2), :] + s[:, pl.ds(start + 1, n, stride=2), :]


def flat(a):
    return a.reshape(a.shape[0] * a.shape[1], a.shape[2])


def add_double(v, es, lo, hi, base=0):
    def step(x, n, _):
        new = [v[x + i] + es[((x - base) >> 1) + (i >> 1)] for i in range(n)]
        for i in range(n):
            v[x + i] = new[i]
        return 0

    blocks(lo, hi, max(2, block_of(v) & ~1), step)


def coef_kernel(
    f_hbm, tags_hbm, table_hbm, rough_hbm, coef, to_next, to_prev, x_next, x_prev, packed,
    tags, table, rough, s, sems,
):
    pairs = (
        (table_hbm, table),
        (tags_hbm, tags),
        (rough_hbm, rough),
        (f_hbm.at[:, 24:32], to_next.at[0:32]),
        (f_hbm.at[:, 0:8], to_prev.at[0:32]),
        (f_hbm.at[24:32], x_next.at[0:8]),
        (f_hbm.at[0:8], x_prev.at[0:8]),
    )
    copies = [pltpu.make_async_copy(a, b, sems.at[i]) for i, (a, b) in enumerate(pairs)]
    for copy in copies:
        copy.start()
    for copy in copies[:3]:
        copy.wait()

    def step(x, n, _):
        new = []
        for i in range(n):
            tag = tags[x + i]
            picked = jnp.zeros(tag.shape, F32)
            for region in range(8):
                picked = jnp.where(tag == region, table[region], picked)
            new.append(picked * rough[x + i])
        for i in range(n):
            coef[x + i] = new[i]
        return 0

    blocks(0, 32, 8, step)
    sum_pairs(coef, 0, 16, s)
    c1 = to_level1(pair_rows(s, 0, 16) * F32(0.25))
    packed[...] = c1
    for out, row, extra in ((to_next, 24, 23), (to_prev, 0, 8)):
        out[32:64] = coef[:, row : row + 8]
        for x in range(32):
            out[64 + x // 8, x % 8 : x % 8 + 1, :] = coef[x, extra : extra + 1, :]
        out[68:84] = c1.reshape(16, 8, 128)
    for out, first in ((x_next, 23), (x_prev, 0)):
        out[8:17] = coef[first : first + 9]
        out[17:21] = c1.reshape(4, 32, 128)
    for copy in copies[3:]:
        copy.wait()


def corners_kernel(above, below, to_next, to_prev):
    for out, fs, cs in (
        (to_next, slice(24, 32), slice(23, 32)),
        (to_prev, slice(0, 8), slice(0, 9)),
    ):
        for i, src in enumerate((above, below)):
            rows = slice(8 * i, 8 * i + 8)
            out[0:8, rows] = src[fs]
            out[8:17, rows] = src[32 + cs.start : 32 + cs.stop]
            out[17 + i] = jnp.zeros((16, 128), F32)
            out[17 + i, 0:9] = flat(src[64:68])[cs]
            out[19 + 8 * i : 27 + 8 * i] = src[68:84].reshape(8, 16, 128)


def to_level1(pairs):
    halves = pairs.reshape(8, 2, 16, 128)
    even, odd = halves[:, 0].reshape(128, 128), halves[:, 1].reshape(128, 128)
    return (dot(even, halver_at(0)) + dot(odd, halver_at(1))).reshape(8, 16, 128)


def assemble(dst, own, left, right, above, below):
    for i in range(8):
        dst[i] = left[i]
        dst[8 + i] = jnp.concatenate([above[i], own[i], below[i]], 0)
        dst[16 + i] = right[i]


def edge_flags(ng, nb):
    g, b = lax.axis_index("grp"), lax.axis_index("box")
    one, zero = F32(1.0), F32(0.0)
    return (
        jnp.where(g > 0, one, zero),
        jnp.where(g < ng - 1, one, zero),
        jnp.where(b > 0, one, zero),
        jnp.where(b < nb - 1, one, zero),
    )


def fine_restrict(v, f, op, s):
    resid_pairs(v, f, op, 8, 16, s)
    return to_level1(pair_rows(s, 8, 16))


def inner_kernel(ng, nb, f, coef, above, below, v, fx, wx, ws, wl, di, cx, edge):
    gl, gr, bl, br = edge_flags(ng, nb)
    fx[8:40, 8:40] = f[...]
    fx[8:40, 0:8] = above[0:32]
    fx[8:40, 40:48] = below[0:32]
    cx[9:41, 8:40] = coef[...]
    cx[9:41, 0:8] = above[32:64] * bl
    cx[9:41, 40:48] = below[32:64] * br
    edge[0, 9:41] = flat(above[64:68]) * bl
    edge[1, 9:41] = flat(below[64:68]) * br
    op = (wx, ws, wl, di)
    weights(cx, 1, op, 9, 39, 127, False, edge)
    first_sweep(v, fx, op, 9, 39)


def start_kernel(ng, nb, left, right, cleft, cright, *refs):
    v, fx, wx, ws, wl, di, cx, edge, packed, s = refs[8:]
    gl, gr, bl, br = edge_flags(ng, nb)
    for x, side, corner, flag in ((0, left, cleft, gl), (40, right, cright, gr)):
        fx[x : x + 8, 8:40] = side[0:8]
        fx[x : x + 8, 0:8] = corner[0:8, 0:8]
        fx[x : x + 8, 40:48] = corner[0:8, 8:16]
        x = 41 if x else 0
        cx[x : x + 9, 8:40] = side[8:17] * flag
        cx[x : x + 9, 0:8] = corner[8:17, 0:8] * (flag * bl)
        cx[x : x + 9, 40:48] = corner[8:17, 8:16] * (flag * br)
        edge[0, x : x + 9] = corner[17, 0:9] * (flag * bl)
        edge[1, x : x + 9] = corner[18, 0:9] * (flag * br)
    op = (wx, ws, wl, di)
    for lo, hi in ((0, 9), (39, 48)):
        weights(cx, 1, op, lo, hi, 127, False, edge)
        first_sweep(v, fx, op, lo, hi)
    sweep(v, fx, op, 1, 47)
    packed[...] = fine_restrict(v, fx, op, s)


def fold_rows(send):
    lanes = iota((2, 128), 1)
    even = jnp.concatenate([send[0:1], send[2:3]], 0)
    odd = jnp.concatenate([send[1:2], send[3:4]], 0)
    return jnp.where(lanes < 64, even, pltpu.roll(odd, 64, 1))


def mid_down(f1, v1, op1, f2, v2, op2, s, payload, extra):
    v1[0] = v1[23] = jnp.zeros((48, 128), F32)
    first_sweep(v1, f1, op1, 1, 23)
    sweep(v1, f1, op1, 1, 23, True)
    resid_each(v1, f1, op1, 2, 20, s)
    half = halver(128)
    f2[2:22] = dot(flat(pair_rows(s.at[0:20], 0, 24)), folder()).reshape(20, 24, 128)
    first_sweep(v2, f2, op2, 2, 22)
    sweep(v2, f2, op2, 3, 21)
    resid_pairs(v2, f2, op2, 8, 4, s.at[0:4, 0:24])
    send = collect(s, half, 0, F32(1.0))
    send = fold_rows(send) if extra is None else send + extra
    payload[...] = jnp.broadcast_to(send[None], payload.shape)


def collect(s, half, lane, scale):
    total = jnp.zeros((12, 128), F32)
    lanes = iota((12, 128), 1)
    for x in range(4):
        pairs = flat(pair_rows(s.at[x : x + 1], 0, 12))
        cut = jnp.where(lanes < 16, dot(pairs * scale, half), F32(0.0))
        shift = lane + 16 * x
        total = total + (pltpu.roll(cut, shift, 1) if shift else cut)
    return total[4:8]


def mid_weights_kernel(
    ng, nb, packed, left, right, above, below, cleft, cright,
    wx1, ws1, wl1, di1, wx2, ws2, wl2, di2, coarser, c1, c2, s,
):
    gl, gr, bl, br = edge_flags(ng, nb)
    rows = iota((48, 128), 0)
    scale = jnp.where(rows < 16, bl, jnp.where(rows < 32, F32(1.0), br))
    for i in range(8):
        parts = [above[68 + 2 * i], above[69 + 2 * i], packed[i]]
        parts += [below[68 + 2 * i], below[69 + 2 * i]]
        c1[8 + i] = jnp.concatenate(parts, 0) * scale
        own = slice(16 * (i % 2), 16 * (i % 2) + 16)
        for at, side, corner, flag in ((0, left, cleft, gl), (16, right, cright, gr)):
            parts = [corner[19 + i], side[17 + i // 2, own], corner[27 + i]]
            c1[at + i] = jnp.concatenate(parts, 0) * (scale * flag)
    wx1[0] = jnp.zeros((48, 128), F32)
    weights(c1, 0, (wx1, ws1, wl1, di1), 1, 23, 127, False, None, True)
    half = halver(128)
    c2[...] = dot(flat(pair_rows(c1, 0, 24) * F32(0.25)), folder()).reshape(24, 24, 128)
    weights(c2, 0, (wx2, ws2, wl2, di2), 1, 23, 31, False)
    for x in range(4):
        s[x, 0:24] = c2[8 + 2 * x] + c2[9 + 2 * x]
    send = collect(s, half, 64, F32(0.25))
    coarser[...] = send


def mid_kernel(
    own, right, left, above, below, wx1, ws1, wl1, di1, wx2, ws2, wl2, di2, coarser,
    f1, v1, f2, v2, payload, s,
):
    assemble(f1, own, left, right, above, below)
    op1, op2 = (wx1, ws1, wl1, di1), (wx2, ws2, wl2, di2)
    mid_down(f1, v1, op1, f2, v2, op2, s, payload, coarser[...])


def mid2_kernel(
    own, right, left, above, below, wx1, ws1, wl1, di1, wx2, ws2, wl2, di2,
    f1, v1, f2, v2, payload, s,
):
    assemble(f1, own, left, right, above, below)
    op1, op2 = (wx1, ws1, wl1, di1), (wx2, ws2, wl2, di2)
    mid_down(f1, v1, op1, f2, v2, op2, s, payload, None)


def apply3(p, wx, ws, wl, diag):
    zero = jnp.zeros_like(p[:1])
    q = wx * jnp.concatenate([p[1:], zero], 0)
    q = q + jnp.concatenate([zero, (wx * p)[:-1]], 0)
    q = q + (ws * up(p, 1) + down(ws * p, 1))
    q = q + (wl * up(p, 2) + down(wl * p, 2))
    return diag * p - q


def bottom(f4, c4, ny4):
    nx, nz, nl = c4.shape
    ch = c4 * F32(0.5)
    zero = jnp.zeros_like(ch[:1])
    rows, lanes, slabs = iota(c4.shape, 1), iota(c4.shape, 2), iota(c4.shape, 0)
    o = F32(0.0)
    x_up = ch + jnp.concatenate([ch[1:], zero], 0)
    x_dn = ch + jnp.concatenate([zero, ch[:-1]], 0)
    s_up = ch + jnp.where(rows == nz - 1, o, up(ch, 1))
    s_dn = ch + jnp.where(rows == 0, o, down(ch, 1))
    l_up = ch + jnp.where(lanes >= ny4 - 1, o, up(ch, 2))
    l_dn = ch + jnp.where(lanes == 0, o, down(ch, 2))
    diag = x_up + x_dn + s_up + s_dn + l_up + l_dn
    wx = jnp.where(slabs == nx - 1, o, x_up)
    ws = jnp.where(rows == nz - 1, o, s_up)
    wl = jnp.where(lanes >= ny4 - 1, o, l_up)

    def total(a):
        for axis in range(3):
            a = jnp.sum(a, axis=axis, keepdims=True)
        return a

    v = None
    r = p = f4
    rr = total(r * r)
    for i in range(NB):
        q = apply3(p, wx, ws, wl, diag)
        alpha = rr / total(p * q)
        v = alpha * p if v is None else v + alpha * p
        if i < NB - 1:
            r = r - alpha * q
            new = total(r * r)
            p = r + (new / rr) * p
            rr = new
    return v


def coarse_weights(ng, nb, got, op3, c4, c3, s3):
    n3, nl = 4 * ng, 4 * nb
    for g in range(ng):
        t = got[g * nl : (g + 1) * nl, :].T
        c3[4 + 4 * g : 8 + 4 * g] = t[64:128].reshape(4, 16, nl)
    pad = jnp.zeros((4, 16, nl), F32)
    for ref in (c3, op3[0]):
        ref[0:4] = pad
        ref[4 + n3 : 8 + n3] = pad
    weights(c3, 0, op3, 4, 4 + n3, nl - 1, True)
    sum_pairs(c3, 4, n3 // 2, s3)
    c4[...] = dot(flat(pair_rows(s3, 0, 8) * F32(0.25)), halver(nl)).reshape(n3 // 2, 8, nl)


def coarse(ng, nb, got, v3, f3, op3, c4, s3):
    n3, nl = 4 * ng, 4 * nb
    if got.shape[0] == ng * nl:
        for g in range(ng):
            t = got[g * nl : (g + 1) * nl, :].T
            f3[4 + 4 * g : 8 + 4 * g] = t[0:64].reshape(4, 16, nl)
    else:
        k, y = iota((nl // 2, nl), 0), iota((nl // 2, nl), 1)
        even = jnp.where(y == 2 * k, F32(1.0), F32(0.0))
        odd = jnp.where(y == 2 * k + 1, F32(1.0), F32(0.0))
        ts = [got[g * (nl // 2) : (g + 1) * (nl // 2), :].T for g in range(ng)]
        lhs0 = jnp.concatenate([t[0:64] for t in ts], 0)
        lhs1 = jnp.concatenate([t[64:128] for t in ts], 0)
        f3[4 : 4 + n3] = (dot(lhs0, even) + dot(lhs1, odd)).reshape(n3, 16, nl)
    pad = jnp.zeros((4, 16, nl), F32)
    v3[0:4] = pad
    v3[4 + n3 : 8 + n3] = pad
    lo, hi = 4, 4 + n3
    first_sweep(v3, f3, op3, lo, hi)
    sweep(v3, f3, op3, lo, hi)
    half = halver(nl)

    resid_pairs(v3, f3, op3, 4, n3 // 2, s3)
    f4 = dot(flat(pair_rows(s3, 0, 8)), half).reshape(n3 // 2, 8, nl)
    v4 = bottom(f4, c4[...], nl // 2)
    e = dot(flat(v4), doubler(nl)).reshape(n3 // 2, 8, nl)
    s3[:, pl.ds(0, 8, stride=2), :] = e
    s3[:, pl.ds(1, 8, stride=2), :] = e

    add_double(v3, s3, 4, 4 + n3, 4)
    sweep(v3, f3, op3, lo, hi)
    sweep(v3, f3, op3, lo, hi)


def coarse_to_mid(nb, v3, v2, s2, nl):
    g, b = lax.axis_index("grp"), lax.axis_index("box")
    for x in range(12):
        e = v3[4 * g + x]
        s2[x : x + 1, pl.ds(0, 16, stride=2), :] = e[None]
        s2[x : x + 1, pl.ds(1, 16, stride=2), :] = e[None]
    j, y = iota((24, nl), 0), iota((24, nl), 1)
    pick = jnp.where(y == 4 * b - 4 + (j >> 1), F32(1.0), F32(0.0))
    lanes = iota((24, 128), 1)
    zero = F32(0.0)
    for q in range(3):
        block = flat(s2[4 * q : 4 * q + 4])
        e = lax.dot_general(
            pick, block, (((1,), (1,)), ((), ())),
            precision=lax.Precision.HIGHEST, preferred_element_type=F32,
        )
        for i in range(4):
            part = e if i == 0 else pltpu.roll(e, 128 - 32 * i, 1)
            part = jnp.where(lanes < 32, part, zero)
            x = 2 * (4 * q + i)
            v2[x] = v2[x] + part
            v2[x + 1] = v2[x + 1] + part


def climb(ng, nb, got, op3, c4, v1, f1, op1, v2, f2, op2, scr):
    v3, f3, s3, s2, es = scr
    coarse(ng, nb, got, v3, f3, op3, c4, s3)
    coarse_to_mid(nb, v3, v2, s2, 4 * nb)
    sweep(v2, f2, op2, 4, 20)
    sweep(v2, f2, op2, 5, 19)
    e = dot(flat(v2[5:19]), spreader()).reshape(14, 24, 128)
    es[5:19, pl.ds(0, 24, stride=2), :] = e
    es[5:19, pl.ds(1, 24, stride=2), :] = e
    v1, f1 = v1.at[:, 8:40], f1.at[:, 8:40]
    op1 = tuple(ref.at[:, 8:40] for ref in op1)
    for i in range(5, 19):
        v1[i] = v1[i] + es[i, 8:40]
    sweep(v1, f1, op1, 5, 19, True)
    sweep(v1, f1, op1, 6, 18, True)
    rows = flat(v1[6:18, 4:28, :])
    e = [dot(rows, doubler_at(h)).reshape(12, 1, 24, 128) for h in (0, 1)]
    e = jnp.concatenate(e, 1).reshape(24, 24, 128)
    es[:, pl.ds(0, 24, stride=2), :] = e
    es[:, pl.ds(1, 24, stride=2), :] = e


def turn_kernel(ng, nb, *refs):
    got, f0, wx0, ws0, wl0, di0, f1, wx1, ws1, wl1, di1, f2, wx2, ws2, wl2, di2 = refs[:16]
    v0i, v1i, v2i = refs[16:19]
    v0, packed = refs[19:21]
    op3, c4 = refs[21:25], refs[25]
    v1, v2, s, c3 = refs[26:30]
    scr = refs[30:]
    coarse_weights(ng, nb, got, op3, c4, c3, scr[2])
    v1[...] = v1i[...]
    v2[...] = v2i[...]
    op0, op1, op2 = (wx0, ws0, wl0, di0), (wx1, ws1, wl1, di1), (wx2, ws2, wl2, di2)
    climb(ng, nb, got, op3, c4, v1, f1, op1, v2, f2, op2, scr)
    add_double(v0, scr[-1], 0, 48)
    for lo in (2, 3, 4, 5):
        sweep(v0, f0, op0, lo, 48 - lo)
    packed[...] = fine_restrict(v0, f0, op0, s)


def end_kernel(ng, nb, *refs):
    got, op3, c4 = refs[0], refs[1:5], refs[5]
    f0, wx0, ws0, wl0, di0, f1, wx1, ws1, wl1, di1, f2, wx2, ws2, wl2, di2 = refs[6:21]
    v0i, v1i, v2i = refs[21:24]
    sol, res = refs[24:26]
    v0, v1, v2 = refs[26:29]
    scr = refs[29:]
    v0[...] = v0i[...]
    v1[...] = v1i[...]
    v2[...] = v2i[...]
    op0, op1, op2 = (wx0, ws0, wl0, di0), (wx1, ws1, wl1, di1), (wx2, ws2, wl2, di2)
    climb(ng, nb, got, op3, c4, v1, f1, op1, v2, f2, op2, scr)
    add_double(v0, scr[-1], 4, 44)
    sweep(v0, f0, op0, 6, 42)
    sweep(v0, f0, op0, 7, 41)

    def step(x, n, _):
        rs = resid_slabs(v0, f0, op0, x + 8, n)
        for i in range(n):
            res[x + i] = rs[i][8:40]
        return 0

    sol[...] = v0[8:40, 8:40]
    blocks(0, 32, 8, step)


def ring(x, axis, n):
    before = lax.ppermute(x[0], axis, [(i, (i + 1) % n) for i in range(n)])
    after = lax.ppermute(x[1], axis, [(i, (i - 1) % n) for i in range(n)])
    return before, after


def tall_of(packed, nb):
    above, below = ring((packed, packed), "box", nb)
    return above, below, jnp.concatenate([above, packed, below], 1)


def around(packed, ng, nb):
    above, below, tall = tall_of(packed, nb)
    left, right = ring((tall, tall), "grp", ng)
    return packed, right, left, above, below


def gather_all(payload):
    got = lax.all_to_all(payload, ("grp", "box"), 0, 0, tiled=True)
    return got.reshape(got.shape[0] * got.shape[1], got.shape[2])


def make_body(ng, nb):
    big, mid, low = (48, 48, 128), (24, 48, 128), (24, 24, 128)
    n3, nl = 4 * ng, 4 * nb
    nd = ng * nb
    pay, pay2 = (nd, 4, 128), (nd, 2, 128)
    lev3 = (n3 + 8, 16, nl)
    climb_scratch = [lev3] * 2 + [(n3 // 2, 16, nl), (12, 32, nl), (24, 48, 128)]

    def fix(kernel):
        return lambda *refs: kernel(ng, nb, *refs)

    def body(f, tags, table, rough):
        coef, to_next, to_prev, x_next, x_prev, cpack = call(
            coef_kernel, (f, tags, table, rough),
            [(32, 32, 128)] + [(84, 8, 128)] * 2 + [(21, 32, 128)] * 2 + [(8, 16, 128)],
            scratch=[
                pltpu.VMEM((32, 32, 128), jnp.int32), pltpu.SMEM((8,), F32), (32, 32, 128),
                (16, 32, 128), pltpu.SemaphoreType.DMA((7,)),
            ],
            hbm=(0, 1, 2, 3),
        )
        above, below = ring((to_next, to_prev), "box", nb)
        left, right = ring((x_next, x_prev), "grp", ng)
        corners = call(corners_kernel, (above, below), [(35, 16, 128)] * 2)
        halo = (left, right, above, below) + ring(corners, "grp", ng)
        inner = call(
            fix(inner_kernel), (f, coef, above, below), [big] * 6 + [(50, 48, 128), (2, 56, 128)],
        )
        v0, f0, wx0, ws0, wl0, di0, _, _, packed = call(
            fix(start_kernel), halo[:2] + halo[4:] + tuple(inner),
            [big] * 6 + [(50, 48, 128), (2, 56, 128), (8, 16, 128)],
            scratch=[(16, 48, 128)], aliases={4 + i: i for i in range(8)},
        )
        l0 = (f0, wx0, ws0, wl0, di0)
        *ops, coarser = call(
            fix(mid_weights_kernel), (cpack,) + halo, [mid] * 4 + [low] * 4 + [(4, 128)],
            scratch=[mid, low, mid],
        )
        f1, v1, f2, v2, payload = call(
            mid_kernel, around(packed, ng, nb) + tuple(ops) + (coarser,),
            [mid, mid, low, low, pay], scratch=[(24, 48, 128)], leave=(4,),
        )
        got_c = gather_all(payload)
        l1, l2 = (f1, *ops[:4]), (f2, *ops[4:])
        v0, packed, *level3 = call(
            fix(turn_kernel), (got_c,) + l0 + l1 + l2 + (v0, v1, v2),
            [big, (8, 16, 128)] + [lev3] * 4 + [(n3 // 2, 8, nl)],
            aliases={16: 0}, scratch=[mid, low, (16, 48, 128), lev3] + climb_scratch,
        )
        f1, v1, f2, v2, payload = call(
            mid2_kernel, around(packed, ng, nb) + l1[1:] + l2[1:],
            [mid, mid, low, low, pay2], scratch=[(24, 48, 128)], leave=(4,),
        )
        got = gather_all(payload)
        l1, l2 = (f1,) + l1[1:], (f2,) + l2[1:]
        return tuple(call(
            fix(end_kernel), (got, *level3) + l0 + l1 + l2 + (v0, v1, v2), [(32, 32, 128)] * 2,
            scratch=[big, mid, low] + climb_scratch, leave=(0, 1),
        ))

    return body


def solution(mesh):
    body = make_body(mesh.shape["grp"], mesh.shape["box"])
    return jax.shard_map(
        body,
        mesh=mesh,
        in_specs=(P("grp", "box", None), P("grp", "box", None), P(), P("grp", "box", None)),
        out_specs=(P("grp", "box", None), P("grp", "box", None)),
        check_vma=False,
    )
```

```python
import jax
import jax.numpy as jnp
from jax import lax
from jax.experimental import pallas as pl
from jax.experimental.pallas import tpu as pltpu
from jax.sharding import PartitionSpec as P

F32 = jnp.float32
NB = 4
INTERPRET = False


def params():
    return pltpu.CompilerParams(vmem_limit_bytes=24 << 20)


def call(kernel, ins, outs, scratch=(), leave=(), aliases=None, hbm=(), touched=0):
    def shape_of(i, s):
        if INTERPRET or i in leave:
            return jax.ShapeDtypeStruct(s, F32)
        return pltpu.VMEM(s, F32)

    def place(i, x):
        if INTERPRET:
            return x
        return pltpu.with_memory_space_constraint(x, pltpu.HBM if i in hbm else pltpu.VMEM)

    specs = [
        pl.BlockSpec(memory_space=pl.ANY if i in hbm else pltpu.VMEM) for i in range(len(ins))
    ]
    return pl.pallas_call(
        kernel,
        out_shape=[shape_of(i, s) for i, s in enumerate(outs)],
        in_specs=specs,
        out_specs=[pl.BlockSpec(memory_space=pltpu.VMEM) for _ in outs],
        scratch_shapes=[pltpu.VMEM(s, F32) if isinstance(s, tuple) else s for s in scratch],
        compiler_params=params(),
        input_output_aliases=aliases or {},
        interpret=INTERPRET,
        cost_estimate=pl.CostEstimate(
            flops=3 * touched, bytes_accessed=touched, transcendentals=0
        )
        if touched
        else None,
    )(*[place(i, x) for i, x in enumerate(ins)])


def iota(shape, dim):
    return lax.broadcasted_iota(jnp.int32, shape, dim)


def halver(n):
    k, j = iota((n, n), 0), iota((n, n), 1)
    return jnp.where((k >> 1) == j, F32(0.5), F32(0.0))


def doubler(n):
    j, k = iota((n, n), 0), iota((n, n), 1)
    return jnp.where((k >> 1) == j, F32(1.0), F32(0.0))


def halver_at(h):
    k, j = iota((128, 128), 0), iota((128, 128), 1)
    return jnp.where((k >> 1) + 64 * h == j, F32(0.5), F32(0.0))


def doubler_at(h):
    j, k = iota((128, 128), 0), iota((128, 128), 1)
    return jnp.where((k >> 1) + 64 * h == j, F32(1.0), F32(0.0))


def folder():
    k, j = iota((128, 128), 0), iota((128, 128), 1)
    return jnp.where(((k & 63) >> 1) == j, F32(0.5), F32(0.0))


def spreader():
    j, k = iota((128, 128), 0), iota((128, 128), 1)
    return jnp.where(((k & 63) >> 1) == j, F32(1.0), F32(0.0))


def dot(a, b):
    return lax.dot_general(
        a, b, (((1,), (0,)), ((), ())), precision=lax.Precision.HIGHEST, preferred_element_type=F32
    )


def up(v, axis):
    return pltpu.roll(v, v.shape[axis] - 1, axis)


def down(v, axis):
    return pltpu.roll(v, 1, axis)


def two_next(here, after):
    low = iota(here.shape, 1) < 64
    return pltpu.roll(jnp.where(low, after, here), 64, 1)


def two_prev(here, before):
    low = iota(here.shape, 1) < 64
    return pltpu.roll(jnp.where(low, here, before), 64, 1)


def near_sum(vc, vn, carry, wxx, wss, wll):
    t = wxx * vn + carry
    t = t + (wss * up(vc, 0) + down(wss * vc, 0))
    return t + (wll * up(vc, 1) + down(wll * vc, 1))


def blocks(lo, hi, size, fn, state=0):
    count = (hi - lo) // size
    if count > 1:
        state = lax.fori_loop(0, count, lambda i, st: fn(lo + i * size, size, st), state)
    elif count == 1:
        state = fn(lo, size, state)
    rest = (hi - lo) - count * size
    if rest:
        state = fn(hi - rest, rest, state)
    return state


def block_of(ref):
    return max(1, 384 // ref.shape[1])


def sweep(v, f, op, lo, hi, two=False):
    wx, ws, wl, di = op

    def step(x, n, state):
        carry, vc = state
        vs = [vc] + [v[x + i + 1] for i in range(n)]
        new = []
        for i in range(n):
            wxx = wx[x + i]
            after, before = vs[i + 1], carry
            carry = wxx * vs[i]
            if two:
                after, before = two_next(vs[i], after), two_prev(carry, before)
            t = near_sum(vs[i], after, before, wxx, ws[x + i], wl[x + i])
            new.append(F32(0.2) * vs[i] + di[x + i] * (f[x + i] + t))
        for i in range(n):
            v[x + i] = new[i]
        return carry, vs[n]

    blocks(lo, hi, block_of(v), step, (wx[lo - 1] * v[lo - 1], v[lo]))


def first_sweep(v, f, op, lo, hi):
    di = op[3]

    def step(x, n, _):
        new = [di[x + i] * f[x + i] for i in range(n)]
        for i in range(n):
            v[x + i] = new[i]
        return 0

    blocks(lo, hi, block_of(v), step)


def resid_slabs(v, f, op, x, n, two=False):
    wx, ws, wl, di = op
    vs = [v[x + i - 1] for i in range(n + 2)]
    wxs = [wx[x + i - 1] for i in range(n + 1)]
    out = []
    for i in range(n):
        vc = vs[i + 1]
        after, before = vs[i + 2], wxs[i] * vs[i]
        if two:
            after, before = two_next(vc, after), two_prev(wxs[i + 1] * vc, before)
        t = near_sum(vc, after, before, wxs[i + 1], ws[x + i], wl[x + i])
        dinv = di[x + i]
        inside = dinv > 0
        diag = jnp.where(inside, F32(0.8) / jnp.where(inside, dinv, F32(1.0)), F32(0.0))
        out.append(f[x + i] - (diag * vc - t))
    return out


def resid_pairs(v, f, op, lo, n, out):
    def step(j, m, _):
        rs = resid_slabs(v, f, op, lo + 2 * j, 2 * m)
        for i in range(m):
            out[j + i] = rs[2 * i] + rs[2 * i + 1]
        return 0

    blocks(0, n, max(1, block_of(v) // 2), step)


def resid_each(v, f, op, lo, n, out):
    def step(j, m, _):
        rs = resid_slabs(v, f, op, lo + j, m, True)
        for i in range(m):
            out[j + i] = rs[i]
        return 0

    blocks(0, n, block_of(v), step)


def sum_pairs(src, lo, n, out):
    def step(j, m, _):
        new = [src[lo + 2 * (j + i)] + src[lo + 2 * (j + i) + 1] for i in range(m)]
        for i in range(m):
            out[j + i] = new[i]
        return 0

    blocks(0, n, max(1, block_of(out) // 2), step)


def weights(c, cbase, op, lo, hi, lane_last, sub_last, edge=None, two=False):
    wx, ws, wl, di = op
    ny, nl = c.shape[1:]
    half, zero = F32(0.5), F32(0.0)

    def step(x, n, _):
        x = x + cbase
        rows, lanes = iota((ny, nl), 0), iota((ny, nl), 1)
        last, first = lanes >= lane_last, lanes == 0
        if two:
            last, first = (lanes & 63) == 63, (lanes & 63) == 0
        hs = [c[x + i - 1] * half for i in range(n + 2)]
        new = []
        for i in range(n):
            ch = hs[i + 1]
            after, before = hs[i + 2], hs[i]
            if two:
                after, before = two_next(ch, after), two_prev(ch, before)
            cp, cm = ch + after, ch + before
            s_next, s_prev = up(ch, 0), down(ch, 0)
            if sub_last:
                s_next = jnp.where(rows == ny - 1, zero, s_next)
                s_prev = jnp.where(rows == 0, zero, s_prev)
            if edge is not None:
                s_next = jnp.where(rows == ny - 1, edge[1, pl.ds(x + i, 1), :] * half, s_next)
                s_prev = jnp.where(rows == 0, edge[0, pl.ds(x + i, 1), :] * half, s_prev)
            l_next = jnp.where(last, zero, up(ch, 1))
            l_prev = jnp.where(first, zero, down(ch, 1))
            s_up, l_up = ch + s_next, ch + l_next
            diag = (cp + cm) + (s_up + (ch + s_prev)) + (l_up + (ch + l_prev))
            inside = ch > 0
            dinv = jnp.where(inside, F32(0.8) / jnp.where(inside, diag, F32(1.0)), zero)
            s_up = jnp.where(rows == ny - 1, zero, s_up) if sub_last else s_up
            new.append((cp, s_up, jnp.where(last, zero, l_up), dinv))
        for i in range(n):
            for ref, value in zip(op, new[i]):
                ref[x - cbase + i] = value
        return 0

    blocks(lo, hi, max(1, block_of(c) // 2), step)


def pair_rows(s, start, n):
    return s[:, pl.ds(start, n, stride=2), :] + s[:, pl.ds(start + 1, n, stride=2), :]


def flat(a):
    return a.reshape(a.shape[0] * a.shape[1], a.shape[2])


def add_double(v, es, lo, hi, base=0):
    def step(x, n, _):
        new = [v[x + i] + es[((x - base) >> 1) + (i >> 1)] for i in range(n)]
        for i in range(n):
            v[x + i] = new[i]
        return 0

    blocks(lo, hi, max(2, block_of(v) & ~1), step)


def coef_kernel(
    f_hbm, tags_hbm, table_hbm, rough_hbm, coef, to_next, to_prev, x_next, x_prev, packed,
    tags, table, rough, s, sems,
):
    pairs = (
        (table_hbm, table),
        (tags_hbm, tags),
        (rough_hbm, rough),
        (f_hbm.at[:, 24:32], to_next.at[0:32]),
        (f_hbm.at[:, 0:8], to_prev.at[0:32]),
        (f_hbm.at[24:32], x_next.at[0:8]),
        (f_hbm.at[0:8], x_prev.at[0:8]),
    )
    copies = [pltpu.make_async_copy(a, b, sems.at[i]) for i, (a, b) in enumerate(pairs)]
    for copy in copies:
        copy.start()
    for copy in copies[:3]:
        copy.wait()

    def step(x, n, _):
        new = []
        for i in range(n):
            tag = tags[x + i]
            picked = jnp.zeros(tag.shape, F32)
            for region in range(8):
                picked = jnp.where(tag == region, table[region], picked)
            new.append(picked * rough[x + i])
        for i in range(n):
            coef[x + i] = new[i]
        return 0

    blocks(0, 32, 8, step)
    sum_pairs(coef, 0, 16, s)
    c1 = to_level1(pair_rows(s, 0, 16) * F32(0.25))
    packed[...] = c1
    for out, row, extra in ((to_next, 24, 23), (to_prev, 0, 8)):
        out[32:64] = coef[:, row : row + 8]
        for x in range(32):
            out[64 + x // 8, x % 8 : x % 8 + 1, :] = coef[x, extra : extra + 1, :]
        out[68:84] = c1.reshape(16, 8, 128)
    for out, first in ((x_next, 23), (x_prev, 0)):
        out[8:17] = coef[first : first + 9]
        out[17:21] = c1.reshape(4, 32, 128)
    for copy in copies[3:]:
        copy.wait()


def corners_kernel(above, below, to_next, to_prev):
    for out, fs, cs in (
        (to_next, slice(24, 32), slice(23, 32)),
        (to_prev, slice(0, 8), slice(0, 9)),
    ):
        for i, src in enumerate((above, below)):
            rows = slice(8 * i, 8 * i + 8)
            out[0:8, rows] = src[fs]
            out[8:17, rows] = src[32 + cs.start : 32 + cs.stop]
            out[17 + i] = jnp.zeros((16, 128), F32)
            out[17 + i, 0:9] = flat(src[64:68])[cs]
            out[19 + 8 * i : 27 + 8 * i] = src[68:84].reshape(8, 16, 128)


def to_level1(pairs):
    halves = pairs.reshape(8, 2, 16, 128)
    even, odd = halves[:, 0].reshape(128, 128), halves[:, 1].reshape(128, 128)
    return (dot(even, halver_at(0)) + dot(odd, halver_at(1))).reshape(8, 16, 128)


def assemble(dst, own, left, right, above, below):
    for i in range(8):
        dst[i] = left[i]
        dst[8 + i] = jnp.concatenate([above[i], own[i], below[i]], 0)
        dst[16 + i] = right[i]


def edge_flags(ng, nb):
    g, b = lax.axis_index("grp"), lax.axis_index("box")
    one, zero = F32(1.0), F32(0.0)
    return (
        jnp.where(g > 0, one, zero),
        jnp.where(g < ng - 1, one, zero),
        jnp.where(b > 0, one, zero),
        jnp.where(b < nb - 1, one, zero),
    )


def fine_restrict(v, f, op, s):
    resid_pairs(v, f, op, 8, 16, s)
    return to_level1(pair_rows(s, 8, 16))


def inner_kernel(ng, nb, f, coef, above, below, v, fx, wx, ws, wl, di, cx, edge):
    gl, gr, bl, br = edge_flags(ng, nb)
    fx[8:40, 8:40] = f[...]
    fx[8:40, 0:8] = above[0:32]
    fx[8:40, 40:48] = below[0:32]
    cx[9:41, 8:40] = coef[...]
    cx[9:41, 0:8] = above[32:64] * bl
    cx[9:41, 40:48] = below[32:64] * br
    edge[0, 9:41] = flat(above[64:68]) * bl
    edge[1, 9:41] = flat(below[64:68]) * br
    op = (wx, ws, wl, di)
    weights(cx, 1, op, 9, 39, 127, False, edge)
    first_sweep(v, fx, op, 9, 39)


def start_kernel(ng, nb, right, left, cright, cleft, *refs):
    v, fx, wx, ws, wl, di, cx, edge, packed, s = refs[8:]
    gl, gr, bl, br = edge_flags(ng, nb)
    for x, side, corner, flag in ((0, left, cleft, gl), (40, right, cright, gr)):
        fx[x : x + 8, 8:40] = side[0:8]
        fx[x : x + 8, 0:8] = corner[0:8, 0:8]
        fx[x : x + 8, 40:48] = corner[0:8, 8:16]
        x = 41 if x else 0
        cx[x : x + 9, 8:40] = side[8:17] * flag
        cx[x : x + 9, 0:8] = corner[8:17, 0:8] * (flag * bl)
        cx[x : x + 9, 40:48] = corner[8:17, 8:16] * (flag * br)
        edge[0, x : x + 9] = corner[17, 0:9] * (flag * bl)
        edge[1, x : x + 9] = corner[18, 0:9] * (flag * br)
    op = (wx, ws, wl, di)
    for lo, hi in ((0, 9), (39, 48)):
        weights(cx, 1, op, lo, hi, 127, False, edge)
        first_sweep(v, fx, op, lo, hi)
    sweep(v, fx, op, 1, 47)
    packed[...] = fine_restrict(v, fx, op, s)


def fold_rows(send):
    lanes = iota((2, 128), 1)
    even = jnp.concatenate([send[0:1], send[2:3]], 0)
    odd = jnp.concatenate([send[1:2], send[3:4]], 0)
    return jnp.where(lanes < 64, even, pltpu.roll(odd, 64, 1))


def mid_down(f1, v1, op1, f2, v2, op2, s, payload, extra):
    v1[0] = v1[23] = jnp.zeros((48, 128), F32)
    first_sweep(v1, f1, op1, 1, 23)
    sweep(v1, f1, op1, 1, 23, True)
    resid_each(v1, f1, op1, 2, 20, s)
    half = halver(128)
    f2[2:22] = dot(flat(pair_rows(s.at[0:20], 0, 24)), folder()).reshape(20, 24, 128)
    first_sweep(v2, f2, op2, 2, 22)
    sweep(v2, f2, op2, 3, 21)
    resid_pairs(v2, f2, op2, 8, 4, s.at[0:4, 0:24])
    send = collect(s, half, 0, F32(1.0))
    send = fold_rows(send) if extra is None else send + extra
    payload[...] = jnp.broadcast_to(send[None], payload.shape)


def collect(s, half, lane, scale):
    total = jnp.zeros((12, 128), F32)
    lanes = iota((12, 128), 1)
    for x in range(4):
        pairs = flat(pair_rows(s.at[x : x + 1], 0, 12))
        cut = jnp.where(lanes < 16, dot(pairs * scale, half), F32(0.0))
        shift = lane + 16 * x
        total = total + (pltpu.roll(cut, shift, 1) if shift else cut)
    return total[4:8]


def mid_weights_kernel(
    ng, nb, packed, right, left, above, below, cright, cleft,
    wx1, ws1, wl1, di1, wx2, ws2, wl2, di2, coarser, c1, c2, s,
):
    gl, gr, bl, br = edge_flags(ng, nb)
    rows = iota((48, 128), 0)
    scale = jnp.where(rows < 16, bl, jnp.where(rows < 32, F32(1.0), br))
    for i in range(8):
        parts = [above[68 + 2 * i], above[69 + 2 * i], packed[i]]
        parts += [below[68 + 2 * i], below[69 + 2 * i]]
        c1[8 + i] = jnp.concatenate(parts, 0) * scale
        own = slice(16 * (i % 2), 16 * (i % 2) + 16)
        for at, side, corner, flag in ((0, left, cleft, gl), (16, right, cright, gr)):
            parts = [corner[19 + i], side[17 + i // 2, own], corner[27 + i]]
            c1[at + i] = jnp.concatenate(parts, 0) * (scale * flag)
    wx1[0] = jnp.zeros((48, 128), F32)
    weights(c1, 0, (wx1, ws1, wl1, di1), 1, 23, 127, False, None, True)
    half = halver(128)
    c2[...] = dot(flat(pair_rows(c1, 0, 24) * F32(0.25)), folder()).reshape(24, 24, 128)
    weights(c2, 0, (wx2, ws2, wl2, di2), 1, 23, 31, False)
    for x in range(4):
        s[x, 0:24] = c2[8 + 2 * x] + c2[9 + 2 * x]
    send = collect(s, half, 64, F32(0.25))
    coarser[...] = send


def mid_kernel(
    own, right, left, above, below, wx1, ws1, wl1, di1, wx2, ws2, wl2, di2, coarser,
    f1, v1, f2, v2, payload, s,
):
    assemble(f1, own, left, right, above, below)
    op1, op2 = (wx1, ws1, wl1, di1), (wx2, ws2, wl2, di2)
    mid_down(f1, v1, op1, f2, v2, op2, s, payload, coarser[...])


def mid2_kernel(
    own, right, left, above, below, wx1, ws1, wl1, di1, wx2, ws2, wl2, di2,
    f1, v1, f2, v2, payload, s,
):
    assemble(f1, own, left, right, above, below)
    op1, op2 = (wx1, ws1, wl1, di1), (wx2, ws2, wl2, di2)
    mid_down(f1, v1, op1, f2, v2, op2, s, payload, None)


def apply3(p, wx, ws, wl, diag):
    zero = jnp.zeros_like(p[:1])
    q = wx * jnp.concatenate([p[1:], zero], 0)
    q = q + jnp.concatenate([zero, (wx * p)[:-1]], 0)
    q = q + (ws * up(p, 1) + down(ws * p, 1))
    q = q + (wl * up(p, 2) + down(wl * p, 2))
    return diag * p - q


def bottom(f4, c4, ny4):
    nx, nz, nl = c4.shape
    ch = c4 * F32(0.5)
    zero = jnp.zeros_like(ch[:1])
    rows, lanes, slabs = iota(c4.shape, 1), iota(c4.shape, 2), iota(c4.shape, 0)
    o = F32(0.0)
    x_up = ch + jnp.concatenate([ch[1:], zero], 0)
    x_dn = ch + jnp.concatenate([zero, ch[:-1]], 0)
    s_up = ch + jnp.where(rows == nz - 1, o, up(ch, 1))
    s_dn = ch + jnp.where(rows == 0, o, down(ch, 1))
    l_up = ch + jnp.where(lanes >= ny4 - 1, o, up(ch, 2))
    l_dn = ch + jnp.where(lanes == 0, o, down(ch, 2))
    diag = x_up + x_dn + s_up + s_dn + l_up + l_dn
    wx = jnp.where(slabs == nx - 1, o, x_up)
    ws = jnp.where(rows == nz - 1, o, s_up)
    wl = jnp.where(lanes >= ny4 - 1, o, l_up)

    def total(a):
        for axis in range(3):
            a = jnp.sum(a, axis=axis, keepdims=True)
        return a

    v = None
    r = p = f4
    rr = total(r * r)
    for i in range(NB):
        q = apply3(p, wx, ws, wl, diag)
        alpha = rr / total(p * q)
        v = alpha * p if v is None else v + alpha * p
        if i < NB - 1:
            r = r - alpha * q
            new = total(r * r)
            p = r + (new / rr) * p
            rr = new
    return v


def coarse_weights(ng, nb, got, op3, c4, c3, s3):
    n3, nl = 4 * ng, 4 * nb
    for g in range(ng):
        t = got[g * nl : (g + 1) * nl, :].T
        c3[4 + 4 * g : 8 + 4 * g] = t[64:128].reshape(4, 16, nl)
    pad = jnp.zeros((4, 16, nl), F32)
    for ref in (c3, op3[0]):
        ref[0:4] = pad
        ref[4 + n3 : 8 + n3] = pad
    weights(c3, 0, op3, 4, 4 + n3, nl - 1, True)
    sum_pairs(c3, 4, n3 // 2, s3)
    c4[...] = dot(flat(pair_rows(s3, 0, 8) * F32(0.25)), halver(nl)).reshape(n3 // 2, 8, nl)


def coarse(ng, nb, got, v3, f3, op3, c4, s3):
    n3, nl = 4 * ng, 4 * nb
    if got.shape[0] == ng * nl:
        for g in range(ng):
            t = got[g * nl : (g + 1) * nl, :].T
            f3[4 + 4 * g : 8 + 4 * g] = t[0:64].reshape(4, 16, nl)
    else:
        k, y = iota((nl // 2, nl), 0), iota((nl // 2, nl), 1)
        even = jnp.where(y == 2 * k, F32(1.0), F32(0.0))
        odd = jnp.where(y == 2 * k + 1, F32(1.0), F32(0.0))
        ts = [got[g * (nl // 2) : (g + 1) * (nl // 2), :].T for g in range(ng)]
        lhs0 = jnp.concatenate([t[0:64] for t in ts], 0)
        lhs1 = jnp.concatenate([t[64:128] for t in ts], 0)
        f3[4 : 4 + n3] = (dot(lhs0, even) + dot(lhs1, odd)).reshape(n3, 16, nl)
    pad = jnp.zeros((4, 16, nl), F32)
    v3[0:4] = pad
    v3[4 + n3 : 8 + n3] = pad
    lo, hi = 4, 4 + n3
    first_sweep(v3, f3, op3, lo, hi)
    sweep(v3, f3, op3, lo, hi)
    half = halver(nl)

    resid_pairs(v3, f3, op3, 4, n3 // 2, s3)
    f4 = dot(flat(pair_rows(s3, 0, 8)), half).reshape(n3 // 2, 8, nl)
    v4 = bottom(f4, c4[...], nl // 2)
    e = dot(flat(v4), doubler(nl)).reshape(n3 // 2, 8, nl)
    s3[:, pl.ds(0, 8, stride=2), :] = e
    s3[:, pl.ds(1, 8, stride=2), :] = e

    add_double(v3, s3, 4, 4 + n3, 4)
    sweep(v3, f3, op3, lo, hi)
    sweep(v3, f3, op3, lo, hi)


def coarse_to_mid(nb, v3, v2, s2, nl):
    g, b = lax.axis_index("grp"), lax.axis_index("box")
    for x in range(12):
        e = v3[4 * g + x]
        s2[x : x + 1, pl.ds(0, 16, stride=2), :] = e[None]
        s2[x : x + 1, pl.ds(1, 16, stride=2), :] = e[None]
    j, y = iota((24, nl), 0), iota((24, nl), 1)
    pick = jnp.where(y == 4 * b - 4 + (j >> 1), F32(1.0), F32(0.0))
    lanes = iota((24, 128), 1)
    zero = F32(0.0)
    for q in range(3):
        block = flat(s2[4 * q : 4 * q + 4])
        e = lax.dot_general(
            pick, block, (((1,), (1,)), ((), ())),
            precision=lax.Precision.HIGHEST, preferred_element_type=F32,
        )
        for i in range(4):
            part = e if i == 0 else pltpu.roll(e, 128 - 32 * i, 1)
            part = jnp.where(lanes < 32, part, zero)
            x = 2 * (4 * q + i)
            v2[x] = v2[x] + part
            v2[x + 1] = v2[x + 1] + part


def climb(ng, nb, got, op3, c4, v1, f1, op1, v2, f2, op2, scr):
    v3, f3, s3, s2, es = scr
    coarse(ng, nb, got, v3, f3, op3, c4, s3)
    coarse_to_mid(nb, v3, v2, s2, 4 * nb)
    sweep(v2, f2, op2, 4, 20)
    sweep(v2, f2, op2, 5, 19)
    e = dot(flat(v2[5:19]), spreader()).reshape(14, 24, 128)
    es[5:19, pl.ds(0, 24, stride=2), :] = e
    es[5:19, pl.ds(1, 24, stride=2), :] = e
    v1, f1 = v1.at[:, 8:40], f1.at[:, 8:40]
    op1 = tuple(ref.at[:, 8:40] for ref in op1)
    for i in range(5, 19):
        v1[i] = v1[i] + es[i, 8:40]
    sweep(v1, f1, op1, 5, 19, True)
    sweep(v1, f1, op1, 6, 18, True)
    rows = flat(v1[6:18, 4:28, :])
    e = [dot(rows, doubler_at(h)).reshape(12, 1, 24, 128) for h in (0, 1)]
    e = jnp.concatenate(e, 1).reshape(24, 24, 128)
    es[:, pl.ds(0, 24, stride=2), :] = e
    es[:, pl.ds(1, 24, stride=2), :] = e


def turn_kernel(ng, nb, *refs):
    got, f0, wx0, ws0, wl0, di0, f1, wx1, ws1, wl1, di1, f2, wx2, ws2, wl2, di2 = refs[:16]
    v0i, v1i, v2i = refs[16:19]
    v0, packed = refs[19:21]
    op3, c4 = refs[21:25], refs[25]
    v1, v2, s, c3 = refs[26:30]
    scr = refs[30:]
    coarse_weights(ng, nb, got, op3, c4, c3, scr[2])
    v1[...] = v1i[...]
    v2[...] = v2i[...]
    op0, op1, op2 = (wx0, ws0, wl0, di0), (wx1, ws1, wl1, di1), (wx2, ws2, wl2, di2)
    climb(ng, nb, got, op3, c4, v1, f1, op1, v2, f2, op2, scr)
    add_double(v0, scr[-1], 0, 48)
    for lo in (2, 3, 4, 5):
        sweep(v0, f0, op0, lo, 48 - lo)
    packed[...] = fine_restrict(v0, f0, op0, s)


def end_kernel(ng, nb, *refs):
    got, op3, c4 = refs[0], refs[1:5], refs[5]
    f0, wx0, ws0, wl0, di0, f1, wx1, ws1, wl1, di1, f2, wx2, ws2, wl2, di2 = refs[6:21]
    v0i, v1i, v2i = refs[21:24]
    sol, res = refs[24:26]
    v0, v1, v2 = refs[26:29]
    scr = refs[29:]
    v0[...] = v0i[...]
    v1[...] = v1i[...]
    v2[...] = v2i[...]
    op0, op1, op2 = (wx0, ws0, wl0, di0), (wx1, ws1, wl1, di1), (wx2, ws2, wl2, di2)
    climb(ng, nb, got, op3, c4, v1, f1, op1, v2, f2, op2, scr)
    add_double(v0, scr[-1], 4, 44)
    sweep(v0, f0, op0, 6, 42)
    sweep(v0, f0, op0, 7, 41)

    def step(x, n, _):
        rs = resid_slabs(v0, f0, op0, x + 8, n)
        for i in range(n):
            res[x + i] = rs[i][8:40]
        return 0

    sol[...] = v0[8:40, 8:40]
    blocks(0, 32, 8, step)


def ring(x, axis, n):
    before = lax.ppermute(x[0], axis, [(i, (i + 1) % n) for i in range(n)])
    after = lax.ppermute(x[1], axis, [(i, (i - 1) % n) for i in range(n)])
    return before, after


def tall_of(packed, nb):
    above, below = ring((packed, packed), "box", nb)
    return above, below, jnp.concatenate([above, packed, below], 1)


def around(packed, ng, nb):
    above, below, tall = tall_of(packed, nb)
    left, right = ring((tall, tall), "grp", ng)
    return packed, right, left, above, below


def gather_all(payload):
    got = lax.all_to_all(payload, ("grp", "box"), 0, 0, tiled=True)
    return got.reshape(got.shape[0] * got.shape[1], got.shape[2])


def make_body(ng, nb):
    big, mid, low = (48, 48, 128), (24, 48, 128), (24, 24, 128)
    n3, nl = 4 * ng, 4 * nb
    nd = ng * nb
    pay, pay2 = (nd, 4, 128), (nd, 2, 128)
    lev3 = (n3 + 8, 16, nl)
    climb_scratch = [lev3] * 2 + [(n3 // 2, 16, nl), (12, 32, nl), (24, 48, 128)]

    def fix(kernel):
        return lambda *refs: kernel(ng, nb, *refs)

    def body(f, tags, table, rough):
        coef, to_next, to_prev, x_next, x_prev, cpack = call(
            coef_kernel, (f, tags, table, rough),
            [(32, 32, 128)] + [(84, 8, 128)] * 2 + [(21, 32, 128)] * 2 + [(8, 16, 128)],
            scratch=[
                pltpu.VMEM((32, 32, 128), jnp.int32), pltpu.SMEM((8,), F32), (32, 32, 128),
                (16, 32, 128), pltpu.SemaphoreType.DMA((7,)),
            ],
            hbm=(0, 1, 2, 3),
        )
        above, below = ring((to_next, to_prev), "box", nb)
        left, right = ring((x_next, x_prev), "grp", ng)
        corners = call(corners_kernel, (above, below), [(35, 16, 128)] * 2)
        corner_left, corner_right = ring(corners, "grp", ng)
        halo = (right, left, above, below, corner_right, corner_left)
        inner = call(
            fix(inner_kernel), (f, coef, above, below), [big] * 6 + [(50, 48, 128), (2, 56, 128)],
        )
        v0, f0, wx0, ws0, wl0, di0, _, _, packed = call(
            fix(start_kernel), halo[:2] + halo[4:] + tuple(inner),
            [big] * 6 + [(50, 48, 128), (2, 56, 128), (8, 16, 128)],
            scratch=[(16, 48, 128)], aliases={4 + i: i for i in range(8)},
        )
        l0 = (f0, wx0, ws0, wl0, di0)
        *ops, coarser = call(
            fix(mid_weights_kernel), (cpack,) + halo, [mid] * 4 + [low] * 4 + [(4, 128)],
            scratch=[mid, low, mid],
        )
        f1, v1, f2, v2, payload = call(
            mid_kernel, around(packed, ng, nb) + tuple(ops) + (coarser,),
            [mid, mid, low, low, pay], scratch=[(24, 48, 128)], leave=(4,),
        )
        got_c = gather_all(payload)
        l1, l2 = (f1, *ops[:4]), (f2, *ops[4:])
        v0, packed, *level3 = call(
            fix(turn_kernel), (got_c,) + l0 + l1 + l2 + (v0, v1, v2),
            [big, (8, 16, 128)] + [lev3] * 4 + [(n3 // 2, 8, nl)],
            aliases={16: 0}, scratch=[mid, low, (16, 48, 128), lev3] + climb_scratch,
        )
        f1, v1, f2, v2, payload = call(
            mid2_kernel, around(packed, ng, nb) + l1[1:] + l2[1:],
            [mid, mid, low, low, pay2], scratch=[(24, 48, 128)], leave=(4,),
        )
        got = gather_all(payload)
        l1, l2 = (f1,) + l1[1:], (f2,) + l2[1:]
        return tuple(call(
            fix(end_kernel), (got, *level3) + l0 + l1 + l2 + (v0, v1, v2), [(32, 32, 128)] * 2,
            scratch=[big, mid, low] + climb_scratch, leave=(0, 1),
        ))

    return body


def solution(mesh):
    body = make_body(mesh.shape["grp"], mesh.shape["box"])
    return jax.shard_map(
        body,
        mesh=mesh,
        in_specs=(P("grp", "box", None), P("grp", "box", None), P(), P("grp", "box", None)),
        out_specs=(P("grp", "box", None), P("grp", "box", None)),
        check_vma=False,
    )
```

```python
import jax
import jax.numpy as jnp
from jax import lax
from jax.experimental import pallas as pl
from jax.experimental.pallas import tpu as pltpu
from jax.sharding import PartitionSpec as P

F32 = jnp.float32
NB = 4
INTERPRET = False


def params():
    return pltpu.CompilerParams(vmem_limit_bytes=24 << 20)


def call(kernel, ins, outs, scratch=(), leave=(), aliases=None, hbm=(), touched=0):
    def shape_of(i, s):
        if INTERPRET or i in leave:
            return jax.ShapeDtypeStruct(s, F32)
        return pltpu.VMEM(s, F32)

    def place(i, x):
        if INTERPRET:
            return x
        return pltpu.with_memory_space_constraint(x, pltpu.HBM if i in hbm else pltpu.VMEM)

    specs = [
        pl.BlockSpec(memory_space=pl.ANY if i in hbm else pltpu.VMEM) for i in range(len(ins))
    ]
    return pl.pallas_call(
        kernel,
        out_shape=[shape_of(i, s) for i, s in enumerate(outs)],
        in_specs=specs,
        out_specs=[pl.BlockSpec(memory_space=pltpu.VMEM) for _ in outs],
        scratch_shapes=[pltpu.VMEM(s, F32) if isinstance(s, tuple) else s for s in scratch],
        compiler_params=params(),
        input_output_aliases=aliases or {},
        interpret=INTERPRET,
        cost_estimate=pl.CostEstimate(
            flops=3 * touched, bytes_accessed=touched, transcendentals=0
        )
        if touched
        else None,
    )(*[place(i, x) for i, x in enumerate(ins)])


def iota(shape, dim):
    return lax.broadcasted_iota(jnp.int32, shape, dim)


def halver(n):
    k, j = iota((n, n), 0), iota((n, n), 1)
    return jnp.where((k >> 1) == j, F32(0.5), F32(0.0))


def doubler(n):
    j, k = iota((n, n), 0), iota((n, n), 1)
    return jnp.where((k >> 1) == j, F32(1.0), F32(0.0))


def halver_at(h):
    k, j = iota((128, 128), 0), iota((128, 128), 1)
    return jnp.where((k >> 1) + 64 * h == j, F32(0.5), F32(0.0))


def doubler_at(h):
    j, k = iota((128, 128), 0), iota((128, 128), 1)
    return jnp.where((k >> 1) + 64 * h == j, F32(1.0), F32(0.0))


def folder():
    k, j = iota((128, 128), 0), iota((128, 128), 1)
    return jnp.where(((k & 63) >> 1) == j, F32(0.5), F32(0.0))


def spreader():
    j, k = iota((128, 128), 0), iota((128, 128), 1)
    return jnp.where(((k & 63) >> 1) == j, F32(1.0), F32(0.0))


def dot(a, b):
    return lax.dot_general(
        a, b, (((1,), (0,)), ((), ())), precision=lax.Precision.HIGHEST, preferred_element_type=F32
    )


def up(v, axis):
    return pltpu.roll(v, v.shape[axis] - 1, axis)


def down(v, axis):
    return pltpu.roll(v, 1, axis)


def two_next(here, after):
    low = iota(here.shape, 1) < 64
    return pltpu.roll(jnp.where(low, after, here), 64, 1)


def two_prev(here, before):
    low = iota(here.shape, 1) < 64
    return pltpu.roll(jnp.where(low, here, before), 64, 1)


def near_sum(vc, vn, carry, wxx, wss, wll):
    t = wxx * vn + carry
    t = t + (wss * up(vc, 0) + down(wss * vc, 0))
    return t + (wll * up(vc, 1) + down(wll * vc, 1))


def blocks(lo, hi, size, fn, state=0):
    count = (hi - lo) // size
    if count > 1:
        state = lax.fori_loop(0, count, lambda i, st: fn(lo + i * size, size, st), state)
    elif count == 1:
        state = fn(lo, size, state)
    rest = (hi - lo) - count * size
    if rest:
        state = fn(hi - rest, rest, state)
    return state


def block_of(ref):
    return max(1, 384 // ref.shape[1])


def sweep(v, f, op, lo, hi, two=False):
    wx, ws, wl, di = op

    def step(x, n, state):
        carry, vc = state
        vs = [vc] + [v[x + i + 1] for i in range(n)]
        new = []
        for i in range(n):
            wxx = wx[x + i]
            after, before = vs[i + 1], carry
            carry = wxx * vs[i]
            if two:
                after, before = two_next(vs[i], after), two_prev(carry, before)
            t = near_sum(vs[i], after, before, wxx, ws[x + i], wl[x + i])
            new.append(F32(0.2) * vs[i] + di[x + i] * (f[x + i] + t))
        for i in range(n):
            v[x + i] = new[i]
        return carry, vs[n]

    blocks(lo, hi, block_of(v), step, (wx[lo - 1] * v[lo - 1], v[lo]))


def first_sweep(v, f, op, lo, hi):
    di = op[3]

    def step(x, n, _):
        new = [di[x + i] * f[x + i] for i in range(n)]
        for i in range(n):
            v[x + i] = new[i]
        return 0

    blocks(lo, hi, block_of(v), step)


def resid_slabs(v, f, op, x, n, two=False):
    wx, ws, wl, di = op
    vs = [v[x + i - 1] for i in range(n + 2)]
    wxs = [wx[x + i - 1] for i in range(n + 1)]
    out = []
    for i in range(n):
        vc = vs[i + 1]
        after, before = vs[i + 2], wxs[i] * vs[i]
        if two:
            after, before = two_next(vc, after), two_prev(wxs[i + 1] * vc, before)
        t = near_sum(vc, after, before, wxs[i + 1], ws[x + i], wl[x + i])
        dinv = di[x + i]
        inside = dinv > 0
        diag = jnp.where(inside, F32(0.8) / jnp.where(inside, dinv, F32(1.0)), F32(0.0))
        out.append(f[x + i] - (diag * vc - t))
    return out


def resid_pairs(v, f, op, lo, n, out):
    def step(j, m, _):
        rs = resid_slabs(v, f, op, lo + 2 * j, 2 * m)
        for i in range(m):
            out[j + i] = rs[2 * i] + rs[2 * i + 1]
        return 0

    blocks(0, n, max(1, block_of(v) // 2), step)


def resid_each(v, f, op, lo, n, out):
    def step(j, m, _):
        rs = resid_slabs(v, f, op, lo + j, m, True)
        for i in range(m):
            out[j + i] = rs[i]
        return 0

    blocks(0, n, block_of(v), step)


def sum_pairs(src, lo, n, out):
    def step(j, m, _):
        new = [src[lo + 2 * (j + i)] + src[lo + 2 * (j + i) + 1] for i in range(m)]
        for i in range(m):
            out[j + i] = new[i]
        return 0

    blocks(0, n, max(1, block_of(out) // 2), step)


def weights(c, cbase, op, lo, hi, lane_last, sub_last, edge=None, two=False):
    wx, ws, wl, di = op
    ny, nl = c.shape[1:]
    half, zero = F32(0.5), F32(0.0)

    def step(x, n, _):
        x = x + cbase
        rows, lanes = iota((ny, nl), 0), iota((ny, nl), 1)
        last, first = lanes >= lane_last, lanes == 0
        if two:
            last, first = (lanes & 63) == 63, (lanes & 63) == 0
        hs = [c[x + i - 1] * half for i in range(n + 2)]
        new = []
        for i in range(n):
            ch = hs[i + 1]
            after, before = hs[i + 2], hs[i]
            if two:
                after, before = two_next(ch, after), two_prev(ch, before)
            cp, cm = ch + after, ch + before
            s_next, s_prev = up(ch, 0), down(ch, 0)
            if sub_last:
                s_next = jnp.where(rows == ny - 1, zero, s_next)
                s_prev = jnp.where(rows == 0, zero, s_prev)
            if edge is not None:
                s_next = jnp.where(rows == ny - 1, edge[1, pl.ds(x + i, 1), :] * half, s_next)
                s_prev = jnp.where(rows == 0, edge[0, pl.ds(x + i, 1), :] * half, s_prev)
            l_next = jnp.where(last, zero, up(ch, 1))
            l_prev = jnp.where(first, zero, down(ch, 1))
            s_up, l_up = ch + s_next, ch + l_next
            diag = (cp + cm) + (s_up + (ch + s_prev)) + (l_up + (ch + l_prev))
            inside = ch > 0
            dinv = jnp.where(inside, F32(0.8) / jnp.where(inside, diag, F32(1.0)), zero)
            s_up = jnp.where(rows == ny - 1, zero, s_up) if sub_last else s_up
            new.append((cp, s_up, jnp.where(last, zero, l_up), dinv))
        for i in range(n):
            for ref, value in zip(op, new[i]):
                ref[x - cbase + i] = value
        return 0

    blocks(lo, hi, max(1, block_of(c) // 2), step)


def pair_rows(s, start, n):
    return s[:, pl.ds(start, n, stride=2), :] + s[:, pl.ds(start + 1, n, stride=2), :]


def flat(a):
    return a.reshape(a.shape[0] * a.shape[1], a.shape[2])


def add_double(v, es, lo, hi, base=0):
    def step(x, n, _):
        new = [v[x + i] + es[((x - base) >> 1) + (i >> 1)] for i in range(n)]
        for i in range(n):
            v[x + i] = new[i]
        return 0

    blocks(lo, hi, max(2, block_of(v) & ~1), step)


def coef_kernel(
    f_hbm, tags_hbm, table_hbm, rough_hbm, coef, to_next, to_prev, x_next, x_prev, packed,
    tags, table, rough, s, sems,
):
    pairs = (
        (table_hbm, table),
        (tags_hbm, tags),
        (rough_hbm, rough),
        (f_hbm.at[:, 24:32], to_next.at[0:32]),
        (f_hbm.at[:, 0:8], to_prev.at[0:32]),
        (f_hbm.at[24:32], x_next.at[0:8]),
        (f_hbm.at[0:8], x_prev.at[0:8]),
    )
    copies = [pltpu.make_async_copy(a, b, sems.at[i]) for i, (a, b) in enumerate(pairs)]
    for copy in copies:
        copy.start()
    for copy in copies[:3]:
        copy.wait()

    def step(x, n, _):
        new = []
        for i in range(n):
            tag = tags[x + i]
            picked = jnp.zeros(tag.shape, F32)
            for region in range(8):
                picked = jnp.where(tag == region, table[region], picked)
            new.append(picked * rough[x + i])
        for i in range(n):
            coef[x + i] = new[i]
        return 0

    blocks(0, 32, 8, step)
    sum_pairs(coef, 0, 16, s)
    c1 = to_level1(pair_rows(s, 0, 16) * F32(0.25))
    packed[...] = c1
    for out, row, extra in ((to_next, 24, 23), (to_prev, 0, 8)):
        out[32:64] = coef[:, row : row + 8]
        for x in range(32):
            out[64 + x // 8, x % 8 : x % 8 + 1, :] = coef[x, extra : extra + 1, :]
        out[68:84] = c1.reshape(16, 8, 128)
    for out, first in ((x_next, 23), (x_prev, 0)):
        out[8:17] = coef[first : first + 9]
        out[17:21] = c1.reshape(4, 32, 128)
    for copy in copies[3:]:
        copy.wait()


def corners_kernel(above, below, to_next, to_prev):
    for out, fs, cs in (
        (to_next, slice(24, 32), slice(23, 32)),
        (to_prev, slice(0, 8), slice(0, 9)),
    ):
        for i, src in enumerate((above, below)):
            rows = slice(8 * i, 8 * i + 8)
            out[0:8, rows] = src[fs]
            out[8:17, rows] = src[32 + cs.start : 32 + cs.stop]
            out[17 + i] = jnp.zeros((16, 128), F32)
            out[17 + i, 0:9] = flat(src[64:68])[cs]
            out[19 + 8 * i : 27 + 8 * i] = src[68:84].reshape(8, 16, 128)


def to_level1(pairs):
    halves = pairs.reshape(8, 2, 16, 128)
    even, odd = halves[:, 0].reshape(128, 128), halves[:, 1].reshape(128, 128)
    return (dot(even, halver_at(0)) + dot(odd, halver_at(1))).reshape(8, 16, 128)


def assemble(dst, own, right, left, above, below, corner_right, corner_left):
    for i in range(8):
        dst[8 + i] = jnp.concatenate([above[i], own[i], below[i]], 0)
        for at, side, corner in ((0, left, corner_left), (16, right, corner_right)):
            dst[at + i] = jnp.concatenate([corner[i, 0:16], side[i], corner[i, 16:32]], 0)


def edge_flags(ng, nb):
    g, b = lax.axis_index("grp"), lax.axis_index("box")
    one, zero = F32(1.0), F32(0.0)
    return (
        jnp.where(g > 0, one, zero),
        jnp.where(g < ng - 1, one, zero),
        jnp.where(b > 0, one, zero),
        jnp.where(b < nb - 1, one, zero),
    )


def fine_restrict(v, f, op, s):
    resid_pairs(v, f, op, 8, 16, s)
    return to_level1(pair_rows(s, 8, 16))


def inner_kernel(ng, nb, f, coef, above, below, v, fx, wx, ws, wl, di, cx, edge):
    gl, gr, bl, br = edge_flags(ng, nb)
    fx[8:40, 8:40] = f[...]
    fx[8:40, 0:8] = above[0:32]
    fx[8:40, 40:48] = below[0:32]
    cx[9:41, 8:40] = coef[...]
    cx[9:41, 0:8] = above[32:64] * bl
    cx[9:41, 40:48] = below[32:64] * br
    edge[0, 9:41] = flat(above[64:68]) * bl
    edge[1, 9:41] = flat(below[64:68]) * br
    op = (wx, ws, wl, di)
    weights(cx, 1, op, 9, 39, 127, False, edge)
    first_sweep(v, fx, op, 9, 39)


def start_kernel(ng, nb, right, left, cright, cleft, *refs):
    v, fx, wx, ws, wl, di, cx, edge, packed, s = refs[8:]
    gl, gr, bl, br = edge_flags(ng, nb)
    for x, side, corner, flag in ((0, left, cleft, gl), (40, right, cright, gr)):
        fx[x : x + 8, 8:40] = side[0:8]
        fx[x : x + 8, 0:8] = corner[0:8, 0:8]
        fx[x : x + 8, 40:48] = corner[0:8, 8:16]
        x = 41 if x else 0
        cx[x : x + 9, 8:40] = side[8:17] * flag
        cx[x : x + 9, 0:8] = corner[8:17, 0:8] * (flag * bl)
        cx[x : x + 9, 40:48] = corner[8:17, 8:16] * (flag * br)
        edge[0, x : x + 9] = corner[17, 0:9] * (flag * bl)
        edge[1, x : x + 9] = corner[18, 0:9] * (flag * br)
    op = (wx, ws, wl, di)
    for lo, hi in ((0, 9), (39, 48)):
        weights(cx, 1, op, lo, hi, 127, False, edge)
        first_sweep(v, fx, op, lo, hi)
    sweep(v, fx, op, 1, 47)
    packed[...] = fine_restrict(v, fx, op, s)


def fold_rows(send):
    lanes = iota((2, 128), 1)
    even = jnp.concatenate([send[0:1], send[2:3]], 0)
    odd = jnp.concatenate([send[1:2], send[3:4]], 0)
    return jnp.where(lanes < 64, even, pltpu.roll(odd, 64, 1))


def mid_down(f1, v1, op1, f2, v2, op2, s, payload, extra):
    v1[0] = v1[23] = jnp.zeros((48, 128), F32)
    first_sweep(v1, f1, op1, 1, 23)
    sweep(v1, f1, op1, 1, 23, True)
    resid_each(v1, f1, op1, 2, 20, s)
    half = halver(128)
    f2[2:22] = dot(flat(pair_rows(s.at[0:20], 0, 24)), folder()).reshape(20, 24, 128)
    first_sweep(v2, f2, op2, 2, 22)
    sweep(v2, f2, op2, 3, 21)
    resid_pairs(v2, f2, op2, 8, 4, s.at[0:4, 0:24])
    send = collect(s, half, 0, F32(1.0))
    send = fold_rows(send) if extra is None else send + extra
    payload[...] = jnp.broadcast_to(send[None], payload.shape)


def collect(s, half, lane, scale):
    total = jnp.zeros((12, 128), F32)
    lanes = iota((12, 128), 1)
    for x in range(4):
        pairs = flat(pair_rows(s.at[x : x + 1], 0, 12))
        cut = jnp.where(lanes < 16, dot(pairs * scale, half), F32(0.0))
        shift = lane + 16 * x
        total = total + (pltpu.roll(cut, shift, 1) if shift else cut)
    return total[4:8]


def mid_weights_kernel(
    ng, nb, packed, right, left, above, below, cright, cleft,
    wx1, ws1, wl1, di1, wx2, ws2, wl2, di2, coarser, c1, c2, s,
):
    gl, gr, bl, br = edge_flags(ng, nb)
    rows = iota((48, 128), 0)
    scale = jnp.where(rows < 16, bl, jnp.where(rows < 32, F32(1.0), br))
    for i in range(8):
        parts = [above[68 + 2 * i], above[69 + 2 * i], packed[i]]
        parts += [below[68 + 2 * i], below[69 + 2 * i]]
        c1[8 + i] = jnp.concatenate(parts, 0) * scale
        own = slice(16 * (i % 2), 16 * (i % 2) + 16)
        for at, side, corner, flag in ((0, left, cleft, gl), (16, right, cright, gr)):
            parts = [corner[19 + i], side[17 + i // 2, own], corner[27 + i]]
            c1[at + i] = jnp.concatenate(parts, 0) * (scale * flag)
    wx1[0] = jnp.zeros((48, 128), F32)
    weights(c1, 0, (wx1, ws1, wl1, di1), 1, 23, 127, False, None, True)
    half = halver(128)
    c2[...] = dot(flat(pair_rows(c1, 0, 24) * F32(0.25)), folder()).reshape(24, 24, 128)
    weights(c2, 0, (wx2, ws2, wl2, di2), 1, 23, 31, False)
    for x in range(4):
        s[x, 0:24] = c2[8 + 2 * x] + c2[9 + 2 * x]
    send = collect(s, half, 64, F32(0.25))
    coarser[...] = send


def mid_kernel(
    own, right, left, above, below, corner_right, corner_left,
    wx1, ws1, wl1, di1, wx2, ws2, wl2, di2, coarser,
    f1, v1, f2, v2, payload, s,
):
    assemble(f1, own, right, left, above, below, corner_right, corner_left)
    op1, op2 = (wx1, ws1, wl1, di1), (wx2, ws2, wl2, di2)
    mid_down(f1, v1, op1, f2, v2, op2, s, payload, coarser[...])


def mid2_kernel(
    own, right, left, above, below, corner_right, corner_left,
    wx1, ws1, wl1, di1, wx2, ws2, wl2, di2,
    f1, v1, f2, v2, payload, s,
):
    assemble(f1, own, right, left, above, below, corner_right, corner_left)
    op1, op2 = (wx1, ws1, wl1, di1), (wx2, ws2, wl2, di2)
    mid_down(f1, v1, op1, f2, v2, op2, s, payload, None)


def apply3(p, wx, ws, wl, diag):
    zero = jnp.zeros_like(p[:1])
    q = wx * jnp.concatenate([p[1:], zero], 0)
    q = q + jnp.concatenate([zero, (wx * p)[:-1]], 0)
    q = q + (ws * up(p, 1) + down(ws * p, 1))
    q = q + (wl * up(p, 2) + down(wl * p, 2))
    return diag * p - q


def bottom(f4, c4, ny4):
    nx, nz, nl = c4.shape
    ch = c4 * F32(0.5)
    zero = jnp.zeros_like(ch[:1])
    rows, lanes, slabs = iota(c4.shape, 1), iota(c4.shape, 2), iota(c4.shape, 0)
    o = F32(0.0)
    x_up = ch + jnp.concatenate([ch[1:], zero], 0)
    x_dn = ch + jnp.concatenate([zero, ch[:-1]], 0)
    s_up = ch + jnp.where(rows == nz - 1, o, up(ch, 1))
    s_dn = ch + jnp.where(rows == 0, o, down(ch, 1))
    l_up = ch + jnp.where(lanes >= ny4 - 1, o, up(ch, 2))
    l_dn = ch + jnp.where(lanes == 0, o, down(ch, 2))
    diag = x_up + x_dn + s_up + s_dn + l_up + l_dn
    wx = jnp.where(slabs == nx - 1, o, x_up)
    ws = jnp.where(rows == nz - 1, o, s_up)
    wl = jnp.where(lanes >= ny4 - 1, o, l_up)

    def total(a):
        for axis in range(3):
            a = jnp.sum(a, axis=axis, keepdims=True)
        return a

    v = None
    r = p = f4
    rr = total(r * r)
    for i in range(NB):
        q = apply3(p, wx, ws, wl, diag)
        alpha = rr / total(p * q)
        v = alpha * p if v is None else v + alpha * p
        if i < NB - 1:
            r = r - alpha * q
            new = total(r * r)
            p = r + (new / rr) * p
            rr = new
    return v


def coarse_weights(ng, nb, got, op3, c4, c3, s3):
    n3, nl = 4 * ng, 4 * nb
    for g in range(ng):
        t = got[g * nl : (g + 1) * nl, :].T
        c3[4 + 4 * g : 8 + 4 * g] = t[64:128].reshape(4, 16, nl)
    pad = jnp.zeros((4, 16, nl), F32)
    for ref in (c3, op3[0]):
        ref[0:4] = pad
        ref[4 + n3 : 8 + n3] = pad
    weights(c3, 0, op3, 4, 4 + n3, nl - 1, True)
    sum_pairs(c3, 4, n3 // 2, s3)
    c4[...] = dot(flat(pair_rows(s3, 0, 8) * F32(0.25)), halver(nl)).reshape(n3 // 2, 8, nl)


def coarse(ng, nb, got, v3, f3, op3, c4, s3):
    n3, nl = 4 * ng, 4 * nb
    if got.shape[0] == ng * nl:
        for g in range(ng):
            t = got[g * nl : (g + 1) * nl, :].T
            f3[4 + 4 * g : 8 + 4 * g] = t[0:64].reshape(4, 16, nl)
    else:
        k, y = iota((nl // 2, nl), 0), iota((nl // 2, nl), 1)
        even = jnp.where(y == 2 * k, F32(1.0), F32(0.0))
        odd = jnp.where(y == 2 * k + 1, F32(1.0), F32(0.0))
        ts = [got[g * (nl // 2) : (g + 1) * (nl // 2), :].T for g in range(ng)]
        lhs0 = jnp.concatenate([t[0:64] for t in ts], 0)
        lhs1 = jnp.concatenate([t[64:128] for t in ts], 0)
        f3[4 : 4 + n3] = (dot(lhs0, even) + dot(lhs1, odd)).reshape(n3, 16, nl)
    pad = jnp.zeros((4, 16, nl), F32)
    v3[0:4] = pad
    v3[4 + n3 : 8 + n3] = pad
    lo, hi = 4, 4 + n3
    first_sweep(v3, f3, op3, lo, hi)
    sweep(v3, f3, op3, lo, hi)
    half = halver(nl)

    resid_pairs(v3, f3, op3, 4, n3 // 2, s3)
    f4 = dot(flat(pair_rows(s3, 0, 8)), half).reshape(n3 // 2, 8, nl)
    v4 = bottom(f4, c4[...], nl // 2)
    e = dot(flat(v4), doubler(nl)).reshape(n3 // 2, 8, nl)
    s3[:, pl.ds(0, 8, stride=2), :] = e
    s3[:, pl.ds(1, 8, stride=2), :] = e

    add_double(v3, s3, 4, 4 + n3, 4)
    sweep(v3, f3, op3, lo, hi)
    sweep(v3, f3, op3, lo, hi)


def coarse_to_mid(nb, v3, v2, s2, nl):
    g, b = lax.axis_index("grp"), lax.axis_index("box")
    for x in range(12):
        e = v3[4 * g + x]
        s2[x : x + 1, pl.ds(0, 16, stride=2), :] = e[None]
        s2[x : x + 1, pl.ds(1, 16, stride=2), :] = e[None]
    j, y = iota((24, nl), 0), iota((24, nl), 1)
    pick = jnp.where(y == 4 * b - 4 + (j >> 1), F32(1.0), F32(0.0))
    lanes = iota((24, 128), 1)
    zero = F32(0.0)
    for q in range(3):
        block = flat(s2[4 * q : 4 * q + 4])
        e = lax.dot_general(
            pick, block, (((1,), (1,)), ((), ())),
            precision=lax.Precision.HIGHEST, preferred_element_type=F32,
        )
        for i in range(4):
            part = e if i == 0 else pltpu.roll(e, 128 - 32 * i, 1)
            part = jnp.where(lanes < 32, part, zero)
            x = 2 * (4 * q + i)
            v2[x] = v2[x] + part
            v2[x + 1] = v2[x + 1] + part


def climb(ng, nb, got, op3, c4, v1, f1, op1, v2, f2, op2, scr):
    v3, f3, s3, s2, es = scr
    coarse(ng, nb, got, v3, f3, op3, c4, s3)
    coarse_to_mid(nb, v3, v2, s2, 4 * nb)
    sweep(v2, f2, op2, 4, 20)
    sweep(v2, f2, op2, 5, 19)
    e = dot(flat(v2[5:19]), spreader()).reshape(14, 24, 128)
    es[5:19, pl.ds(0, 24, stride=2), :] = e
    es[5:19, pl.ds(1, 24, stride=2), :] = e
    v1, f1 = v1.at[:, 8:40], f1.at[:, 8:40]
    op1 = tuple(ref.at[:, 8:40] for ref in op1)
    for i in range(5, 19):
        v1[i] = v1[i] + es[i, 8:40]
    sweep(v1, f1, op1, 5, 19, True)
    sweep(v1, f1, op1, 6, 18, True)
    rows = flat(v1[6:18, 4:28, :])
    e = [dot(rows, doubler_at(h)).reshape(12, 1, 24, 128) for h in (0, 1)]
    e = jnp.concatenate(e, 1).reshape(24, 24, 128)
    es[:, pl.ds(0, 24, stride=2), :] = e
    es[:, pl.ds(1, 24, stride=2), :] = e


def turn_kernel(ng, nb, *refs):
    got, f0, wx0, ws0, wl0, di0, f1, wx1, ws1, wl1, di1, f2, wx2, ws2, wl2, di2 = refs[:16]
    v0i, v1i, v2i = refs[16:19]
    v0, packed = refs[19:21]
    op3, c4 = refs[21:25], refs[25]
    v1, v2, s, c3 = refs[26:30]
    scr = refs[30:]
    coarse_weights(ng, nb, got, op3, c4, c3, scr[2])
    v1[...] = v1i[...]
    v2[...] = v2i[...]
    op0, op1, op2 = (wx0, ws0, wl0, di0), (wx1, ws1, wl1, di1), (wx2, ws2, wl2, di2)
    climb(ng, nb, got, op3, c4, v1, f1, op1, v2, f2, op2, scr)
    add_double(v0, scr[-1], 0, 48)
    for lo in (2, 3, 4, 5):
        sweep(v0, f0, op0, lo, 48 - lo)
    packed[...] = fine_restrict(v0, f0, op0, s)


def end_kernel(ng, nb, *refs):
    got, op3, c4 = refs[0], refs[1:5], refs[5]
    f0, wx0, ws0, wl0, di0, f1, wx1, ws1, wl1, di1, f2, wx2, ws2, wl2, di2 = refs[6:21]
    v0i, v1i, v2i = refs[21:24]
    sol, res = refs[24:26]
    v0, v1, v2 = refs[26:29]
    scr = refs[29:]
    v0[...] = v0i[...]
    v1[...] = v1i[...]
    v2[...] = v2i[...]
    op0, op1, op2 = (wx0, ws0, wl0, di0), (wx1, ws1, wl1, di1), (wx2, ws2, wl2, di2)
    climb(ng, nb, got, op3, c4, v1, f1, op1, v2, f2, op2, scr)
    add_double(v0, scr[-1], 4, 44)
    sweep(v0, f0, op0, 6, 42)
    sweep(v0, f0, op0, 7, 41)

    def step(x, n, _):
        rs = resid_slabs(v0, f0, op0, x + 8, n)
        for i in range(n):
            res[x + i] = rs[i][8:40]
        return 0

    sol[...] = v0[8:40, 8:40]
    blocks(0, 32, 8, step)


def ring(x, axis, n):
    before = lax.ppermute(x[0], axis, [(i, (i + 1) % n) for i in range(n)])
    after = lax.ppermute(x[1], axis, [(i, (i - 1) % n) for i in range(n)])
    return before, after


def around(packed, ng, nb):
    above, below = ring((packed, packed), "box", nb)
    left, right = ring((packed, packed), "grp", ng)
    above, below, left, right = lax.optimization_barrier((above, below, left, right))
    corners = jnp.concatenate([above, below], 1)
    corner_left, corner_right = ring((corners, corners), "grp", ng)
    return packed, right, left, above, below, corner_right, corner_left


def gather_all(payload):
    got = lax.all_to_all(payload, ("grp", "box"), 0, 0, tiled=True)
    return got.reshape(got.shape[0] * got.shape[1], got.shape[2])


def make_body(ng, nb):
    big, mid, low = (48, 48, 128), (24, 48, 128), (24, 24, 128)
    n3, nl = 4 * ng, 4 * nb
    nd = ng * nb
    pay, pay2 = (nd, 4, 128), (nd, 2, 128)
    lev3 = (n3 + 8, 16, nl)
    climb_scratch = [lev3] * 2 + [(n3 // 2, 16, nl), (12, 32, nl), (24, 48, 128)]

    def fix(kernel):
        return lambda *refs: kernel(ng, nb, *refs)

    def body(f, tags, table, rough):
        coef, to_next, to_prev, x_next, x_prev, cpack = call(
            coef_kernel, (f, tags, table, rough),
            [(32, 32, 128)] + [(84, 8, 128)] * 2 + [(21, 32, 128)] * 2 + [(8, 16, 128)],
            scratch=[
                pltpu.VMEM((32, 32, 128), jnp.int32), pltpu.SMEM((8,), F32), (32, 32, 128),
                (16, 32, 128), pltpu.SemaphoreType.DMA((7,)),
            ],
            hbm=(0, 1, 2, 3),
        )
        above, below = ring((to_next, to_prev), "box", nb)
        left, right = ring((x_next, x_prev), "grp", ng)
        corners = call(corners_kernel, (above, below), [(35, 16, 128)] * 2)
        corner_left, corner_right = ring(corners, "grp", ng)
        halo = (right, left, above, below, corner_right, corner_left)
        inner = call(
            fix(inner_kernel), (f, coef, above, below), [big] * 6 + [(50, 48, 128), (2, 56, 128)],
        )
        v0, f0, wx0, ws0, wl0, di0, _, _, packed = call(
            fix(start_kernel), halo[:2] + halo[4:] + tuple(inner),
            [big] * 6 + [(50, 48, 128), (2, 56, 128), (8, 16, 128)],
            scratch=[(16, 48, 128)], aliases={4 + i: i for i in range(8)},
        )
        l0 = (f0, wx0, ws0, wl0, di0)
        *ops, coarser = call(
            fix(mid_weights_kernel), (cpack,) + halo, [mid] * 4 + [low] * 4 + [(4, 128)],
            scratch=[mid, low, mid],
        )
        f1, v1, f2, v2, payload = call(
            mid_kernel, around(packed, ng, nb) + tuple(ops) + (coarser,),
            [mid, mid, low, low, pay], scratch=[(24, 48, 128)], leave=(4,),
        )
        got_c = gather_all(payload)
        l1, l2 = (f1, *ops[:4]), (f2, *ops[4:])
        v0, packed, *level3 = call(
            fix(turn_kernel), (got_c,) + l0 + l1 + l2 + (v0, v1, v2),
            [big, (8, 16, 128)] + [lev3] * 4 + [(n3 // 2, 8, nl)],
            aliases={16: 0}, scratch=[mid, low, (16, 48, 128), lev3] + climb_scratch,
        )
        f1, v1, f2, v2, payload = call(
            mid2_kernel, around(packed, ng, nb) + l1[1:] + l2[1:],
            [mid, mid, low, low, pay2], scratch=[(24, 48, 128)], leave=(4,),
        )
        got = gather_all(payload)
        l1, l2 = (f1,) + l1[1:], (f2,) + l2[1:]
        return tuple(call(
            fix(end_kernel), (got, *level3) + l0 + l1 + l2 + (v0, v1, v2), [(32, 32, 128)] * 2,
            scratch=[big, mid, low] + climb_scratch, leave=(0, 1),
        ))

    return body


def solution(mesh):
    body = make_body(mesh.shape["grp"], mesh.shape["box"])
    return jax.shard_map(
        body,
        mesh=mesh,
        in_specs=(P("grp", "box", None), P("grp", "box", None), P(), P("grp", "box", None)),
        out_specs=(P("grp", "box", None), P("grp", "box", None)),
        check_vma=False,
    )
```
